512 devices in a mesh: gx: 8 (over z), gy: 4 (over y_hi), gz: 16 (over y_lo, x, core).
Axes of the slice: x: 4, y: 8 (y_hi: 4, y_lo: 2; y = y_hi * 2 + y_lo), z: 8, core: 2. Of those that a mesh axis runs over, the one named last changes fastest.
Arguments:
- phi_start: float32 [64, 64, 2048], P('gx', 'gy', 'gz'), may hold values from -6 to 6
- section_first: float32 [64, 64, 2048], P('gx', 'gy', 'gz'), may hold values from -6 to 6
- section_middle: float32 [64, 64, 2048], P('gx', 'gy', 'gz'), may hold values from -6 to 6
- section_second: float32 [64, 64, 2048], P('gx', 'gy', 'gz'), may hold values from -6 to 6
- cot_final: float32 [64, 64, 2048], P('gx', 'gy', 'gz'), may hold values from -6 to 6
Outputs:
- cot_start: float32 [64, 64, 2048], P('gx', 'gy', 'gz')
The draws below stay inside these ranges and needn't reach their ends.
All inputs are finite; a program needn't handle non-finite values.
Results may differ from the reference program's by a relative error of at most 0.0003.
Values sent between devices are 32-bit elements; how exact they have to be, the bound alone decides.
No kernel may reach another device: no remote copies, remote signals or barrier semaphores. Data moves between devices by JAX's collectives and lax.ppermute only.
A program may use at most 64 MiB of HBM per device.

```python
import jax
import jax.numpy as jnp
from jax import lax

NX = 64
NY = 64
NZ = 2048
N_GX = 8


def level_of(rng, shape, shards, low, high):
    def one(axis_at, blocks):
        steps = jax.random.uniform(jax.random.fold_in(jax.random.fold_in(rng, 6), axis_at), (blocks,), jnp.float32, low / len(shards), high / len(shards))
        return jnp.repeat(jnp.exp(steps), shape[axis_at] // blocks).reshape((-1,) + (1,) * (len(shape) - axis_at - 1))

    loudness = one(*shards[0])
    for cut in shards[1:]:
        loudness = loudness * one(*cut)
    return loudness


def centred(key, extent, spread, most, cuts=(), kind=jnp.bfloat16):
    result = jax.random.normal(key, extent, jnp.float32) * spread
    if len(cuts) > 0:
        result = level_of(key, extent, cuts, -0.22, 0.18) * result
    return jnp.clip(result, min=-most, max=most).astype(kind)


def setup_inputs(seed: int = 0) -> dict:
    keys = jax.random.split(jax.random.key(seed), 6)
    return {
        "phi_start": centred(keys[0], (NX, NY, NZ), 1.0, 6.0, ((0, 8), (1, 4), (2, 16)), jnp.float32),
        "section_first": centred(keys[1], (NX, NY, NZ), 1.0, 6.0, ((0, 8), (1, 4), (2, 16)), jnp.float32),
        "section_middle": centred(keys[2], (NX, NY, NZ), 1.0, 6.0, ((0, 8), (1, 4), (2, 16)), jnp.float32),
        "section_second": centred(keys[3], (NX, NY, NZ), 1.0, 6.0, ((0, 8), (1, 4), (2, 16)), jnp.float32),
        "cot_final": centred(keys[4], (NX, NY, NZ), 1.0, 6.0, ((0, 8), (1, 4), (2, 16)), jnp.float32),
    }


tau_step = 0.3
weno_epsilon = 1e-06
smooth_epsilon = 0.01

def weno_five(value_one, value_two, value_three, value_four, value_five):
    candidate_one = value_one / 3.0 - 7.0 * value_two / 6.0 + 11.0 * value_three / 6.0
    candidate_two = -value_two / 6.0 + 5.0 * value_three / 6.0 + value_four / 3.0
    candidate_three = value_three / 3.0 + 5.0 * value_four / 6.0 - value_five / 6.0
    beta_one = 13.0 / 12.0 * (value_one - 2.0 * value_two + value_three) ** 2 + 0.25 * (value_one - 4.0 * value_two + 3.0 * value_three) ** 2
    beta_two = 13.0 / 12.0 * (value_two - 2.0 * value_three + value_four) ** 2 + 0.25 * (value_two - value_four) ** 2
    beta_three = 13.0 / 12.0 * (value_three - 2.0 * value_four + value_five) ** 2 + 0.25 * (3.0 * value_three - 4.0 * value_four + value_five) ** 2
    weight_one = 0.1 / (weno_epsilon + beta_one) ** 2
    weight_two = 0.6 / (weno_epsilon + beta_two) ** 2
    weight_three = 0.3 / (weno_epsilon + beta_three) ** 2
    weighted = weight_one * candidate_one + weight_two * candidate_two + weight_three * candidate_three
    return weighted / (weight_one + weight_two + weight_three)

def one_sided(grid_field, along_axis):
    full_length = grid_field.shape[along_axis]
    cell_count = full_length - 6
    differences = lax.slice_in_dim(grid_field, 1, full_length, axis=along_axis) - lax.slice_in_dim(grid_field, 0, full_length - 1, axis=along_axis)
    shifted = [lax.slice_in_dim(differences, offset, offset + cell_count, axis=along_axis) for offset in range(6)]
    minus_side = weno_five(shifted[0], shifted[1], shifted[2], shifted[3], shifted[4])
    plus_side = weno_five(shifted[5], shifted[4], shifted[3], shifted[2], shifted[1])
    return (minus_side, plus_side)

def smooth_max(first_term, second_term):
    return 0.5 * (first_term + second_term + jnp.sqrt((first_term - second_term) ** 2 + smooth_epsilon))

def hamiltonian(padded_field, positive):
    squared_sum = None
    for along_axis in range(3):
        window = [slice(3, -3)] * 3
        window[along_axis] = slice(None)
        minus_side, plus_side = one_sided(padded_field[tuple(window)], along_axis)
        upwind = jnp.where(positive, jax.nn.relu(minus_side), jax.nn.relu(-minus_side))
        downwind = jnp.where(positive, jax.nn.relu(-plus_side), jax.nn.relu(plus_side))
        axis_term = smooth_max(upwind * upwind, downwind * downwind)
        squared_sum = axis_term if squared_sum is None else squared_sum + axis_term
    return jnp.sqrt(squared_sum)

def fold_axis(accumulated, along_axis):
    axis_length = accumulated.shape[along_axis]
    inner_length = axis_length - 6
    core_part = lax.slice_in_dim(accumulated, 3, axis_length - 3, axis=along_axis)
    low_ghost = lax.slice_in_dim(accumulated, 0, 3, axis=along_axis)
    high_ghost = lax.slice_in_dim(accumulated, axis_length - 3, axis_length, axis=along_axis)
    widths_low = [(0, 0)] * 3
    widths_low[along_axis] = (inner_length - 3, 0)
    widths_high = [(0, 0)] * 3
    widths_high[along_axis] = (0, inner_length - 3)
    return core_part + jnp.pad(low_ghost, widths_low) + jnp.pad(high_ghost, widths_high)

def section_reference(grid_field, positive, weight):
    padded = jnp.pad(grid_field, 3, mode='wrap')
    block_rows = NX // N_GX

    def one_block(accumulated, block_index):
        row_start = (block_index * block_rows).astype(jnp.int32)
        slab_field = lax.dynamic_slice_in_dim(padded, row_start, block_rows + 6, 0)
        slab_mask = lax.dynamic_slice_in_dim(positive, row_start, block_rows, 0)
        slab_weight = lax.dynamic_slice_in_dim(weight, row_start, block_rows, 0)
        values, pullback = jax.vjp(lambda field_in: hamiltonian(field_in, slab_mask), slab_field)
        gradient, = pullback(slab_weight)
        current = lax.dynamic_slice_in_dim(accumulated, row_start, block_rows + 6, 0)
        accumulated = lax.dynamic_update_slice_in_dim(accumulated, current + gradient, row_start, 0)
        return (accumulated, values)
    accumulated, values = lax.scan(one_block, jnp.zeros_like(padded), jnp.arange(N_GX, dtype=jnp.int32))
    values = values.reshape(grid_field.shape)
    for along_axis in range(3):
        accumulated = fold_axis(accumulated, along_axis)
    return (accumulated, values)

def reference(phi_start, section_first, section_middle, section_second, cot_final):
    positive = phi_start > 0
    squared_one = phi_start * phi_start + 1.0
    sign_value = phi_start / jnp.sqrt(squared_one)
    sign_slope = 1.0 / (squared_one * jnp.sqrt(squared_one))

    def section_terms(grid_field, incoming):
        gradient, values = section_reference(grid_field, positive, -tau_step * sign_value * incoming)
        return (gradient, -tau_step * sign_slope * (values - 1.0) * incoming)
    half_final = 0.5 * cot_final
    back_second, part_second = section_terms(section_second, half_final)
    cot_second = half_final + back_second
    back_middle, part_middle = section_terms(section_middle, cot_second)
    cot_middle = half_final + cot_second + back_middle
    half_middle = 0.5 * cot_middle
    back_first, part_first = section_terms(section_first, half_middle)
    cot_first = half_middle + back_first
    back_start, part_start = section_terms(phi_start, cot_first)
    return half_middle + cot_first + back_start + part_second + part_middle + part_first + part_start
```

```python
import jax
import jax.numpy as jnp
from jax import lax
from jax.experimental import pallas as pl
from jax.experimental.pallas import tpu as pltpu
from jax.sharding import PartitionSpec as P

TAU = 0.3
WENO_EPS = 1e-06
SMOOTH_EPS = 0.01
LANES = 128
BX, BY = 8, 16
F32 = jnp.float32


def lane_iota(shape):
    return lax.broadcasted_iota(jnp.int32, shape, len(shape) - 1)


def major_roll(v, k):
    n = v.shape[0]
    return jnp.concatenate([v[(g + k) % n][None] for g in range(n)], axis=0)


def shift_x(v, k):
    lane = lane_iota(v.shape)
    rolled = pltpu.roll(v, (-BY * k) % LANES, 2)
    carried = pltpu.roll(rolled, (-1 if k > 0 else 1) % v.shape[1], 1)
    crossing = lane >= LANES - BY * k if k > 0 else lane < -BY * k
    return jnp.where(crossing, carried, rolled)


def shift_y(v, k):
    inner = lane_iota(v.shape) % BY
    rolled = pltpu.roll(v, (-k) % LANES, 2)
    if k > 0:
        carried = major_roll(pltpu.roll(v, (BY - k) % LANES, 2), 1)
        return jnp.where(inner >= BY - k, carried, rolled)
    carried = major_roll(pltpu.roll(v, (-BY - k) % LANES, 2), -1)
    return jnp.where(inner < -k, carried, rolled)


def weno_center(b, dm, d0, d1, d2):
    e1, e2, e3 = d0 - dm, d1 - d0, d2 - d1
    p1, p2, p3 = 0.5 * e1 + d0, 0.5 * (d0 + d1), 0.5 * e3 - d1
    f1, f2, f3 = (13.0 / 12.0) * e1, (13.0 / 12.0) * e2, (13.0 / 12.0) * e3
    t1 = WENO_EPS + (f1 * e1 + p1 * p1)
    t2 = WENO_EPS + (f2 * e2 + p2 * p2)
    t3 = WENO_EPS + (f3 * e3 + p3 * p3)
    t12 = t1 * t2
    whole = 1.0 / (t12 * t3)
    i3 = whole * t12
    whole3 = whole * t3
    i1, i2 = whole3 * t2, whole3 * t1
    a1, a2, a3 = i1 * i1, i2 * i2, i3 * i3
    m1, m2, m3 = 0.1 * a1, 0.6 * a2, 0.3 * a3
    r1, r3 = 0.1 * a3, 0.3 * a1
    sum_m, sum_p = m1 + m2 + m3, r1 + m2 + r3
    both = 1.0 / (sum_m * sum_p)
    inv_m, inv_p = both * sum_p, both * sum_m
    w1, w2, w3 = m1 * inv_m, m2 * inv_m, m3 * inv_m
    v1, v2, v3 = r1 * inv_p, m2 * inv_p, r3 * inv_p
    y1, y3 = (e1 - e2) * (1.0 / 3.0), (e2 - e3) * (1.0 / 6.0)
    y1h, y3d = 0.5 * y1, 2.0 * y3
    corr_m = w1 * y1 + w3 * y3
    corr_p = v1 * y3d + v3 * y1h
    base = b + e2 * (1.0 / 3.0)
    minus = base + 0.5 * d0 + corr_m
    plus = base - 0.5 * d1 - corr_p
    j1, j2, j3 = -4.0 * i1, -4.0 * i2, -4.0 * i3
    g1, g3 = f1 + 0.5 * p1, f3 + 0.5 * p3
    half_p2 = 0.5 * p2

    def spread(s1, s2, s3, cy1, cy3, own0, own1):
        ce1 = cy1 + s1 * g1
        ce2 = (cy3 - cy1) + ((1.0 / 3.0) + s2 * f2)
        ce3 = s3 * g3 - cy3
        s2p = s2 * half_p2
        cd0 = s1 * p1 + s2p
        cd1 = s2p - s3 * p3
        if own0:
            cd0 = cd0 + 0.5
        if own1:
            cd1 = cd1 - 0.5
        return (-ce1, cd0 + (ce1 - ce2), cd1 + (ce2 - ce3), ce3)

    jac_m = spread(
        j1 * (w1 * (y1 - corr_m)), -j2 * (w2 * corr_m), j3 * (w3 * (y3 - corr_m)),
        w1 * (1.0 / 3.0), w3 * (1.0 / 6.0), True, False,
    )
    jac_p = spread(
        j1 * (v3 * (corr_p - y1h)), j2 * (v2 * corr_p), j3 * (v1 * (corr_p - y3d)),
        v3 * (-1.0 / 6.0), v1 * (-1.0 / 3.0), False, True,
    )
    return minus, plus, jac_m, jac_p


def upwind_term(minus, plus, side):
    u = jnp.maximum(side * minus, 0.0)
    v = jnp.maximum(-side * plus, 0.0)
    uu, vv = u * u, v * v
    gap = uu - vv
    square = gap * gap + SMOOTH_EPS
    root = lax.rsqrt(square)
    slope = gap * root
    term = 0.5 * (uu + vv + square * root)
    return term, 2.0 * ((1.0 + slope) * (u * side)), -2.0 * ((1.0 - slope) * (v * side))


PER_AXIS = 10


def coef_kernel(section, f_ref, lo_ref, hi_ref, phi_ref, co_ref, pc_ref):
    fref = f_ref

    def keep(axis, z, minus_plus, jac_m, jac_p):
        for n, part in enumerate(minus_plus + jac_m + jac_p):
            co_ref[PER_AXIS * axis + n, z] = part

    def plane(z, carry):
        f = fref[z]
        side = jnp.where(phi_ref[z] > 0, 1.0, -1.0).astype(F32)
        total = None
        for axis, shift in ((0, shift_x), (1, shift_y)):
            b = f - shift(f, -1)
            d = b - shift(b, -1)
            minus, plus, jac_m, jac_p = weno_center(b, shift(d, -1), d, shift(d, 1), shift(d, 2))
            term, by_minus, by_plus = upwind_term(minus, shift(plus, 1), side)
            keep(axis, z, (by_minus, by_plus), jac_m, jac_p)
            total = term if total is None else total + term
        pc_ref[z] = total
        return carry

    lax.fori_loop(0, 4, plane, 0)

    def column(g, carry):
        f = (
            [lo_ref[3 * section + i, g] for i in range(3)]
            + [fref[i, g] for i in range(4)]
            + [hi_ref[3 * section + i, g] for i in range(3)]
        )
        b = [None] + [f[i] - f[i - 1] for i in range(1, 10)]
        d = [None, None] + [b[i] - b[i - 1] for i in range(2, 10)]
        centers = [weno_center(b[m + 3], d[m + 2], d[m + 3], d[m + 4], d[m + 5]) for m in range(5)]
        for z in range(4):
            phi = phi_ref[z, g]
            side = jnp.where(phi > 0, 1.0, -1.0).astype(F32)
            term, by_minus, by_plus = upwind_term(centers[z][0], centers[z + 1][1], side)
            square = phi * phi + 1.0
            root = lax.rsqrt(square)
            ham2 = pc_ref[z, g] + term
            inv = lax.rsqrt(ham2)
            ham = ham2 * inv
            scale = (-0.25 * TAU) * ((phi * root) * inv)
            pc_ref[z, g] = (-TAU) * ((root * root * root) * (ham - 1.0))
            for axis in (0, 1):
                for n in (0, 1):
                    co_ref[PER_AXIS * axis + n, z, g] = co_ref[PER_AXIS * axis + n, z, g] * scale
            parts = (by_minus * scale, by_plus * scale) + centers[z][2] + centers[z + 1][3]
            for n, part in enumerate(parts):
                co_ref[PER_AXIS * 2 + n, z, g] = part
        return carry

    lax.fori_loop(0, 4, column, 0)


def apply_local(c_ref, co_ref, out_ref, up_ref, dn_ref):
    def plane(z, carry):
        c = c_ref[z]
        total = None
        for axis, shift in ((0, shift_x), (1, shift_y)):
            co = lambda n: co_ref[PER_AXIS * axis + n, z]
            a = c * co(0)
            g = shift(c * co(1), -1)
            t = [a * co(2 + k) + g * co(6 + k) for k in range(4)]
            dbar = t[1] + shift(t[0], 1) + shift(t[2], -1) + shift(t[3], -2)
            bbar = (a + g) + (dbar - shift(dbar, 1))
            part = bbar - shift(bbar, 1)
            total = part if total is None else total + part
        out_ref[z] = total
        return carry

    lax.fori_loop(0, 4, plane, 0)

    def column(g, carry):
        dbar = [None] * 8
        bbar = [None] * 9

        def add(into, at, value):
            into[at] = value if into[at] is None else into[at] + value

        for z in range(4):
            c = c_ref[z, g]
            co = lambda n: co_ref[PER_AXIS * 2 + n, z, g]
            a, p = c * co(0), c * co(1)
            for k in range(4):
                add(dbar, z + k, a * co(2 + k))
                add(dbar, z + k + 1, p * co(6 + k))
            add(bbar, z + 2, a)
            add(bbar, z + 3, p)
        for j in range(8):
            add(bbar, j + 1, dbar[j])
            add(bbar, j, -dbar[j])
        for z in range(4):
            out_ref[z, g] = out_ref[z, g] + (bbar[z + 2] - bbar[z + 3])
        for k in range(3):
            up_ref[k, g] = bbar[6 + k]
            dn_ref[k, g] = bbar[k]
        return carry

    lax.fori_loop(0, 4, column, 0)


def joined(own_ref, lo_ref, hi_ref):
    lo0, lo1, lo2 = lo_ref[0], lo_ref[1], lo_ref[2]
    hi0, hi1, hi2 = hi_ref[0], hi_ref[1], hi_ref[2]
    return (
        own_ref[0] + (lo0 - lo1),
        own_ref[1] + (lo1 - lo2 - hi0),
        own_ref[2] + (lo2 + hi0 - hi1),
        own_ref[3] + (hi1 - hi2),
    )


def stage_one(cot_ref, co_ref, pc_ref, own_ref, up_ref, dn_ref, c_ref, acc_ref):
    half = 0.5 * cot_ref[...]
    c_ref[...] = half
    acc_ref[...] = pc_ref[...] * half
    apply_local(c_ref, co_ref, own_ref, up_ref, dn_ref)


def stage_two(half_ref, own_in, lo_ref, hi_ref, acc_in, co_ref, pc_ref, own_ref, up_ref, dn_ref, c_ref, acc_ref):
    for z, back in enumerate(joined(own_in, lo_ref, hi_ref)):
        c = half_ref[z] + back
        c_ref[z] = c
        acc_ref[z] = acc_in[z] + pc_ref[z] * c
    apply_local(c_ref, co_ref, own_ref, up_ref, dn_ref)


def stage_three(half_ref, second_ref, own_in, lo_ref, hi_ref, acc_in, co_ref, pc_ref, own_ref, up_ref, dn_ref, c_ref, acc_ref):
    for z, back in enumerate(joined(own_in, lo_ref, hi_ref)):
        c = 0.5 * (half_ref[z] + second_ref[z] + back)
        c_ref[z] = c
        acc_ref[z] = acc_in[z] + pc_ref[z] * c
    apply_local(c_ref, co_ref, own_ref, up_ref, dn_ref)


def stage_four(middle_ref, own_in, lo_ref, hi_ref, acc_in, co_ref, pc_ref, own_ref, up_ref, dn_ref, c_ref, acc_ref):
    for z, back in enumerate(joined(own_in, lo_ref, hi_ref)):
        c = middle_ref[z] + back
        c_ref[z] = c
        acc_ref[z] = acc_in[z] + pc_ref[z] * c + (middle_ref[z] + c)
    apply_local(c_ref, co_ref, own_ref, up_ref, dn_ref)


def finish(own_in, lo_ref, hi_ref, acc_in, out_ref):
    for z, back in enumerate(joined(own_in, lo_ref, hi_ref)):
        whole = acc_in[z] + back
        for gy in range(whole.shape[0]):
            for gx in range(whole.shape[1]):
                out_ref[gy * whole.shape[1] + gx, z] = whole[gy, gx]


def slab_path(n_gx, n_gy):
    position = {}
    for gy in range(n_gy):
        for step in range(n_gx):
            gx = step if gy % 2 == 0 else n_gx - 1 - step
            position[gy, gx] = gy * n_gx + step
    return position


def to_slabs(count, depth, position, *refs):
    odd_ref, ins, out_ref, scratch = refs[0], refs[1:-2], refs[-2], refs[-1]
    odd = odd_ref[0] == 1
    for n, ref in enumerate(ins):
        block = ref[...].reshape(BX * BY, LANES)
        scratch[...] = block.T
        for j in range(count):
            at = position[j]
            even_rows = scratch[pl.ds(depth * at, depth), :]
            odd_rows = scratch[pl.ds(depth * (count - 1 - at), depth), :]
            out_ref[j, pl.ds(depth * n, depth), :] = jnp.where(odd, odd_rows, even_rows)


def from_slabs(count, depth, position, odd_ref, in_ref, out_ref, scratch):
    odd = odd_ref[0] == 1
    for j in range(count):
        at = position[j]
        rows = in_ref[j]

        @pl.when(odd)
        def _():
            scratch[pl.ds(depth * (count - 1 - at), depth), :] = rows

        @pl.when(jnp.logical_not(odd))
        def _():
            scratch[pl.ds(depth * at, depth), :] = rows

    out_ref[...] = scratch[...].T.reshape(BX, BY, LANES)


def unpack(n_gy, n_gx, in_ref, f0, f1, f2, f3, f4, up_ref, dn_ref):
    outs = (f0, f1, f2, f3, f4)
    for n, out in enumerate(outs):
        for z in range(4):
            for gy in range(n_gy):
                rows = in_ref[pl.ds(gy * n_gx, n_gx), 4 * n + z, :]
                out[z, gy] = rows
                if n < 4:
                    if z >= 1:
                        up_ref[3 * n + z - 1, gy] = rows
                    if z <= 2:
                        dn_ref[3 * n + z, gy] = rows


def make_shards(sizes, interpret=False):
    n_gx, n_gy, n_gz = sizes["gx"], sizes["gy"], sizes["gz"]
    count = n_gx * n_gy
    depth = LANES // count
    assert depth == 4
    position = slab_path(n_gx, n_gy)
    flat_position = [position[j // n_gx, j % n_gx] for j in range(count)]
    order = []
    for gz in range(n_gz):
        line = sorted(position, key=position.get, reverse=gz % 2 == 1)
        order += [(gx * n_gy + gy) * n_gz + gz for gy, gx in line]
    total = len(order)
    upward = [(order[i], order[(i + 1) % total]) for i in range(total)]
    downward = [(order[(i + 1) % total], order[i]) for i in range(total)]
    everywhere = ("gx", "gy", "gz")
    vmem = pl.BlockSpec(memory_space=pltpu.VMEM)
    smem = pl.BlockSpec(memory_space=pltpu.SMEM)
    slab = (4, n_gy, n_gx, LANES)
    rim = (3, n_gy, n_gx, LANES)

    def like(*shape):
        return jax.ShapeDtypeStruct(shape, F32)

    def call(kernel, out_shape, *args, first=vmem, scratch=(), name=None):
        many = isinstance(out_shape, list)
        return pl.pallas_call(
            kernel,
            out_shape=out_shape,
            in_specs=[first] + [vmem] * (len(args) - 1),
            out_specs=[vmem] * len(out_shape) if many else vmem,
            scratch_shapes=list(scratch),
            name=name,
            interpret=interpret,
        )(*args)

    def exchange(up, dn):
        return lax.ppermute(up, everywhere, upward), lax.ppermute(dn, everywhere, downward)

    def shards(phi_start, section_first, section_middle, section_second, cot_final):
        odd = (lax.axis_index("gz") % 2).astype(jnp.int32).reshape(1)
        turn = pltpu.VMEM((LANES, LANES), F32)

        packed = call(
            lambda *refs: to_slabs(count, depth, flat_position, *refs),
            like(count, 5 * depth, LANES),
            odd, section_second, section_middle, section_first, phi_start, cot_final,
            first=smem, scratch=[turn], name="to_slabs",
        )
        packed = lax.all_to_all(packed, ("gy", "gx"), 0, 0)
        *fields, rim_up, rim_dn = call(
            lambda *refs: unpack(n_gy, n_gx, *refs),
            [like(*slab)] * 5 + [like(12, *slab[1:])] * 2,
            packed, name="unpack",
        )
        phi, cot = fields[3], fields[4]
        rim_lo, rim_hi = exchange(rim_up, rim_dn)

        def coefs(n):
            return call(
                lambda *refs: coef_kernel(n, *refs),
                [like(3 * PER_AXIS, *slab), like(*slab)],
                fields[n], rim_lo, rim_hi, phi, name=f"coefs_{n}",
            )

        results = [like(*slab), like(*rim), like(*rim), like(*slab), like(*slab)]
        co, pc = coefs(0)
        own, up, dn, half, acc = call(stage_one, results, cot, co, pc, name="stage_one")
        lo, hi = exchange(up, dn)
        co, pc = coefs(1)
        own, up, dn, second, acc = call(stage_two, results, half, own, lo, hi, acc, co, pc, name="stage_two")
        lo, hi = exchange(up, dn)
        co, pc = coefs(2)
        own, up, dn, middle, acc = call(stage_three, results, half, second, own, lo, hi, acc, co, pc, name="stage_three")
        lo, hi = exchange(up, dn)
        co, pc = coefs(3)
        own, up, dn, _, acc = call(stage_four, results, middle, own, lo, hi, acc, co, pc, name="stage_four")
        lo, hi = exchange(up, dn)
        slabs = call(finish, like(count, depth, LANES), own, lo, hi, acc, name="finish")
        slabs = lax.all_to_all(slabs, ("gy", "gx"), 0, 0)
        return call(
            lambda *refs: from_slabs(count, depth, flat_position, *refs),
            like(BX, BY, LANES), odd, slabs, first=smem, scratch=[turn], name="from_slabs",
        )

    return shards


def solution(mesh):
    spec = P("gx", "gy", "gz")
    return jax.shard_map(
        make_shards(dict(mesh.shape)),
        mesh=mesh,
        in_specs=(spec,) * 5,
        out_specs=spec,
        check_vma=False,
    )
```

```python
import jax
import jax.numpy as jnp
from jax import lax
from jax.experimental import pallas as pl
from jax.experimental.pallas import tpu as pltpu
from jax.sharding import PartitionSpec as P

TAU = 0.3
WENO_EPS = 1e-06
SMOOTH_EPS = 0.01
LANES = 128
BX, BY = 8, 16
F32 = jnp.float32


def lane_iota(shape):
    return lax.broadcasted_iota(jnp.int32, shape, len(shape) - 1)


def major_roll(v, k):
    n = v.shape[0]
    return jnp.concatenate([v[(g + k) % n][None] for g in range(n)], axis=0)


def shift_x(v, k):
    lane = lane_iota(v.shape)
    rolled = pltpu.roll(v, (-BY * k) % LANES, 2)
    carried = pltpu.roll(rolled, (-1 if k > 0 else 1) % v.shape[1], 1)
    crossing = lane >= LANES - BY * k if k > 0 else lane < -BY * k
    return jnp.where(crossing, carried, rolled)


def shift_y(v, k):
    inner = lane_iota(v.shape) % BY
    rolled = pltpu.roll(v, (-k) % LANES, 2)
    if k > 0:
        carried = major_roll(pltpu.roll(v, (BY - k) % LANES, 2), 1)
        return jnp.where(inner >= BY - k, carried, rolled)
    carried = major_roll(pltpu.roll(v, (-BY - k) % LANES, 2), -1)
    return jnp.where(inner < -k, carried, rolled)


def weno_center(b, dm, d0, d1, d2):
    e1, e2, e3 = d0 - dm, d1 - d0, d2 - d1
    p1, p2, p3 = 0.5 * e1 + d0, 0.5 * (d0 + d1), 0.5 * e3 - d1
    f1, f2, f3 = (13.0 / 12.0) * e1, (13.0 / 12.0) * e2, (13.0 / 12.0) * e3
    t1 = WENO_EPS + (f1 * e1 + p1 * p1)
    t2 = WENO_EPS + (f2 * e2 + p2 * p2)
    t3 = WENO_EPS + (f3 * e3 + p3 * p3)
    t12 = t1 * t2
    whole = 1.0 / (t12 * t3)
    i3 = whole * t12
    whole3 = whole * t3
    i1, i2 = whole3 * t2, whole3 * t1
    a1, a2, a3 = i1 * i1, i2 * i2, i3 * i3
    m1, m2, m3 = 0.1 * a1, 0.6 * a2, 0.3 * a3
    r1, r3 = 0.1 * a3, 0.3 * a1
    sum_m, sum_p = m1 + m2 + m3, r1 + m2 + r3
    both = 1.0 / (sum_m * sum_p)
    inv_m, inv_p = both * sum_p, both * sum_m
    w1, w2, w3 = m1 * inv_m, m2 * inv_m, m3 * inv_m
    v1, v2, v3 = r1 * inv_p, m2 * inv_p, r3 * inv_p
    y1, y3 = (e1 - e2) * (1.0 / 3.0), (e2 - e3) * (1.0 / 6.0)
    y1h, y3d = 0.5 * y1, 2.0 * y3
    corr_m = w1 * y1 + w3 * y3
    corr_p = v1 * y3d + v3 * y1h
    base = b + e2 * (1.0 / 3.0)
    minus = base + 0.5 * d0 + corr_m
    plus = base - 0.5 * d1 - corr_p
    j1, j2, j3 = -4.0 * i1, -4.0 * i2, -4.0 * i3
    g1, g3 = f1 + 0.5 * p1, f3 + 0.5 * p3
    half_p2 = 0.5 * p2

    def spread(s1, s2, s3, cy1, cy3, own0, own1):
        ce1 = cy1 + s1 * g1
        ce2 = (cy3 - cy1) + ((1.0 / 3.0) + s2 * f2)
        ce3 = s3 * g3 - cy3
        s2p = s2 * half_p2
        cd0 = s1 * p1 + s2p
        cd1 = s2p - s3 * p3
        if own0:
            cd0 = cd0 + 0.5
        if own1:
            cd1 = cd1 - 0.5
        return (-ce1, cd0 + (ce1 - ce2), cd1 + (ce2 - ce3), ce3)

    jac_m = spread(
        j1 * (w1 * (y1 - corr_m)), -j2 * (w2 * corr_m), j3 * (w3 * (y3 - corr_m)),
        w1 * (1.0 / 3.0), w3 * (1.0 / 6.0), True, False,
    )
    jac_p = spread(
        j1 * (v3 * (corr_p - y1h)), j2 * (v2 * corr_p), j3 * (v1 * (corr_p - y3d)),
        v3 * (-1.0 / 6.0), v1 * (-1.0 / 3.0), False, True,
    )
    return minus, plus, jac_m, jac_p


def upwind_term(minus, plus, side):
    u = jnp.maximum(side * minus, 0.0)
    v = jnp.maximum(-side * plus, 0.0)
    uu, vv = u * u, v * v
    gap = uu - vv
    square = gap * gap + SMOOTH_EPS
    root = lax.rsqrt(square)
    slope = gap * root
    term = 0.5 * (uu + vv + square * root)
    return term, 2.0 * ((1.0 + slope) * (u * side)), -2.0 * ((1.0 - slope) * (v * side))


PER_AXIS = 10


def coef_kernel(section, f_ref, lo_ref, hi_ref, phi_ref, co_ref, pc_ref):
    fref = f_ref

    def keep(axis, z, minus_plus, jac_m, jac_p):
        for n, part in enumerate(minus_plus + jac_m + jac_p):
            co_ref[PER_AXIS * axis + n, z] = part

    def plane(z, carry):
        f = fref[z]
        side = jnp.where(phi_ref[z] > 0, 1.0, -1.0).astype(F32)
        total = None
        for axis, shift in ((0, shift_x), (1, shift_y)):
            b = f - shift(f, -1)
            d = b - shift(b, -1)
            minus, plus, jac_m, jac_p = weno_center(b, shift(d, -1), d, shift(d, 1), shift(d, 2))
            term, by_minus, by_plus = upwind_term(minus, shift(plus, 1), side)
            keep(axis, z, (by_minus, by_plus), jac_m, jac_p)
            total = term if total is None else total + term
        pc_ref[z] = total
        return carry

    lax.fori_loop(0, 4, plane, 0)

    def column(g, carry):
        f = (
            [lo_ref[3 * section + i, g] for i in range(3)]
            + [fref[i, g] for i in range(4)]
            + [hi_ref[3 * section + i, g] for i in range(3)]
        )
        b = [None] + [f[i] - f[i - 1] for i in range(1, 10)]
        d = [None, None] + [b[i] - b[i - 1] for i in range(2, 10)]
        centers = [weno_center(b[m + 3], d[m + 2], d[m + 3], d[m + 4], d[m + 5]) for m in range(5)]
        for z in range(4):
            phi = phi_ref[z, g]
            side = jnp.where(phi > 0, 1.0, -1.0).astype(F32)
            term, by_minus, by_plus = upwind_term(centers[z][0], centers[z + 1][1], side)
            square = phi * phi + 1.0
            root = lax.rsqrt(square)
            ham2 = pc_ref[z, g] + term
            inv = lax.rsqrt(ham2)
            ham = ham2 * inv
            scale = (-0.25 * TAU) * ((phi * root) * inv)
            pc_ref[z, g] = (-TAU) * ((root * root * root) * (ham - 1.0))
            for axis in (0, 1):
                for n in (0, 1):
                    co_ref[PER_AXIS * axis + n, z, g] = co_ref[PER_AXIS * axis + n, z, g] * scale
            parts = (by_minus * scale, by_plus * scale) + centers[z][2] + centers[z + 1][3]
            for n, part in enumerate(parts):
                co_ref[PER_AXIS * 2 + n, z, g] = part
        return carry

    lax.fori_loop(0, 4, column, 0)


def apply_local(c_ref, co_ref, out_ref, up_ref, dn_ref):
    def plane(z, carry):
        c = c_ref[z]
        total = None
        for axis, shift in ((0, shift_x), (1, shift_y)):
            co = lambda n: co_ref[PER_AXIS * axis + n, z]
            a = c * co(0)
            g = shift(c * co(1), -1)
            t = [a * co(2 + k) + g * co(6 + k) for k in range(4)]
            dbar = t[1] + shift(t[0], 1) + shift(t[2], -1) + shift(t[3], -2)
            bbar = (a + g) + (dbar - shift(dbar, 1))
            part = bbar - shift(bbar, 1)
            total = part if total is None else total + part
        out_ref[z] = total
        return carry

    lax.fori_loop(0, 4, plane, 0)

    def column(g, carry):
        dbar = [None] * 8
        bbar = [None] * 9

        def add(into, at, value):
            into[at] = value if into[at] is None else into[at] + value

        for z in range(4):
            c = c_ref[z, g]
            co = lambda n: co_ref[PER_AXIS * 2 + n, z, g]
            a, p = c * co(0), c * co(1)
            for k in range(4):
                add(dbar, z + k, a * co(2 + k))
                add(dbar, z + k + 1, p * co(6 + k))
            add(bbar, z + 2, a)
            add(bbar, z + 3, p)
        for j in range(8):
            add(bbar, j + 1, dbar[j])
            add(bbar, j, -dbar[j])
        for z in range(4):
            out_ref[z, g] = out_ref[z, g] + (bbar[z + 2] - bbar[z + 3])
        for k in range(3):
            up_ref[k, g] = bbar[6 + k]
            dn_ref[k, g] = bbar[k]
        return carry

    lax.fori_loop(0, 4, column, 0)


def joined(own_ref, lo_ref, hi_ref):
    lo0, lo1, lo2 = lo_ref[0], lo_ref[1], lo_ref[2]
    hi0, hi1, hi2 = hi_ref[0], hi_ref[1], hi_ref[2]
    return (
        own_ref[0] + (lo0 - lo1),
        own_ref[1] + (lo1 - lo2 - hi0),
        own_ref[2] + (lo2 + hi0 - hi1),
        own_ref[3] + (hi1 - hi2),
    )


def stage_one(cot_ref, co_ref, pc_ref, own_ref, up_ref, dn_ref, c_ref, acc_ref):
    half = 0.5 * cot_ref[...]
    c_ref[...] = half
    acc_ref[...] = pc_ref[...] * half
    apply_local(c_ref, co_ref, own_ref, up_ref, dn_ref)


def stage_two(half_ref, own_in, lo_ref, hi_ref, acc_in, co_ref, pc_ref, own_ref, up_ref, dn_ref, c_ref, acc_ref):
    for z, back in enumerate(joined(own_in, lo_ref, hi_ref)):
        c = half_ref[z] + back
        c_ref[z] = c
        acc_ref[z] = acc_in[z] + pc_ref[z] * c
    apply_local(c_ref, co_ref, own_ref, up_ref, dn_ref)


def stage_three(half_ref, second_ref, own_in, lo_ref, hi_ref, acc_in, co_ref, pc_ref, own_ref, up_ref, dn_ref, c_ref, acc_ref):
    for z, back in enumerate(joined(own_in, lo_ref, hi_ref)):
        c = 0.5 * (half_ref[z] + second_ref[z] + back)
        c_ref[z] = c
        acc_ref[z] = acc_in[z] + pc_ref[z] * c
    apply_local(c_ref, co_ref, own_ref, up_ref, dn_ref)


def stage_four(middle_ref, own_in, lo_ref, hi_ref, acc_in, co_ref, pc_ref, own_ref, up_ref, dn_ref, c_ref, acc_ref):
    for z, back in enumerate(joined(own_in, lo_ref, hi_ref)):
        c = middle_ref[z] + back
        c_ref[z] = c
        acc_ref[z] = acc_in[z] + pc_ref[z] * c + (middle_ref[z] + c)
    apply_local(c_ref, co_ref, own_ref, up_ref, dn_ref)


def finish(own_in, lo_ref, hi_ref, acc_in, out_ref):
    for z, back in enumerate(joined(own_in, lo_ref, hi_ref)):
        whole = acc_in[z] + back
        for gy in range(whole.shape[0]):
            for gx in range(whole.shape[1]):
                out_ref[gy * whole.shape[1] + gx, z] = whole[gy, gx]


def slab_path(n_gx, n_gy):
    position = {}
    for gy in range(n_gy):
        for step in range(n_gx):
            gx = step if gy % 2 == 0 else n_gx - 1 - step
            position[gy, gx] = gy * n_gx + step
    return position


def to_slabs(count, depth, position, *refs):
    odd_ref, ins, out_ref, scratch = refs[0], refs[1:-2], refs[-2], refs[-1]
    odd = odd_ref[0] == 1
    for n, ref in enumerate(ins):
        block = ref[...].reshape(BX * BY, LANES)
        scratch[...] = block.T
        for j in range(count):
            at = position[j]
            even_rows = scratch[pl.ds(depth * at, depth), :]
            odd_rows = scratch[pl.ds(depth * (count - 1 - at), depth), :]
            out_ref[j, pl.ds(depth * n, depth), :] = jnp.where(odd, odd_rows, even_rows)


def from_slabs(count, depth, position, odd_ref, in_ref, out_ref, scratch):
    odd = odd_ref[0] == 1
    for j in range(count):
        at = position[j]
        rows = in_ref[j]

        @pl.when(odd)
        def _():
            scratch[pl.ds(depth * (count - 1 - at), depth), :] = rows

        @pl.when(jnp.logical_not(odd))
        def _():
            scratch[pl.ds(depth * at, depth), :] = rows

    out_ref[...] = scratch[...].T.reshape(BX, BY, LANES)


def unpack(n_gy, n_gx, in_ref, f0, f1, f2, f3, f4, up_ref, dn_ref):
    outs = (f0, f1, f2, f3, f4)
    for n, out in enumerate(outs):
        for z in range(4):
            for gy in range(n_gy):
                rows = in_ref[pl.ds(gy * n_gx, n_gx), 4 * n + z, :]
                out[z, gy] = rows
                if n < 4:
                    if z >= 1:
                        up_ref[3 * n + z - 1, gy] = rows
                    if z <= 2:
                        dn_ref[3 * n + z, gy] = rows


def make_shards(sizes, interpret=False):
    n_gx, n_gy, n_gz = sizes["gx"], sizes["gy"], sizes["gz"]
    count = n_gx * n_gy
    depth = LANES // count
    assert depth == 4
    position = slab_path(n_gx, n_gy)
    flat_position = [position[j // n_gx, j % n_gx] for j in range(count)]
    order = []
    for gz in range(n_gz):
        line = sorted(position, key=position.get, reverse=gz % 2 == 1)
        order += [(gx * n_gy + gy) * n_gz + gz for gy, gx in line]
    total = len(order)
    upward = [(order[i], order[(i + 1) % total]) for i in range(total)]
    downward = [(order[(i + 1) % total], order[i]) for i in range(total)]
    everywhere = ("gx", "gy", "gz")
    vmem = pl.BlockSpec(memory_space=pltpu.VMEM)
    smem = pl.BlockSpec(memory_space=pltpu.SMEM)
    slab = (4, n_gy, n_gx, LANES)
    rim = (3, n_gy, n_gx, LANES)

    def like(*shape):
        return jax.ShapeDtypeStruct(shape, F32)

    def near(*shape):
        return like(*shape) if interpret else pltpu.VMEM(shape, F32)

    def call(kernel, out_shape, *args, first=vmem, scratch=(), name=None, far=False):
        many = isinstance(out_shape, list)
        if not (far or interpret):
            args = [
                x if x.ndim == 1 else pltpu.with_memory_space_constraint(x, pltpu.VMEM) for x in args
            ]
        return pl.pallas_call(
            kernel,
            out_shape=out_shape,
            in_specs=[first] + [vmem] * (len(args) - 1),
            out_specs=[vmem] * len(out_shape) if many else vmem,
            scratch_shapes=list(scratch),
            compiler_params=pltpu.CompilerParams(vmem_limit_bytes=8 << 20),
            name=name,
            interpret=interpret,
        )(*args)

    def exchange(up, dn):
        return lax.ppermute(up, everywhere, upward), lax.ppermute(dn, everywhere, downward)

    def shards(phi_start, section_first, section_middle, section_second, cot_final):
        odd = (lax.axis_index("gz") % 2).astype(jnp.int32).reshape(1)
        turn = pltpu.VMEM((LANES, LANES), F32)

        packed = call(
            lambda *refs: to_slabs(count, depth, flat_position, *refs),
            near(count, 5 * depth, LANES),
            odd, section_second, section_middle, section_first, phi_start, cot_final,
            first=smem, far=True, scratch=[turn], name="to_slabs",
        )
        packed = lax.all_to_all(packed, ("gy", "gx"), 0, 0)
        *fields, rim_up, rim_dn = call(
            lambda *refs: unpack(n_gy, n_gx, *refs),
            [near(*slab)] * 5 + [near(12, *slab[1:])] * 2,
            packed, name="unpack",
        )
        phi, cot = fields[3], fields[4]
        rim_lo, rim_hi = exchange(rim_up, rim_dn)

        def coefs(n):
            return call(
                lambda *refs: coef_kernel(n, *refs),
                [near(3 * PER_AXIS, *slab), near(*slab)],
                fields[n], rim_lo, rim_hi, phi, name=f"coefs_{n}",
            )

        results = [near(*slab), near(*rim), near(*rim), near(*slab), near(*slab)]
        co, pc = coefs(0)
        own, up, dn, half, acc = call(stage_one, results, cot, co, pc, name="stage_one")
        lo, hi = exchange(up, dn)
        co, pc = coefs(1)
        own, up, dn, second, acc = call(stage_two, results, half, own, lo, hi, acc, co, pc, name="stage_two")
        lo, hi = exchange(up, dn)
        co, pc = coefs(2)
        own, up, dn, middle, acc = call(stage_three, results, half, second, own, lo, hi, acc, co, pc, name="stage_three")
        lo, hi = exchange(up, dn)
        co, pc = coefs(3)
        own, up, dn, _, acc = call(stage_four, results, middle, own, lo, hi, acc, co, pc, name="stage_four")
        lo, hi = exchange(up, dn)
        slabs = call(finish, near(count, depth, LANES), own, lo, hi, acc, name="finish")
        slabs = lax.all_to_all(slabs, ("gy", "gx"), 0, 0)
        return call(
            lambda *refs: from_slabs(count, depth, flat_position, *refs),
            like(BX, BY, LANES), odd, slabs, first=smem, scratch=[turn], name="from_slabs",
        )

    return shards


def solution(mesh):
    spec = P("gx", "gy", "gz")
    return jax.shard_map(
        make_shards(dict(mesh.shape)),
        mesh=mesh,
        in_specs=(spec,) * 5,
        out_specs=spec,
        check_vma=False,
    )
```

```python
import jax
import jax.numpy as jnp
from jax import lax
from jax.experimental import pallas as pl
from jax.experimental.pallas import tpu as pltpu
from jax.sharding import PartitionSpec as P

TAU = 0.3
WENO_EPS = 1e-06
SMOOTH_EPS = 0.01
UNROLL = 1
LANES = 128
BX, BY = 8, 16
F32 = jnp.float32


def lane_iota(shape):
    return lax.broadcasted_iota(jnp.int32, shape, len(shape) - 1)


def major_roll(v, k):
    n = v.shape[0]
    return jnp.concatenate([v[(g + k) % n][None] for g in range(n)], axis=0)


def shift_x(v, k):
    lane = lane_iota(v.shape)
    rolled = pltpu.roll(v, (-BY * k) % LANES, 2)
    carried = pltpu.roll(rolled, (-1 if k > 0 else 1) % v.shape[1], 1)
    crossing = lane >= LANES - BY * k if k > 0 else lane < -BY * k
    return jnp.where(crossing, carried, rolled)


def shift_y(v, k):
    inner = lane_iota(v.shape) % BY
    rolled = pltpu.roll(v, (-k) % LANES, 2)
    if k > 0:
        carried = major_roll(pltpu.roll(v, (BY - k) % LANES, 2), 1)
        return jnp.where(inner >= BY - k, carried, rolled)
    carried = major_roll(pltpu.roll(v, (-BY - k) % LANES, 2), -1)
    return jnp.where(inner < -k, carried, rolled)


def weno_center(b, dm, d0, d1, d2):
    e1, e2, e3 = d0 - dm, d1 - d0, d2 - d1
    p1, p2, p3 = 0.5 * e1 + d0, 0.5 * (d0 + d1), 0.5 * e3 - d1
    f1, f2, f3 = (13.0 / 12.0) * e1, (13.0 / 12.0) * e2, (13.0 / 12.0) * e3
    t1 = WENO_EPS + (f1 * e1 + p1 * p1)
    t2 = WENO_EPS + (f2 * e2 + p2 * p2)
    t3 = WENO_EPS + (f3 * e3 + p3 * p3)
    t12 = t1 * t2
    whole = 1.0 / (t12 * t3)
    i3 = whole * t12
    whole3 = whole * t3
    i1, i2 = whole3 * t2, whole3 * t1
    a1, a2, a3 = i1 * i1, i2 * i2, i3 * i3
    m1, m2, m3 = 0.1 * a1, 0.6 * a2, 0.3 * a3
    r1, r3 = 0.1 * a3, 0.3 * a1
    sum_m, sum_p = m1 + m2 + m3, r1 + m2 + r3
    both = 1.0 / (sum_m * sum_p)
    inv_m, inv_p = both * sum_p, both * sum_m
    w1, w2, w3 = m1 * inv_m, m2 * inv_m, m3 * inv_m
    v1, v2, v3 = r1 * inv_p, m2 * inv_p, r3 * inv_p
    y1, y3 = (e1 - e2) * (1.0 / 3.0), (e2 - e3) * (1.0 / 6.0)
    y1h, y3d = 0.5 * y1, 2.0 * y3
    corr_m = w1 * y1 + w3 * y3
    corr_p = v1 * y3d + v3 * y1h
    base = b + e2 * (1.0 / 3.0)
    minus = base + 0.5 * d0 + corr_m
    plus = base - 0.5 * d1 - corr_p
    j1, j2, j3 = -4.0 * i1, -4.0 * i2, -4.0 * i3
    g1, g3 = f1 + 0.5 * p1, f3 + 0.5 * p3
    half_p2 = 0.5 * p2

    def spread(s1, s2, s3, cy1, cy3, own0, own1):
        ce1 = cy1 + s1 * g1
        ce2 = (cy3 - cy1) + ((1.0 / 3.0) + s2 * f2)
        ce3 = s3 * g3 - cy3
        s2p = s2 * half_p2
        cd0 = s1 * p1 + s2p
        cd1 = s2p - s3 * p3
        if own0:
            cd0 = cd0 + 0.5
        if own1:
            cd1 = cd1 - 0.5
        return (-ce1, cd0 + (ce1 - ce2), cd1 + (ce2 - ce3), ce3)

    jac_m = spread(
        j1 * (w1 * (y1 - corr_m)), -j2 * (w2 * corr_m), j3 * (w3 * (y3 - corr_m)),
        w1 * (1.0 / 3.0), w3 * (1.0 / 6.0), True, False,
    )
    jac_p = spread(
        j1 * (v3 * (corr_p - y1h)), j2 * (v2 * corr_p), j3 * (v1 * (corr_p - y3d)),
        v3 * (-1.0 / 6.0), v1 * (-1.0 / 3.0), False, True,
    )
    return minus, plus, jac_m, jac_p


def upwind_term(minus, plus, side):
    u = jnp.maximum(side * minus, 0.0)
    v = jnp.maximum(-side * plus, 0.0)
    uu, vv = u * u, v * v
    gap = uu - vv
    square = gap * gap + SMOOTH_EPS
    root = lax.rsqrt(square)
    slope = gap * root
    term = 0.5 * (uu + vv + square * root)
    return term, 2.0 * ((1.0 + slope) * (u * side)), -2.0 * ((1.0 - slope) * (v * side))


PER_AXIS = 10


def side_of(phi):
    return jnp.where(phi > 0, 1.0, -1.0).astype(F32)


def coef_plane_kernel(f_ref, phi_ref, co_ref, sum_ref):
    def plane(z, carry):
        f = f_ref[z]
        side = side_of(phi_ref[z])
        total = None
        for axis, shift in ((0, shift_x), (1, shift_y)):
            b = f - shift(f, -1)
            d = b - shift(b, -1)
            minus, plus, jac_m, jac_p = weno_center(b, shift(d, -1), d, shift(d, 1), shift(d, 2))
            term, by_minus, by_plus = upwind_term(minus, shift(plus, 1), side)
            for n, part in enumerate((by_minus, by_plus) + jac_m + jac_p):
                co_ref[PER_AXIS * axis + n, z] = part
            total = term if total is None else total + term
        sum_ref[z] = total
        return carry

    lax.fori_loop(0, 4, plane, 0)


def coef_depth_kernel(section, f_ref, lo_ref, hi_ref, phi_ref, sum_ref, co_ref, scale_ref, pc_ref):
    def column(g, carry):
        f = (
            [lo_ref[3 * section + i, g] for i in range(3)]
            + [f_ref[i, g] for i in range(4)]
            + [hi_ref[3 * section + i, g] for i in range(3)]
        )
        b = [None] + [f[i] - f[i - 1] for i in range(1, 10)]
        d = [None, None] + [b[i] - b[i - 1] for i in range(2, 10)]
        centers = [weno_center(b[m + 3], d[m + 2], d[m + 3], d[m + 4], d[m + 5]) for m in range(5)]
        for z in range(4):
            phi = phi_ref[z, g]
            term, by_minus, by_plus = upwind_term(centers[z][0], centers[z + 1][1], side_of(phi))
            root = lax.rsqrt(phi * phi + 1.0)
            square = sum_ref[z, g] + term
            inv = lax.rsqrt(square)
            scale_ref[z, g] = (-0.25 * TAU) * ((phi * root) * inv)
            pc_ref[z, g] = (-TAU) * ((root * root * root) * (square * inv - 1.0))
            parts = (by_minus, by_plus) + centers[z][2] + centers[z + 1][3]
            for n, part in enumerate(parts):
                co_ref[n, z, g] = part
        return carry

    lax.fori_loop(0, 4, column, 0)


def apply_local(c_ref, cxy_ref, cz_ref, scale_ref, out_ref, up_ref, dn_ref):
    def plane(z, carry):
        c = c_ref[z] * scale_ref[z]
        total = None
        for axis, shift in ((0, shift_x), (1, shift_y)):
            co = lambda n: cxy_ref[PER_AXIS * axis + n, z]
            a = c * co(0)
            g = shift(c * co(1), -1)
            t = [a * co(2 + k) + g * co(6 + k) for k in range(4)]
            dbar = t[1] + shift(t[0], 1) + shift(t[2], -1) + shift(t[3], -2)
            bbar = (a + g) + (dbar - shift(dbar, 1))
            part = bbar - shift(bbar, 1)
            total = part if total is None else total + part
        out_ref[z] = total
        return carry

    lax.fori_loop(0, 4, plane, 0, unroll=UNROLL)

    def column(g, carry):
        dbar = [None] * 8
        bbar = [None] * 9

        def add(into, at, value):
            into[at] = value if into[at] is None else into[at] + value

        for z in range(4):
            c = c_ref[z, g] * scale_ref[z, g]
            co = lambda n: cz_ref[n, z, g]
            a, p = c * co(0), c * co(1)
            for k in range(4):
                add(dbar, z + k, a * co(2 + k))
                add(dbar, z + k + 1, p * co(6 + k))
            add(bbar, z + 2, a)
            add(bbar, z + 3, p)
        for j in range(8):
            add(bbar, j + 1, dbar[j])
            add(bbar, j, -dbar[j])
        for z in range(4):
            out_ref[z, g] = out_ref[z, g] + (bbar[z + 2] - bbar[z + 3])
        for k in range(3):
            up_ref[k, g] = bbar[6 + k]
            dn_ref[k, g] = bbar[k]
        return carry

    lax.fori_loop(0, 4, column, 0, unroll=UNROLL)


def joined(own_ref, lo_ref, hi_ref):
    lo0, lo1, lo2 = lo_ref[0], lo_ref[1], lo_ref[2]
    hi0, hi1, hi2 = hi_ref[0], hi_ref[1], hi_ref[2]
    return (
        own_ref[0] + (lo0 - lo1),
        own_ref[1] + (lo1 - lo2 - hi0),
        own_ref[2] + (lo2 + hi0 - hi1),
        own_ref[3] + (hi1 - hi2),
    )


def stage_one(cot_ref, cxy_ref, cz_ref, scale_ref, pc_ref, own_ref, up_ref, dn_ref, c_ref, acc_ref):
    half = 0.5 * cot_ref[...]
    c_ref[...] = half
    acc_ref[...] = pc_ref[...] * half
    apply_local(c_ref, cxy_ref, cz_ref, scale_ref, own_ref, up_ref, dn_ref)


def stage_two(half_ref, own_in, lo_ref, hi_ref, acc_in, cxy_ref, cz_ref, scale_ref, pc_ref, own_ref, up_ref, dn_ref, c_ref, acc_ref):
    for z, back in enumerate(joined(own_in, lo_ref, hi_ref)):
        c = half_ref[z] + back
        c_ref[z] = c
        acc_ref[z] = acc_in[z] + pc_ref[z] * c
    apply_local(c_ref, cxy_ref, cz_ref, scale_ref, own_ref, up_ref, dn_ref)


def stage_three(half_ref, second_ref, own_in, lo_ref, hi_ref, acc_in, cxy_ref, cz_ref, scale_ref, pc_ref, own_ref, up_ref, dn_ref, c_ref, acc_ref):
    for z, back in enumerate(joined(own_in, lo_ref, hi_ref)):
        c = 0.5 * (half_ref[z] + second_ref[z] + back)
        c_ref[z] = c
        acc_ref[z] = acc_in[z] + pc_ref[z] * c
    apply_local(c_ref, cxy_ref, cz_ref, scale_ref, own_ref, up_ref, dn_ref)


def stage_four(middle_ref, own_in, lo_ref, hi_ref, acc_in, cxy_ref, cz_ref, scale_ref, pc_ref, own_ref, up_ref, dn_ref, c_ref, acc_ref):
    for z, back in enumerate(joined(own_in, lo_ref, hi_ref)):
        c = middle_ref[z] + back
        c_ref[z] = c
        acc_ref[z] = acc_in[z] + pc_ref[z] * c + (middle_ref[z] + c)
    apply_local(c_ref, cxy_ref, cz_ref, scale_ref, own_ref, up_ref, dn_ref)


def finish(own_in, lo_ref, hi_ref, acc_in, out_ref):
    for z, back in enumerate(joined(own_in, lo_ref, hi_ref)):
        whole = acc_in[z] + back
        for gy in range(whole.shape[0]):
            for gx in range(whole.shape[1]):
                out_ref[gy * whole.shape[1] + gx, z] = whole[gy, gx]


def slab_path(n_gx, n_gy):
    position = {}
    for gy in range(n_gy):
        for step in range(n_gx):
            gx = step if gy % 2 == 0 else n_gx - 1 - step
            position[gy, gx] = gy * n_gx + step
    return position


def to_slabs(count, depth, position, *refs):
    odd_ref, ins, out_ref, scratch = refs[0], refs[1:-2], refs[-2], refs[-1]
    odd = odd_ref[0] == 1
    for n, ref in enumerate(ins):
        block = ref[...].reshape(BX * BY, LANES)
        scratch[...] = block.T
        for j in range(count):
            at = position[j]
            even_rows = scratch[pl.ds(depth * at, depth), :]
            odd_rows = scratch[pl.ds(depth * (count - 1 - at), depth), :]
            out_ref[j, pl.ds(depth * n, depth), :] = jnp.where(odd, odd_rows, even_rows)


def from_slabs(count, depth, position, odd_ref, in_ref, out_ref, scratch):
    odd = odd_ref[0] == 1
    for j in range(count):
        at = position[j]
        rows = in_ref[j]

        @pl.when(odd)
        def _():
            scratch[pl.ds(depth * (count - 1 - at), depth), :] = rows

        @pl.when(jnp.logical_not(odd))
        def _():
            scratch[pl.ds(depth * at, depth), :] = rows

    out_ref[...] = scratch[...].T.reshape(BX, BY, LANES)


def unpack(n_gy, n_gx, in_ref, f0, f1, f2, f3, f4, up_ref, dn_ref):
    outs = (f0, f1, f2, f3, f4)
    for n, out in enumerate(outs):
        for z in range(4):
            for gy in range(n_gy):
                rows = in_ref[pl.ds(gy * n_gx, n_gx), 4 * n + z, :]
                out[z, gy] = rows
                if n < 4:
                    if z >= 1:
                        up_ref[3 * n + z - 1, gy] = rows
                    if z <= 2:
                        dn_ref[3 * n + z, gy] = rows


def make_shards(sizes, interpret=False):
    n_gx, n_gy, n_gz = sizes["gx"], sizes["gy"], sizes["gz"]
    count = n_gx * n_gy
    depth = LANES // count
    assert depth == 4
    position = slab_path(n_gx, n_gy)
    flat_position = [position[j // n_gx, j % n_gx] for j in range(count)]
    order = []
    for gz in range(n_gz):
        line = sorted(position, key=position.get, reverse=gz % 2 == 1)
        order += [(gx * n_gy + gy) * n_gz + gz for gy, gx in line]
    total = len(order)
    upward = [(order[i], order[(i + 1) % total]) for i in range(total)]
    downward = [(order[(i + 1) % total], order[i]) for i in range(total)]
    everywhere = ("gx", "gy", "gz")
    vmem = pl.BlockSpec(memory_space=pltpu.VMEM)
    smem = pl.BlockSpec(memory_space=pltpu.SMEM)
    slab = (4, n_gy, n_gx, LANES)
    rim = (3, n_gy, n_gx, LANES)

    def like(*shape):
        return jax.ShapeDtypeStruct(shape, F32)

    def near(*shape):
        return like(*shape) if interpret else pltpu.VMEM(shape, F32)

    def call(kernel, out_shape, *args, first=vmem, scratch=(), name=None, far=False):
        many = isinstance(out_shape, list)
        if not interpret:
            space = pltpu.HBM if far else pltpu.VMEM
            args = [x if x.ndim == 1 else pltpu.with_memory_space_constraint(x, space) for x in args]
        return pl.pallas_call(
            kernel,
            out_shape=out_shape,
            in_specs=[first] + [vmem] * (len(args) - 1),
            out_specs=[vmem] * len(out_shape) if many else vmem,
            scratch_shapes=list(scratch),
            compiler_params=pltpu.CompilerParams(vmem_limit_bytes=8 << 20),
            name=name,
            interpret=interpret,
        )(*args)

    def exchange(up, dn):
        return lax.ppermute(up, everywhere, upward), lax.ppermute(dn, everywhere, downward)

    def shards(phi_start, section_first, section_middle, section_second, cot_final):
        odd = (lax.axis_index("gz") % 2).astype(jnp.int32).reshape(1)
        turn = pltpu.VMEM((LANES, LANES), F32)

        packed = call(
            lambda *refs: to_slabs(count, depth, flat_position, *refs),
            near(count, 5 * depth, LANES),
            odd, section_second, section_middle, section_first, phi_start, cot_final,
            first=smem, far=True, scratch=[turn], name="to_slabs",
        )
        packed = lax.all_to_all(packed, ("gy", "gx"), 0, 0)
        *fields, rim_up, rim_dn = call(
            lambda *refs: unpack(n_gy, n_gx, *refs),
            [near(*slab)] * 5 + [near(12, *slab[1:])] * 2,
            packed, name="unpack",
        )
        phi, cot = fields[3], fields[4]
        rim_lo, rim_hi = exchange(rim_up, rim_dn)

        def coef_plane(n):
            return call(
                coef_plane_kernel, [near(2 * PER_AXIS, *slab), near(*slab)],
                fields[n], phi, name=f"coef_plane_{n}",
            )

        def coef_depth(n, total):
            return call(
                lambda *refs: coef_depth_kernel(n, *refs),
                [near(PER_AXIS, *slab), near(*slab), near(*slab)],
                fields[n], rim_lo, rim_hi, phi, total, name=f"coef_depth_{n}",
            )

        def coefs(n):
            flat, total = coef_plane(n)
            return (flat, *coef_depth(n, total))

        results = [near(*slab), near(*rim), near(*rim), near(*slab), near(*slab)]
        own, up, dn, half, acc = call(stage_one, results, cot, *coefs(0), name="stage_one")
        lo, hi = exchange(up, dn)
        own, up, dn, second, acc = call(
            stage_two, results, half, own, lo, hi, acc, *coefs(1), name="stage_two"
        )
        lo, hi = exchange(up, dn)
        own, up, dn, middle, acc = call(
            stage_three, results, half, second, own, lo, hi, acc, *coefs(2), name="stage_three"
        )
        lo, hi = exchange(up, dn)
        own, up, dn, _, acc = call(
            stage_four, results, middle, own, lo, hi, acc, *coefs(3), name="stage_four"
        )
        lo, hi = exchange(up, dn)
        slabs = call(finish, near(count, depth, LANES), own, lo, hi, acc, name="finish")
        slabs = lax.all_to_all(slabs, ("gy", "gx"), 0, 0)
        return call(
            lambda *refs: from_slabs(count, depth, flat_position, *refs),
            like(BX, BY, LANES), odd, slabs, first=smem, scratch=[turn], name="from_slabs",
        )

    return shards


def solution(mesh):
    spec = P("gx", "gy", "gz")
    return jax.shard_map(
        make_shards(dict(mesh.shape)),
        mesh=mesh,
        in_specs=(spec,) * 5,
        out_specs=spec,
        check_vma=False,
    )
```

```python
import jax
import jax.numpy as jnp
from jax import lax
from jax.experimental import pallas as pl
from jax.experimental.pallas import tpu as pltpu
from jax.sharding import PartitionSpec as P

TAU = 0.3
WENO_EPS = 1e-06
SMOOTH_EPS = 0.01
UNROLL_COEF = 2
UNROLL_DEPTH = 2
UNROLL_APPLY = 4
LANES = 128
BX, BY = 8, 16
F32 = jnp.float32


def lane_iota(shape):
    return lax.broadcasted_iota(jnp.int32, shape, len(shape) - 1)


def major_roll(v, k):
    n = v.shape[0]
    return jnp.concatenate([v[(g + k) % n][None] for g in range(n)], axis=0)


def shift_x(v, k):
    lane = lane_iota(v.shape)
    rolled = pltpu.roll(v, (-BY * k) % LANES, 2)
    carried = pltpu.roll(rolled, (-1 if k > 0 else 1) % v.shape[1], 1)
    crossing = lane >= LANES - BY * k if k > 0 else lane < -BY * k
    return jnp.where(crossing, carried, rolled)


def shift_y(v, k):
    inner = lane_iota(v.shape) % BY
    rolled = pltpu.roll(v, (-k) % LANES, 2)
    if k > 0:
        carried = major_roll(pltpu.roll(v, (BY - k) % LANES, 2), 1)
        return jnp.where(inner >= BY - k, carried, rolled)
    carried = major_roll(pltpu.roll(v, (-BY - k) % LANES, 2), -1)
    return jnp.where(inner < -k, carried, rolled)


def shifts_x(v, steps):
    lane = lane_iota(v.shape)
    n = v.shape[1]
    rolled = {k: pltpu.roll(v, (-BY * k) % LANES, 2) for k in steps}
    out = {}
    for k, r in rolled.items():
        carried = pltpu.roll(r, (-1 if k > 0 else 1) % n, 1)
        out[k] = jnp.where(lane >= LANES - BY * k if k > 0 else lane < -BY * k, carried, r)
    return out, rolled


def shifts_y(v, steps, rolled):
    inner = lane_iota(v.shape) % BY
    ahead, behind = major_roll(rolled[-1], 1), major_roll(rolled[1], -1)
    out = {}
    for k in steps:
        mixed = jnp.where(inner < k, ahead, v) if k > 0 else jnp.where(inner >= BY + k, behind, v)
        out[k] = pltpu.roll(mixed, (-k) % LANES, 2)
    return out


def gather_x(parts):
    total = parts[0]
    for k, part in parts.items():
        if k:
            total = total + shift_x(part, k)
    return total


def gather_y(parts):
    total = parts[0]
    inner = lane_iota(total.shape) % BY
    ahead = behind = None
    for k, part in parts.items():
        if k == 0:
            continue
        moved = pltpu.roll(part, (-k) % LANES, 2)
        crossing = inner >= BY - k if k > 0 else inner < -k
        total = total + jnp.where(crossing, 0.0, moved)
        over = jnp.where(crossing, moved, 0.0)
        if k > 0:
            ahead = over if ahead is None else ahead + over
        else:
            behind = over if behind is None else behind + over
    if ahead is not None:
        total = total + major_roll(pltpu.roll(ahead, BY, 2), 1)
    if behind is not None:
        total = total + major_roll(pltpu.roll(behind, LANES - BY, 2), -1)
    return total


def weno_center(b, dm, d0, d1, d2):
    e1, e2, e3 = d0 - dm, d1 - d0, d2 - d1
    p1, p2, p3 = 0.5 * e1 + d0, 0.5 * (d0 + d1), 0.5 * e3 - d1
    f1, f2, f3 = (13.0 / 12.0) * e1, (13.0 / 12.0) * e2, (13.0 / 12.0) * e3
    t1 = WENO_EPS + (f1 * e1 + p1 * p1)
    t2 = WENO_EPS + (f2 * e2 + p2 * p2)
    t3 = WENO_EPS + (f3 * e3 + p3 * p3)
    t12 = t1 * t2
    whole = 1.0 / (t12 * t3)
    i3 = whole * t12
    whole3 = whole * t3
    i1, i2 = whole3 * t2, whole3 * t1
    a1, a2, a3 = i1 * i1, i2 * i2, i3 * i3
    m1, m2, m3 = 0.1 * a1, 0.6 * a2, 0.3 * a3
    r1, r3 = 0.1 * a3, 0.3 * a1
    sum_m, sum_p = m1 + m2 + m3, r1 + m2 + r3
    both = 1.0 / (sum_m * sum_p)
    inv_m, inv_p = both * sum_p, both * sum_m
    w1, w2, w3 = m1 * inv_m, m2 * inv_m, m3 * inv_m
    v1, v2, v3 = r1 * inv_p, m2 * inv_p, r3 * inv_p
    y1, y3 = (e1 - e2) * (1.0 / 3.0), (e2 - e3) * (1.0 / 6.0)
    y1h, y3d = 0.5 * y1, 2.0 * y3
    corr_m = w1 * y1 + w3 * y3
    corr_p = v1 * y3d + v3 * y1h
    base = b + e2 * (1.0 / 3.0)
    minus = base + 0.5 * d0 + corr_m
    plus = base - 0.5 * d1 - corr_p
    j1, j2, j3 = -4.0 * i1, -4.0 * i2, -4.0 * i3
    g1, g3 = f1 + 0.5 * p1, f3 + 0.5 * p3
    half_p2 = 0.5 * p2

    def spread(s1, s2, s3, cy1, cy3, own0, own1):
        ce1 = cy1 + s1 * g1
        ce2 = (cy3 - cy1) + ((1.0 / 3.0) + s2 * f2)
        ce3 = s3 * g3 - cy3
        s2p = s2 * half_p2
        cd0 = s1 * p1 + s2p
        cd1 = s2p - s3 * p3
        if own0:
            cd0 = cd0 + 0.5
        if own1:
            cd1 = cd1 - 0.5
        return (-ce1, cd0 + (ce1 - ce2), cd1 + (ce2 - ce3), ce3)

    jac_m = spread(
        j1 * (w1 * (y1 - corr_m)), -j2 * (w2 * corr_m), j3 * (w3 * (y3 - corr_m)),
        w1 * (1.0 / 3.0), w3 * (1.0 / 6.0), True, False,
    )
    jac_p = spread(
        j1 * (v3 * (corr_p - y1h)), j2 * (v2 * corr_p), j3 * (v1 * (corr_p - y3d)),
        v3 * (-1.0 / 6.0), v1 * (-1.0 / 3.0), False, True,
    )
    return minus, plus, jac_m, jac_p


def upwind_term(minus, plus, side):
    u = jnp.maximum(side * minus, 0.0)
    v = jnp.maximum(-side * plus, 0.0)
    uu, vv = u * u, v * v
    gap = uu - vv
    square = gap * gap + SMOOTH_EPS
    root = lax.rsqrt(square)
    slope = gap * root
    term = 0.5 * (uu + vv + square * root)
    return term, 2.0 * ((1.0 + slope) * (u * side)), -2.0 * ((1.0 - slope) * (v * side))


PER_AXIS = 10


def side_of(phi):
    return jnp.where(phi > 0, 1.0, -1.0).astype(F32)


def coef_planes(f_ref, phi_ref, co_ref, sum_ref):
    def plane(z, carry):
        f = f_ref[z]
        side = side_of(phi_ref[z])
        steps = (-3, -2, -1, 1, 2)
        along_x, rolled = shifts_x(f, steps)
        along_y = shifts_y(f, steps, rolled)
        total = None
        for axis, shift, near in ((0, shift_x, along_x), (1, shift_y, along_y)):
            b = [near[-2] - near[-3], near[-1] - near[-2], f - near[-1], near[1] - f, near[2] - near[1]]
            d = [b[i + 1] - b[i] for i in range(4)]
            minus, plus, jac_m, jac_p = weno_center(b[2], *d)
            term, by_minus, by_plus = upwind_term(minus, shift(plus, 1), side)
            for n, part in enumerate((by_minus, by_plus) + jac_m + jac_p):
                co_ref[PER_AXIS * axis + n, z] = part
            total = term if total is None else total + term
        sum_ref[z] = total
        return carry

    lax.fori_loop(0, 4, plane, 0, unroll=UNROLL_COEF)


def coef_depth(section, f_ref, lo_ref, hi_ref, phi_ref, sum_ref, co_ref, scale_ref, pc_ref):
    def column(g, carry):
        f = (
            [lo_ref[3 * section + i, g] for i in range(3)]
            + [f_ref[i, g] for i in range(4)]
            + [hi_ref[3 * section + i, g] for i in range(3)]
        )
        b = [None] + [f[i] - f[i - 1] for i in range(1, 10)]
        d = [None, None] + [b[i] - b[i - 1] for i in range(2, 10)]
        centers = [weno_center(b[m + 3], d[m + 2], d[m + 3], d[m + 4], d[m + 5]) for m in range(5)]
        for z in range(4):
            phi = phi_ref[z, g]
            term, by_minus, by_plus = upwind_term(centers[z][0], centers[z + 1][1], side_of(phi))
            root = lax.rsqrt(phi * phi + 1.0)
            square = sum_ref[z, g] + term
            inv = lax.rsqrt(square)
            scale_ref[z, g] = (-0.25 * TAU) * ((phi * root) * inv)
            pc_ref[z, g] = (-TAU) * ((root * root * root) * (square * inv - 1.0))
            parts = (by_minus, by_plus) + centers[z][2] + centers[z + 1][3]
            for n, part in enumerate(parts):
                co_ref[n, z, g] = part
        return carry

    lax.fori_loop(0, 4, column, 0)


def apply_depth(c_ref, co_ref, scale_ref, out_ref, up_ref, dn_ref):
    def column(g, carry):
        dbar = [None] * 8
        bbar = [None] * 9

        def add(into, at, value):
            into[at] = value if into[at] is None else into[at] + value

        for z in range(4):
            c = c_ref[z, g] * scale_ref[z, g]
            co = lambda n: co_ref[n, z, g]
            a, p = c * co(0), c * co(1)
            for k in range(4):
                add(dbar, z + k, a * co(2 + k))
                add(dbar, z + k + 1, p * co(6 + k))
            add(bbar, z + 2, a)
            add(bbar, z + 3, p)
        for j in range(8):
            add(bbar, j + 1, dbar[j])
            add(bbar, j, -dbar[j])
        for z in range(4):
            out_ref[z, g] = bbar[z + 2] - bbar[z + 3]
        for k in range(3):
            up_ref[k, g] = bbar[6 + k]
            dn_ref[k, g] = bbar[k]
        return carry

    lax.fori_loop(0, 4, column, 0, unroll=UNROLL_DEPTH)


def apply_planes(c_ref, co_ref, scale_ref, pc_ref, part_ref, acc_ref, out_ref, acc_out_ref):
    def plane(z, carry):
        whole = c_ref[z]
        c = whole * scale_ref[z]
        total = part_ref[z]
        for axis, shift, gather in ((0, shift_x, gather_x), (1, shift_y, gather_y)):
            co = lambda n: co_ref[PER_AXIS * axis + n, z]
            a = c * co(0)
            g = shift(c * co(1), -1)
            t = [a * co(2 + k) + g * co(6 + k) for k in range(4)]
            b = [-t[0], t[0] - t[1], (a + g) + (t[1] - t[2]), t[2] - t[3], t[3]]
            total = total + gather(
                {0: b[2] - b[3], -1: b[3] - b[4], -2: b[4], 1: b[1] - b[2], 2: b[0] - b[1], 3: t[0]}
            )
        out_ref[z] = total
        local = pc_ref[z] * whole
        acc_out_ref[z] = local if acc_ref is None else acc_ref[z] + local
        return carry

    lax.fori_loop(0, 4, plane, 0, unroll=UNROLL_APPLY)


def joined(own_ref, lo_ref, hi_ref):
    lo0, lo1, lo2 = lo_ref[0], lo_ref[1], lo_ref[2]
    hi0, hi1, hi2 = hi_ref[0], hi_ref[1], hi_ref[2]
    return (
        own_ref[0] + (lo0 - lo1),
        own_ref[1] + (lo1 - lo2 - hi0),
        own_ref[2] + (lo2 + hi0 - hi1),
        own_ref[3] + (hi1 - hi2),
    )


def planes_kernel(*refs):
    phi_ref = refs[3]
    for n in range(3):
        coef_planes(refs[n], phi_ref, refs[4 + 2 * n], refs[5 + 2 * n])


def first_stage(f_ref, lo_ref, hi_ref, phi_ref, sum_ref, cot_ref, c_ref, part_ref, up_ref, dn_ref, scale_ref, pc_ref, co_ref):
    coef_depth(0, f_ref, lo_ref, hi_ref, phi_ref, sum_ref, co_ref, scale_ref, pc_ref)
    c_ref[...] = 0.5 * cot_ref[...]
    apply_depth(c_ref, co_ref, scale_ref, part_ref, up_ref, dn_ref)


def later_stage(halve, *refs):
    earlier, (own_in, lo_ref, hi_ref, co_ref, scale_ref) = refs[:-9], refs[-9:-4]
    c_ref, part_ref, up_ref, dn_ref = refs[-4:]
    for z, back in enumerate(joined(own_in, lo_ref, hi_ref)):
        c = back
        for ref in earlier:
            c = c + ref[z]
        c_ref[z] = 0.5 * c if halve else c
    apply_depth(c_ref, co_ref, scale_ref, part_ref, up_ref, dn_ref)


def window_one(c_ref, co_ref, scale_ref, pc_ref, part_ref, f_ref, lo_ref, hi_ref, phi_ref, sum_ref, own_ref, acc_ref, *coef_refs):
    apply_planes(c_ref, co_ref, scale_ref, pc_ref, part_ref, None, own_ref, acc_ref)
    coef_depth(1, f_ref, lo_ref, hi_ref, phi_ref, sum_ref, *coef_refs)


def window_two(c_ref, co_ref, scale_ref, pc_ref, part_ref, acc_in, f_ref, lo_ref, hi_ref, phi_ref, sum_ref, own_ref, acc_ref, *coef_refs):
    apply_planes(c_ref, co_ref, scale_ref, pc_ref, part_ref, acc_in, own_ref, acc_ref)
    coef_depth(2, f_ref, lo_ref, hi_ref, phi_ref, sum_ref, *coef_refs[:3])
    coef_planes(phi_ref, phi_ref, *coef_refs[3:])


def window_three(c_ref, co_ref, scale_ref, pc_ref, part_ref, acc_in, lo_ref, hi_ref, phi_ref, sum_ref, own_ref, acc_ref, *coef_refs):
    apply_planes(c_ref, co_ref, scale_ref, pc_ref, part_ref, acc_in, own_ref, acc_ref)
    coef_depth(3, phi_ref, lo_ref, hi_ref, phi_ref, sum_ref, *coef_refs)


def window_four(c_ref, co_ref, scale_ref, pc_ref, part_ref, acc_in, own_ref, acc_ref):
    apply_planes(c_ref, co_ref, scale_ref, pc_ref, part_ref, acc_in, own_ref, acc_ref)


def finish(first_ref, middle_ref, own_in, lo_ref, hi_ref, acc_in, out_ref):
    for z, back in enumerate(joined(own_in, lo_ref, hi_ref)):
        whole = (acc_in[z] + back) + (first_ref[z] + middle_ref[z])
        for gy in range(whole.shape[0]):
            for gx in range(whole.shape[1]):
                out_ref[gy * whole.shape[1] + gx, z] = whole[gy, gx]


def slab_path(n_gx, n_gy):
    position = {}
    for gy in range(n_gy):
        for step in range(n_gx):
            gx = step if gy % 2 == 0 else n_gx - 1 - step
            position[gy, gx] = gy * n_gx + step
    return position


def to_slabs(count, depth, position, *refs):
    odd_ref, ins, out_ref, scratch = refs[0], refs[1:-2], refs[-2], refs[-1]
    odd = odd_ref[0] == 1
    for n, ref in enumerate(ins):
        block = ref[...].reshape(BX * BY, LANES)
        scratch[...] = block.T
        for j in range(count):
            at = position[j]
            even_rows = scratch[pl.ds(depth * at, depth), :]
            odd_rows = scratch[pl.ds(depth * (count - 1 - at), depth), :]
            out_ref[j, pl.ds(depth * n, depth), :] = jnp.where(odd, odd_rows, even_rows)


def from_slabs(count, depth, position, odd_ref, in_ref, out_ref, scratch):
    odd = odd_ref[0] == 1
    for j in range(count):
        at = position[j]
        rows = in_ref[j]

        @pl.when(odd)
        def _():
            scratch[pl.ds(depth * (count - 1 - at), depth), :] = rows

        @pl.when(jnp.logical_not(odd))
        def _():
            scratch[pl.ds(depth * at, depth), :] = rows

    out_ref[...] = scratch[...].T.reshape(BX, BY, LANES)


def unpack(n_gy, n_gx, in_ref, f0, f1, f2, f3, f4, up_ref, dn_ref):
    outs = (f0, f1, f2, f3, f4)
    for n, out in enumerate(outs):
        for z in range(4):
            for gy in range(n_gy):
                rows = in_ref[pl.ds(gy * n_gx, n_gx), 4 * n + z, :]
                out[z, gy] = rows
                if n < 4:
                    if z >= 1:
                        up_ref[3 * n + z - 1, gy] = rows
                    if z <= 2:
                        dn_ref[3 * n + z, gy] = rows


def make_shards(sizes, interpret=False):
    n_gx, n_gy, n_gz = sizes["gx"], sizes["gy"], sizes["gz"]
    count = n_gx * n_gy
    depth = LANES // count
    assert depth == 4
    position = slab_path(n_gx, n_gy)
    flat_position = [position[j // n_gx, j % n_gx] for j in range(count)]
    order = []
    for gz in range(n_gz):
        line = sorted(position, key=position.get, reverse=gz % 2 == 1)
        order += [(gx * n_gy + gy) * n_gz + gz for gy, gx in line]
    total = len(order)
    upward = [(order[i], order[(i + 1) % total]) for i in range(total)]
    downward = [(order[(i + 1) % total], order[i]) for i in range(total)]
    everywhere = ("gx", "gy", "gz")
    vmem = pl.BlockSpec(memory_space=pltpu.VMEM)
    smem = pl.BlockSpec(memory_space=pltpu.SMEM)
    slab = (4, n_gy, n_gx, LANES)
    rim = (3, n_gy, n_gx, LANES)

    def like(*shape):
        return jax.ShapeDtypeStruct(shape, F32)

    def near(*shape):
        return like(*shape) if interpret else pltpu.VMEM(shape, F32)

    def call(kernel, out_shape, *args, first=vmem, scratch=(), name=None, far=False):
        many = isinstance(out_shape, list)
        if not interpret:
            space = pltpu.HBM if far else pltpu.VMEM
            args = [x if x.ndim == 1 else pltpu.with_memory_space_constraint(x, space) for x in args]
        return pl.pallas_call(
            kernel,
            out_shape=out_shape,
            in_specs=[first] + [vmem] * (len(args) - 1),
            out_specs=[vmem] * len(out_shape) if many else vmem,
            scratch_shapes=list(scratch),
            compiler_params=pltpu.CompilerParams(vmem_limit_bytes=8 << 20),
            name=name,
            interpret=interpret,
        )(*args)

    def exchange(up, dn):
        return lax.ppermute(up, everywhere, upward), lax.ppermute(dn, everywhere, downward)

    def shards(phi_start, section_first, section_middle, section_second, cot_final):
        odd = (lax.axis_index("gz") % 2).astype(jnp.int32).reshape(1)
        turn = pltpu.VMEM((LANES, LANES), F32)

        packed = call(
            lambda *refs: to_slabs(count, depth, flat_position, *refs),
            near(count, 5 * depth, LANES),
            odd, section_second, section_middle, section_first, phi_start, cot_final,
            first=smem, far=True, scratch=[turn], name="to_slabs",
        )
        packed = lax.all_to_all(packed, ("gy", "gx"), 0, 0)
        *fields, rim_up, rim_dn = call(
            lambda *refs: unpack(n_gy, n_gx, *refs),
            [near(*slab)] * 5 + [near(12, *slab[1:])] * 2,
            packed, name="unpack",
        )
        phi, cot = fields[3], fields[4]
        rim_lo, rim_hi = exchange(rim_up, rim_dn)

        coef_flat = [near(2 * PER_AXIS, *slab), near(*slab)]
        coef_deep = [near(PER_AXIS, *slab), near(*slab), near(*slab)]
        stage_out = [near(*slab), near(*slab), near(*rim), near(*rim)]
        window_out = [near(*slab), near(*slab)]

        flat0, sum0, flat1, sum1, flat2, sum2 = call(
            planes_kernel, coef_flat * 3, *fields[:3], phi, name="coef_planes"
        )
        c1, part, up, dn, scale0, pc0, _ = call(
            first_stage, stage_out + [near(*slab), near(*slab), near(PER_AXIS, *slab)],
            fields[0], rim_lo, rim_hi, phi, sum0, cot, name="stage_one",
        )
        lo, hi = exchange(up, dn)
        own, acc, deep, scale, pc = call(
            window_one, window_out + coef_deep,
            c1, flat0, scale0, pc0, part, fields[1], rim_lo, rim_hi, phi, sum1, name="window_one",
        )
        c2, part, up, dn = call(
            lambda *refs: later_stage(False, *refs), stage_out,
            c1, own, lo, hi, deep, scale, name="stage_two",
        )
        lo, hi = exchange(up, dn)
        own, acc, deep, scale2, pc2, flat3, sum3 = call(
            window_two, window_out + coef_deep + coef_flat,
            c2, flat1, scale, pc, part, acc, fields[2], rim_lo, rim_hi, phi, sum2, name="window_two",
        )
        c3, part, up, dn = call(
            lambda *refs: later_stage(True, *refs), stage_out,
            c1, c2, own, lo, hi, deep, scale2, name="stage_three",
        )
        lo, hi = exchange(up, dn)
        own, acc, deep, scale, pc = call(
            window_three, window_out + coef_deep,
            c3, flat2, scale2, pc2, part, acc, rim_lo, rim_hi, phi, sum3, name="window_three",
        )
        c4, part, up, dn = call(
            lambda *refs: later_stage(False, *refs), stage_out,
            c3, own, lo, hi, deep, scale, name="stage_four",
        )
        lo, hi = exchange(up, dn)
        own, acc = call(
            window_four, window_out, c4, flat3, scale, pc, part, acc, name="window_four",
        )
        slabs = call(finish, near(count, depth, LANES), c4, c3, own, lo, hi, acc, name="finish")
        slabs = lax.all_to_all(slabs, ("gy", "gx"), 0, 0)
        return call(
            lambda *refs: from_slabs(count, depth, flat_position, *refs),
            like(BX, BY, LANES), odd, slabs, first=smem, scratch=[turn], name="from_slabs",
        )

    return shards


def solution(mesh):
    spec = P("gx", "gy", "gz")
    return jax.shard_map(
        make_shards(dict(mesh.shape)),
        mesh=mesh,
        in_specs=(spec,) * 5,
        out_specs=spec,
        check_vma=False,
    )
```

```python
import jax
import jax.numpy as jnp
from jax import lax
from jax.experimental import pallas as pl
from jax.experimental.pallas import tpu as pltpu
from jax.sharding import PartitionSpec as P

TAU = 0.3
WENO_EPS = 1e-06
SMOOTH_EPS = 0.01
UNROLL_COEF = 2
UNROLL_DEPTH = 2
LANES = 128
BX, BY = 8, 16
F32 = jnp.float32


def lane_iota(shape):
    return lax.broadcasted_iota(jnp.int32, shape, len(shape) - 1)


def major_roll(v, k):
    n = v.shape[0]
    return jnp.concatenate([v[(g + k) % n][None] for g in range(n)], axis=0)


def shift_x(v, k):
    lane = lane_iota(v.shape)
    rolled = pltpu.roll(v, (-BY * k) % LANES, 2)
    carried = pltpu.roll(rolled, (-1 if k > 0 else 1) % v.shape[1], 1)
    crossing = lane >= LANES - BY * k if k > 0 else lane < -BY * k
    return jnp.where(crossing, carried, rolled)


def shift_y(v, k):
    inner = lane_iota(v.shape) % BY
    rolled = pltpu.roll(v, (-k) % LANES, 2)
    if k > 0:
        carried = major_roll(pltpu.roll(v, (BY - k) % LANES, 2), 1)
        return jnp.where(inner >= BY - k, carried, rolled)
    carried = major_roll(pltpu.roll(v, (-BY - k) % LANES, 2), -1)
    return jnp.where(inner < -k, carried, rolled)


def shifts_x(v, steps):
    lane = lane_iota(v.shape)
    n = v.shape[1]
    rolled = {k: pltpu.roll(v, (-BY * k) % LANES, 2) for k in steps}
    out = {}
    for k, r in rolled.items():
        carried = pltpu.roll(r, (-1 if k > 0 else 1) % n, 1)
        out[k] = jnp.where(lane >= LANES - BY * k if k > 0 else lane < -BY * k, carried, r)
    return out, rolled


def shifts_y(v, steps, rolled):
    inner = lane_iota(v.shape) % BY
    ahead, behind = major_roll(rolled[-1], 1), major_roll(rolled[1], -1)
    out = {}
    for k in steps:
        mixed = jnp.where(inner < k, ahead, v) if k > 0 else jnp.where(inner >= BY + k, behind, v)
        out[k] = pltpu.roll(mixed, (-k) % LANES, 2)
    return out


def gather_x(parts):
    total = parts[0]
    for k, part in parts.items():
        if k:
            total = total + shift_x(part, k)
    return total


def gather_y(parts):
    total = parts[0]
    inner = lane_iota(total.shape) % BY
    ahead = behind = None
    for k, part in parts.items():
        if k == 0:
            continue
        moved = pltpu.roll(part, (-k) % LANES, 2)
        crossing = inner >= BY - k if k > 0 else inner < -k
        total = total + jnp.where(crossing, 0.0, moved)
        over = jnp.where(crossing, moved, 0.0)
        if k > 0:
            ahead = over if ahead is None else ahead + over
        else:
            behind = over if behind is None else behind + over
    if ahead is not None:
        total = total + major_roll(pltpu.roll(ahead, BY, 2), 1)
    if behind is not None:
        total = total + major_roll(pltpu.roll(behind, LANES - BY, 2), -1)
    return total


def weno_center(b, dm, d0, d1, d2):
    e1, e2, e3 = d0 - dm, d1 - d0, d2 - d1
    p1, p2, p3 = 0.5 * e1 + d0, 0.5 * (d0 + d1), 0.5 * e3 - d1
    f1, f2, f3 = (13.0 / 12.0) * e1, (13.0 / 12.0) * e2, (13.0 / 12.0) * e3
    t1 = WENO_EPS + (f1 * e1 + p1 * p1)
    t2 = WENO_EPS + (f2 * e2 + p2 * p2)
    t3 = WENO_EPS + (f3 * e3 + p3 * p3)
    t12 = t1 * t2
    whole = 1.0 / (t12 * t3)
    i3 = whole * t12
    whole3 = whole * t3
    i1, i2 = whole3 * t2, whole3 * t1
    a1, a2, a3 = i1 * i1, i2 * i2, i3 * i3
    m1, m2, m3 = 0.1 * a1, 0.6 * a2, 0.3 * a3
    r1, r3 = 0.1 * a3, 0.3 * a1
    sum_m, sum_p = m1 + m2 + m3, r1 + m2 + r3
    both = 1.0 / (sum_m * sum_p)
    inv_m, inv_p = both * sum_p, both * sum_m
    w1, w2, w3 = m1 * inv_m, m2 * inv_m, m3 * inv_m
    v1, v2, v3 = r1 * inv_p, m2 * inv_p, r3 * inv_p
    y1, y3 = (e1 - e2) * (1.0 / 3.0), (e2 - e3) * (1.0 / 6.0)
    y1h, y3d = 0.5 * y1, 2.0 * y3
    corr_m = w1 * y1 + w3 * y3
    corr_p = v1 * y3d + v3 * y1h
    base = b + e2 * (1.0 / 3.0)
    minus = base + 0.5 * d0 + corr_m
    plus = base - 0.5 * d1 - corr_p
    j1, j2, j3 = -4.0 * i1, -4.0 * i2, -4.0 * i3
    g1, g3 = f1 + 0.5 * p1, f3 + 0.5 * p3
    half_p2 = 0.5 * p2

    def spread(s1, s2, s3, cy1, cy3, own0, own1):
        ce1 = cy1 + s1 * g1
        ce2 = (cy3 - cy1) + ((1.0 / 3.0) + s2 * f2)
        ce3 = s3 * g3 - cy3
        s2p = s2 * half_p2
        cd0 = s1 * p1 + s2p
        cd1 = s2p - s3 * p3
        if own0:
            cd0 = cd0 + 0.5
        if own1:
            cd1 = cd1 - 0.5
        return (-ce1, cd0 + (ce1 - ce2), cd1 + (ce2 - ce3), ce3)

    jac_m = spread(
        j1 * (w1 * (y1 - corr_m)), -j2 * (w2 * corr_m), j3 * (w3 * (y3 - corr_m)),
        w1 * (1.0 / 3.0), w3 * (1.0 / 6.0), True, False,
    )
    jac_p = spread(
        j1 * (v3 * (corr_p - y1h)), j2 * (v2 * corr_p), j3 * (v1 * (corr_p - y3d)),
        v3 * (-1.0 / 6.0), v1 * (-1.0 / 3.0), False, True,
    )
    return minus, plus, jac_m, jac_p


def upwind_term(minus, plus, side):
    u = jnp.maximum(side * minus, 0.0)
    v = jnp.maximum(-side * plus, 0.0)
    uu, vv = u * u, v * v
    gap = uu - vv
    square = gap * gap + SMOOTH_EPS
    root = lax.rsqrt(square)
    slope = gap * root
    term = 0.5 * (uu + vv + square * root)
    return term, 2.0 * ((1.0 + slope) * (u * side)), -2.0 * ((1.0 - slope) * (v * side))


PER_AXIS = 10


def side_of(phi):
    return jnp.where(phi > 0, 1.0, -1.0).astype(F32)


class Halves:
    def __init__(self, low, high, at):
        self.refs, self.at = (low, high), at

    def __getitem__(self, index):
        index = index if isinstance(index, tuple) else (index,)
        half, plane = divmod(index[self.at], 2)
        return self.refs[half][index[: self.at] + (plane,) + index[self.at + 1 :]]


def coef_planes(f_ref, phi_ref, co_ref, sum_ref, first=0, count=4):
    def plane(z, carry):
        f = f_ref[first + z]
        side = side_of(phi_ref[first + z])
        steps = (-3, -2, -1, 1, 2)
        along_x, rolled = shifts_x(f, steps)
        along_y = shifts_y(f, steps, rolled)
        total = None
        for axis, shift, near in ((0, shift_x, along_x), (1, shift_y, along_y)):
            b = [near[-2] - near[-3], near[-1] - near[-2], f - near[-1], near[1] - f, near[2] - near[1]]
            d = [b[i + 1] - b[i] for i in range(4)]
            minus, plus, jac_m, jac_p = weno_center(b[2], *d)
            term, by_minus, by_plus = upwind_term(minus, shift(plus, 1), side)
            for n, part in enumerate((by_minus, by_plus) + jac_m + jac_p):
                co_ref[PER_AXIS * axis + n, z] = part
            total = term if total is None else total + term
        sum_ref[z] = total
        return carry

    lax.fori_loop(0, count, plane, 0, unroll=UNROLL_COEF)


def coef_depth(section, f_ref, lo_ref, hi_ref, phi_ref, sum_ref, co_ref, scale_ref, pc_ref):
    def column(g, carry):
        f = (
            [lo_ref[3 * section + i, g] for i in range(3)]
            + [f_ref[i, g] for i in range(4)]
            + [hi_ref[3 * section + i, g] for i in range(3)]
        )
        b = [None] + [f[i] - f[i - 1] for i in range(1, 10)]
        d = [None, None] + [b[i] - b[i - 1] for i in range(2, 10)]
        centers = [weno_center(b[m + 3], d[m + 2], d[m + 3], d[m + 4], d[m + 5]) for m in range(5)]
        for z in range(4):
            phi = phi_ref[z, g]
            term, by_minus, by_plus = upwind_term(centers[z][0], centers[z + 1][1], side_of(phi))
            root = lax.rsqrt(phi * phi + 1.0)
            square = sum_ref[z, g] + term
            inv = lax.rsqrt(square)
            scale_ref[z, g] = (-0.25 * TAU) * ((phi * root) * inv)
            pc_ref[z, g] = (-TAU) * ((root * root * root) * (square * inv - 1.0))
            parts = (by_minus, by_plus) + centers[z][2] + centers[z + 1][3]
            for n, part in enumerate(parts):
                co_ref[n, z, g] = part
        return carry

    lax.fori_loop(0, 4, column, 0)


def apply_depth(c_ref, co_ref, scale_ref, out_ref, up_ref, dn_ref):
    def column(g, carry):
        dbar = [None] * 8
        bbar = [None] * 9

        def add(into, at, value):
            into[at] = value if into[at] is None else into[at] + value

        for z in range(4):
            c = c_ref[z, g] * scale_ref[z, g]
            co = lambda n: co_ref[n, z, g]
            a, p = c * co(0), c * co(1)
            for k in range(4):
                add(dbar, z + k, a * co(2 + k))
                add(dbar, z + k + 1, p * co(6 + k))
            add(bbar, z + 2, a)
            add(bbar, z + 3, p)
        for j in range(8):
            add(bbar, j + 1, dbar[j])
            add(bbar, j, -dbar[j])
        for z in range(4):
            out_ref[z, g] = bbar[z + 2] - bbar[z + 3]
        for k in range(3):
            up_ref[k, g] = bbar[6 + k]
            dn_ref[k, g] = bbar[k]
        return carry

    lax.fori_loop(0, 4, column, 0, unroll=UNROLL_DEPTH)


def apply_planes(c_ref, co_ref, scale_ref, pc_ref, part_ref, acc_ref, out_ref, acc_out_ref):
    for z in range(4):
        whole = c_ref[z]
        c = whole * scale_ref[z]
        total = part_ref[z]
        for axis, shift, gather in ((0, shift_x, gather_x), (1, shift_y, gather_y)):
            co = lambda n: co_ref[PER_AXIS * axis + n, z]
            a = c * co(0)
            g = shift(c * co(1), -1)
            t = [a * co(2 + k) + g * co(6 + k) for k in range(4)]
            b = [-t[0], t[0] - t[1], (a + g) + (t[1] - t[2]), t[2] - t[3], t[3]]
            total = total + gather(
                {0: b[2] - b[3], -1: b[3] - b[4], -2: b[4], 1: b[1] - b[2], 2: b[0] - b[1], 3: t[0]}
            )
        out_ref[z] = total
        local = pc_ref[z] * whole
        acc_out_ref[z] = local if acc_ref is None else acc_ref[z] + local


def joined(own_ref, lo_ref, hi_ref):
    lo0, lo1, lo2 = lo_ref[0], lo_ref[1], lo_ref[2]
    hi0, hi1, hi2 = hi_ref[0], hi_ref[1], hi_ref[2]
    return (
        own_ref[0] + (lo0 - lo1),
        own_ref[1] + (lo1 - lo2 - hi0),
        own_ref[2] + (lo2 + hi0 - hi1),
        own_ref[3] + (hi1 - hi2),
    )


def planes_kernel(*refs):
    phi_ref = refs[3]
    for n in range(3):
        coef_planes(refs[n], phi_ref, refs[4 + 2 * n], refs[5 + 2 * n])


def first_stage(f_ref, lo_ref, hi_ref, phi_ref, sum_ref, cot_ref, c_ref, part_ref, up_ref, dn_ref, scale_ref, pc_ref, co_ref):
    coef_depth(0, f_ref, lo_ref, hi_ref, phi_ref, sum_ref, co_ref, scale_ref, pc_ref)
    c_ref[...] = 0.5 * cot_ref[...]
    apply_depth(c_ref, co_ref, scale_ref, part_ref, up_ref, dn_ref)


def later_stage(halve, *refs):
    earlier, (own_in, lo_ref, hi_ref, co_ref, scale_ref) = refs[:-9], refs[-9:-4]
    c_ref, part_ref, up_ref, dn_ref = refs[-4:]
    for z, back in enumerate(joined(own_in, lo_ref, hi_ref)):
        c = back
        for ref in earlier:
            c = c + ref[z]
        c_ref[z] = 0.5 * c if halve else c
    apply_depth(c_ref, co_ref, scale_ref, part_ref, up_ref, dn_ref)


def window_one(c_ref, co_ref, scale_ref, pc_ref, part_ref, f_ref, lo_ref, hi_ref, phi_ref, sum_ref, own_ref, acc_ref, *coef_refs):
    apply_planes(c_ref, co_ref, scale_ref, pc_ref, part_ref, None, own_ref, acc_ref)
    coef_depth(1, f_ref, lo_ref, hi_ref, phi_ref, sum_ref, *coef_refs[:3])
    coef_planes(phi_ref, phi_ref, *coef_refs[3:], first=0, count=2)


def window_two(c_ref, co_ref, scale_ref, pc_ref, part_ref, acc_in, f_ref, lo_ref, hi_ref, phi_ref, sum_ref, own_ref, acc_ref, *coef_refs):
    apply_planes(c_ref, co_ref, scale_ref, pc_ref, part_ref, acc_in, own_ref, acc_ref)
    coef_depth(2, f_ref, lo_ref, hi_ref, phi_ref, sum_ref, *coef_refs[:3])
    coef_planes(phi_ref, phi_ref, *coef_refs[3:], first=2, count=2)


def window_three(c_ref, co_ref, scale_ref, pc_ref, part_ref, acc_in, lo_ref, hi_ref, phi_ref, sum_low, sum_high, own_ref, acc_ref, *coef_refs):
    apply_planes(c_ref, co_ref, scale_ref, pc_ref, part_ref, acc_in, own_ref, acc_ref)
    coef_depth(3, phi_ref, lo_ref, hi_ref, phi_ref, Halves(sum_low, sum_high, 0), *coef_refs)


def window_four(c_ref, co_low, co_high, scale_ref, pc_ref, part_ref, acc_in, own_ref, acc_ref):
    apply_planes(c_ref, Halves(co_low, co_high, 1), scale_ref, pc_ref, part_ref, acc_in, own_ref, acc_ref)


def finish(first_ref, middle_ref, own_in, lo_ref, hi_ref, acc_in, out_ref):
    for z, back in enumerate(joined(own_in, lo_ref, hi_ref)):
        whole = (acc_in[z] + back) + (first_ref[z] + middle_ref[z])
        for gy in range(whole.shape[0]):
            for gx in range(whole.shape[1]):
                out_ref[gy * whole.shape[1] + gx, z] = whole[gy, gx]


def slab_path(n_gx, n_gy):
    position = {}
    for gy in range(n_gy):
        for step in range(n_gx):
            gx = step if gy % 2 == 0 else n_gx - 1 - step
            position[gy, gx] = gy * n_gx + step
    return position


def to_slabs(count, depth, position, *refs):
    odd_ref, ins, out_ref, scratch = refs[0], refs[1:-2], refs[-2], refs[-1]
    odd = odd_ref[0] == 1
    for n, ref in enumerate(ins):
        block = ref[...].reshape(BX * BY, LANES)
        scratch[...] = block.T
        for j in range(count):
            at = position[j]
            even_rows = scratch[pl.ds(depth * at, depth), :]
            odd_rows = scratch[pl.ds(depth * (count - 1 - at), depth), :]
            out_ref[j, pl.ds(depth * n, depth), :] = jnp.where(odd, odd_rows, even_rows)


def from_slabs(count, depth, position, odd_ref, in_ref, out_ref, scratch):
    odd = odd_ref[0] == 1
    for j in range(count):
        at = position[j]
        rows = in_ref[j]

        @pl.when(odd)
        def _():
            scratch[pl.ds(depth * (count - 1 - at), depth), :] = rows

        @pl.when(jnp.logical_not(odd))
        def _():
            scratch[pl.ds(depth * at, depth), :] = rows

    out_ref[...] = scratch[...].T.reshape(BX, BY, LANES)


def unpack(n_gy, n_gx, in_ref, f0, f1, f2, f3, f4, up_ref, dn_ref):
    outs = (f0, f1, f2, f3, f4)
    for n, out in enumerate(outs):
        for z in range(4):
            for gy in range(n_gy):
                rows = in_ref[pl.ds(gy * n_gx, n_gx), 4 * n + z, :]
                out[z, gy] = rows
                if n < 4:
                    if z >= 1:
                        up_ref[3 * n + z - 1, gy] = rows
                    if z <= 2:
                        dn_ref[3 * n + z, gy] = rows


def make_shards(sizes, interpret=False):
    n_gx, n_gy, n_gz = sizes["gx"], sizes["gy"], sizes["gz"]
    count = n_gx * n_gy
    depth = LANES // count
    assert depth == 4
    position = slab_path(n_gx, n_gy)
    flat_position = [position[j // n_gx, j % n_gx] for j in range(count)]
    order = []
    for gz in range(n_gz):
        line = sorted(position, key=position.get, reverse=gz % 2 == 1)
        order += [(gx * n_gy + gy) * n_gz + gz for gy, gx in line]
    total = len(order)
    upward = [(order[i], order[(i + 1) % total]) for i in range(total)]
    downward = [(order[(i + 1) % total], order[i]) for i in range(total)]
    everywhere = ("gx", "gy", "gz")
    vmem = pl.BlockSpec(memory_space=pltpu.VMEM)
    smem = pl.BlockSpec(memory_space=pltpu.SMEM)
    slab = (4, n_gy, n_gx, LANES)
    rim = (3, n_gy, n_gx, LANES)

    def like(*shape):
        return jax.ShapeDtypeStruct(shape, F32)

    def near(*shape):
        return like(*shape) if interpret else pltpu.VMEM(shape, F32)

    def call(kernel, out_shape, *args, first=vmem, scratch=(), name=None, far=False):
        many = isinstance(out_shape, list)
        if not interpret:
            space = pltpu.HBM if far else pltpu.VMEM
            args = [x if x.ndim == 1 else pltpu.with_memory_space_constraint(x, space) for x in args]
        return pl.pallas_call(
            kernel,
            out_shape=out_shape,
            in_specs=[first] + [vmem] * (len(args) - 1),
            out_specs=[vmem] * len(out_shape) if many else vmem,
            scratch_shapes=list(scratch),
            compiler_params=pltpu.CompilerParams(vmem_limit_bytes=8 << 20),
            name=name,
            interpret=interpret,
        )(*args)

    def exchange(up, dn):
        return lax.ppermute(up, everywhere, upward), lax.ppermute(dn, everywhere, downward)

    def shards(phi_start, section_first, section_middle, section_second, cot_final):
        odd = (lax.axis_index("gz") % 2).astype(jnp.int32).reshape(1)
        turn = pltpu.VMEM((LANES, LANES), F32)

        packed = call(
            lambda *refs: to_slabs(count, depth, flat_position, *refs),
            near(count, 5 * depth, LANES),
            odd, section_second, section_middle, section_first, phi_start, cot_final,
            first=smem, far=True, scratch=[turn], name="to_slabs",
        )
        packed = lax.all_to_all(packed, ("gy", "gx"), 0, 0)
        *fields, rim_up, rim_dn = call(
            lambda *refs: unpack(n_gy, n_gx, *refs),
            [near(*slab)] * 5 + [near(12, *slab[1:])] * 2,
            packed, name="unpack",
        )
        phi, cot = fields[3], fields[4]
        rim_lo, rim_hi = exchange(rim_up, rim_dn)

        coef_flat = [near(2 * PER_AXIS, *slab), near(*slab)]
        coef_half = [near(2 * PER_AXIS, 2, *slab[1:]), near(2, *slab[1:])]
        coef_deep = [near(PER_AXIS, *slab), near(*slab), near(*slab)]
        stage_out = [near(*slab), near(*slab), near(*rim), near(*rim)]
        window_out = [near(*slab), near(*slab)]

        flat0, sum0, flat1, sum1, flat2, sum2 = call(
            planes_kernel, coef_flat * 3, *fields[:3], phi, name="coef_planes"
        )
        c1, part, up, dn, scale0, pc0 = call(
            first_stage, stage_out + [near(*slab), near(*slab)],
            fields[0], rim_lo, rim_hi, phi, sum0, cot,
            scratch=[pltpu.VMEM((PER_AXIS, *slab), F32)], name="stage_one",
        )
        lo, hi = exchange(up, dn)
        own, acc, deep, scale, pc, flat3a, sum3a = call(
            window_one, window_out + coef_deep + coef_half,
            c1, flat0, scale0, pc0, part, fields[1], rim_lo, rim_hi, phi, sum1, name="window_one",
        )
        c2, part, up, dn = call(
            lambda *refs: later_stage(False, *refs), stage_out,
            c1, own, lo, hi, deep, scale, name="stage_two",
        )
        lo, hi = exchange(up, dn)
        own, acc, deep, scale2, pc2, flat3b, sum3b = call(
            window_two, window_out + coef_deep + coef_half,
            c2, flat1, scale, pc, part, acc, fields[2], rim_lo, rim_hi, phi, sum2, name="window_two",
        )
        c3, part, up, dn = call(
            lambda *refs: later_stage(True, *refs), stage_out,
            c1, c2, own, lo, hi, deep, scale2, name="stage_three",
        )
        lo, hi = exchange(up, dn)
        own, acc, deep, scale, pc = call(
            window_three, window_out + coef_deep,
            c3, flat2, scale2, pc2, part, acc, rim_lo, rim_hi, phi, sum3a, sum3b, name="window_three",
        )
        c4, part, up, dn = call(
            lambda *refs: later_stage(False, *refs), stage_out,
            c3, own, lo, hi, deep, scale, name="stage_four",
        )
        lo, hi = exchange(up, dn)
        own, acc = call(
            window_four, window_out, c4, flat3a, flat3b, scale, pc, part, acc, name="window_four",
        )
        slabs = call(finish, near(count, depth, LANES), c4, c3, own, lo, hi, acc, name="finish")
        slabs = lax.all_to_all(slabs, ("gy", "gx"), 0, 0)
        return call(
            lambda *refs: from_slabs(count, depth, flat_position, *refs),
            like(BX, BY, LANES), odd, slabs, first=smem, scratch=[turn], name="from_slabs",
        )

    return shards


def solution(mesh):
    spec = P("gx", "gy", "gz")
    return jax.shard_map(
        make_shards(dict(mesh.shape)),
        mesh=mesh,
        in_specs=(spec,) * 5,
        out_specs=spec,
        check_vma=False,
    )
```

```python
import jax
import jax.numpy as jnp
from jax import lax
from jax.experimental import pallas as pl
from jax.experimental.pallas import tpu as pltpu
from jax.sharding import PartitionSpec as P

TAU = 0.3
WENO_EPS = 1e-06
SMOOTH_EPS = 0.01
UNROLL_COEF = 2
EVEN_TURNS, ODD_TURNS = (1, 1, -1, -1), (-1, -1, 1, 1)
UNROLL_DEPTH = 2
LANES = 128
BX, BY = 8, 16
F32 = jnp.float32


def lane_iota(shape):
    return lax.broadcasted_iota(jnp.int32, shape, len(shape) - 1)


def major_roll(v, k):
    n = v.shape[0]
    return jnp.concatenate([v[(g + k) % n][None] for g in range(n)], axis=0)


def shift_x(v, k):
    lane = lane_iota(v.shape)
    rolled = pltpu.roll(v, (-BY * k) % LANES, 2)
    carried = pltpu.roll(rolled, (-1 if k > 0 else 1) % v.shape[1], 1)
    crossing = lane >= LANES - BY * k if k > 0 else lane < -BY * k
    return jnp.where(crossing, carried, rolled)


def shift_y(v, k):
    inner = lane_iota(v.shape) % BY
    rolled = pltpu.roll(v, (-k) % LANES, 2)
    if k > 0:
        carried = major_roll(pltpu.roll(v, (BY - k) % LANES, 2), 1)
        return jnp.where(inner >= BY - k, carried, rolled)
    carried = major_roll(pltpu.roll(v, (-BY - k) % LANES, 2), -1)
    return jnp.where(inner < -k, carried, rolled)


def shifts_x(v, steps):
    lane = lane_iota(v.shape)
    n = v.shape[1]
    rolled = {k: pltpu.roll(v, (-BY * k) % LANES, 2) for k in steps}
    out = {}
    for k, r in rolled.items():
        carried = pltpu.roll(r, (-1 if k > 0 else 1) % n, 1)
        out[k] = jnp.where(lane >= LANES - BY * k if k > 0 else lane < -BY * k, carried, r)
    return out, rolled


def shifts_y(v, steps, rolled):
    inner = lane_iota(v.shape) % BY
    ahead, behind = major_roll(rolled[-1], 1), major_roll(rolled[1], -1)
    out = {}
    for k in steps:
        mixed = jnp.where(inner < k, ahead, v) if k > 0 else jnp.where(inner >= BY + k, behind, v)
        out[k] = pltpu.roll(mixed, (-k) % LANES, 2)
    return out


def gather_x(parts):
    total = parts[0]
    for k, part in parts.items():
        if k:
            total = total + shift_x(part, k)
    return total


def gather_y(parts):
    total = parts[0]
    inner = lane_iota(total.shape) % BY
    ahead = behind = None
    for k, part in parts.items():
        if k == 0:
            continue
        moved = pltpu.roll(part, (-k) % LANES, 2)
        crossing = inner >= BY - k if k > 0 else inner < -k
        total = total + jnp.where(crossing, 0.0, moved)
        over = jnp.where(crossing, moved, 0.0)
        if k > 0:
            ahead = over if ahead is None else ahead + over
        else:
            behind = over if behind is None else behind + over
    if ahead is not None:
        total = total + major_roll(pltpu.roll(ahead, BY, 2), 1)
    if behind is not None:
        total = total + major_roll(pltpu.roll(behind, LANES - BY, 2), -1)
    return total


def weno_center(b, dm, d0, d1, d2):
    e1, e2, e3 = d0 - dm, d1 - d0, d2 - d1
    p1, p2, p3 = 0.5 * e1 + d0, 0.5 * (d0 + d1), 0.5 * e3 - d1
    f1, f2, f3 = (13.0 / 12.0) * e1, (13.0 / 12.0) * e2, (13.0 / 12.0) * e3
    t1 = WENO_EPS + (f1 * e1 + p1 * p1)
    t2 = WENO_EPS + (f2 * e2 + p2 * p2)
    t3 = WENO_EPS + (f3 * e3 + p3 * p3)
    t12 = t1 * t2
    whole = 1.0 / (t12 * t3)
    i3 = whole * t12
    whole3 = whole * t3
    i1, i2 = whole3 * t2, whole3 * t1
    a1, a2, a3 = i1 * i1, i2 * i2, i3 * i3
    m1, m2, m3 = 0.1 * a1, 0.6 * a2, 0.3 * a3
    r1, r3 = 0.1 * a3, 0.3 * a1
    sum_m, sum_p = m1 + m2 + m3, r1 + m2 + r3
    both = 1.0 / (sum_m * sum_p)
    inv_m, inv_p = both * sum_p, both * sum_m
    w1, w2, w3 = m1 * inv_m, m2 * inv_m, m3 * inv_m
    v1, v2, v3 = r1 * inv_p, m2 * inv_p, r3 * inv_p
    y1, y3 = (e1 - e2) * (1.0 / 3.0), (e2 - e3) * (1.0 / 6.0)
    y1h, y3d = 0.5 * y1, 2.0 * y3
    corr_m = w1 * y1 + w3 * y3
    corr_p = v1 * y3d + v3 * y1h
    base = b + e2 * (1.0 / 3.0)
    minus = base + 0.5 * d0 + corr_m
    plus = base - 0.5 * d1 - corr_p
    j1, j2, j3 = -4.0 * i1, -4.0 * i2, -4.0 * i3
    g1, g3 = f1 + 0.5 * p1, f3 + 0.5 * p3
    half_p2 = 0.5 * p2

    def spread(s1, s2, s3, cy1, cy3, own0, own1):
        ce1 = cy1 + s1 * g1
        ce2 = (cy3 - cy1) + ((1.0 / 3.0) + s2 * f2)
        ce3 = s3 * g3 - cy3
        s2p = s2 * half_p2
        cd0 = s1 * p1 + s2p
        cd1 = s2p - s3 * p3
        if own0:
            cd0 = cd0 + 0.5
        if own1:
            cd1 = cd1 - 0.5
        return (-ce1, cd0 + (ce1 - ce2), cd1 + (ce2 - ce3), ce3)

    jac_m = spread(
        j1 * (w1 * (y1 - corr_m)), -j2 * (w2 * corr_m), j3 * (w3 * (y3 - corr_m)),
        w1 * (1.0 / 3.0), w3 * (1.0 / 6.0), True, False,
    )
    jac_p = spread(
        j1 * (v3 * (corr_p - y1h)), j2 * (v2 * corr_p), j3 * (v1 * (corr_p - y3d)),
        v3 * (-1.0 / 6.0), v1 * (-1.0 / 3.0), False, True,
    )
    return minus, plus, jac_m, jac_p


def upwind_term(minus, plus, side):
    u = jnp.maximum(side * minus, 0.0)
    v = jnp.maximum(-side * plus, 0.0)
    uu, vv = u * u, v * v
    gap = uu - vv
    square = gap * gap + SMOOTH_EPS
    root = lax.rsqrt(square)
    slope = gap * root
    term = 0.5 * (uu + vv + square * root)
    return term, 2.0 * ((1.0 + slope) * (u * side)), -2.0 * ((1.0 - slope) * (v * side))


PER_AXIS = 10


def side_of(phi):
    return jnp.where(phi > 0, 1.0, -1.0).astype(F32)


class Halves:
    def __init__(self, low, high, at):
        self.refs, self.at = (low, high), at

    def __getitem__(self, index):
        index = index if isinstance(index, tuple) else (index,)
        half, plane = divmod(index[self.at], 2)
        return self.refs[half][index[: self.at] + (plane,) + index[self.at + 1 :]]


def coef_planes(f_ref, phi_ref, co_ref, sum_ref, first=0, count=4):
    def plane(z, carry):
        f = f_ref[first + z]
        side = side_of(phi_ref[first + z])
        steps = (-3, -2, -1, 1, 2)
        along_x, rolled = shifts_x(f, steps)
        along_y = shifts_y(f, steps, rolled)
        total = None
        for axis, shift, near in ((0, shift_x, along_x), (1, shift_y, along_y)):
            b = [near[-2] - near[-3], near[-1] - near[-2], f - near[-1], near[1] - f, near[2] - near[1]]
            d = [b[i + 1] - b[i] for i in range(4)]
            minus, plus, jac_m, jac_p = weno_center(b[2], *d)
            term, by_minus, by_plus = upwind_term(minus, shift(plus, 1), side)
            for n, part in enumerate((by_minus, by_plus) + jac_m + jac_p):
                co_ref[PER_AXIS * axis + n, z] = part
            total = term if total is None else total + term
        sum_ref[z] = total
        return carry

    lax.fori_loop(0, count, plane, 0, unroll=UNROLL_COEF)


def coef_depth(section, f_ref, lo_ref, hi_ref, phi_ref, sum_ref, co_ref, scale_ref, pc_ref):
    def column(g, carry):
        f = (
            [lo_ref[3 * section + i, g] for i in range(3)]
            + [f_ref[i, g] for i in range(4)]
            + [hi_ref[3 * section + i, g] for i in range(3)]
        )
        b = [None] + [f[i] - f[i - 1] for i in range(1, 10)]
        d = [None, None] + [b[i] - b[i - 1] for i in range(2, 10)]
        centers = [weno_center(b[m + 3], d[m + 2], d[m + 3], d[m + 4], d[m + 5]) for m in range(5)]
        for z in range(4):
            phi = phi_ref[z, g]
            term, by_minus, by_plus = upwind_term(centers[z][0], centers[z + 1][1], side_of(phi))
            root = lax.rsqrt(phi * phi + 1.0)
            square = sum_ref[z, g] + term
            inv = lax.rsqrt(square)
            scale_ref[z, g] = (-0.25 * TAU) * ((phi * root) * inv)
            pc_ref[z, g] = (-TAU) * ((root * root * root) * (square * inv - 1.0))
            parts = (by_minus, by_plus) + centers[z][2] + centers[z + 1][3]
            for n, part in enumerate(parts):
                co_ref[n, z, g] = part
        return carry

    lax.fori_loop(0, 4, column, 0, unroll=UNROLL_COEF)


def apply_depth(c_ref, co_ref, scale_ref, out_ref, up_ref, dn_ref):
    def column(g, carry):
        dbar = [None] * 8
        bbar = [None] * 9

        def add(into, at, value):
            into[at] = value if into[at] is None else into[at] + value

        for z in range(4):
            c = c_ref[z, g] * scale_ref[z, g]
            co = lambda n: co_ref[n, z, g]
            a, p = c * co(0), c * co(1)
            for k in range(4):
                add(dbar, z + k, a * co(2 + k))
                add(dbar, z + k + 1, p * co(6 + k))
            add(bbar, z + 2, a)
            add(bbar, z + 3, p)
        for j in range(8):
            add(bbar, j + 1, dbar[j])
            add(bbar, j, -dbar[j])
        for z in range(4):
            out_ref[z, g] = bbar[z + 2] - bbar[z + 3]
        for k in range(3):
            up_ref[k, g] = bbar[6 + k]
            dn_ref[k, g] = bbar[k]
        return carry

    lax.fori_loop(0, 4, column, 0, unroll=UNROLL_DEPTH)


def apply_planes(c_ref, co_ref, scale_ref, pc_ref, part_ref, acc_ref, out_ref, acc_out_ref):
    for z in range(4):
        whole = c_ref[z]
        c = whole * scale_ref[z]
        total = part_ref[z]
        for axis, shift, gather in ((0, shift_x, gather_x), (1, shift_y, gather_y)):
            co = lambda n: co_ref[PER_AXIS * axis + n, z]
            a = c * co(0)
            g = shift(c * co(1), -1)
            t = [a * co(2 + k) + g * co(6 + k) for k in range(4)]
            b = [-t[0], t[0] - t[1], (a + g) + (t[1] - t[2]), t[2] - t[3], t[3]]
            total = total + gather(
                {0: b[2] - b[3], -1: b[3] - b[4], -2: b[4], 1: b[1] - b[2], 2: b[0] - b[1], 3: t[0]}
            )
        out_ref[z] = total
        local = pc_ref[z] * whole
        acc_out_ref[z] = local if acc_ref is None else acc_ref[z] + local


def joined(own_ref, lo_ref, hi_ref):
    lo0, lo1, lo2 = lo_ref[0], lo_ref[1], lo_ref[2]
    hi0, hi1, hi2 = hi_ref[0], hi_ref[1], hi_ref[2]
    return (
        own_ref[0] + (lo0 - lo1),
        own_ref[1] + (lo1 - lo2 - hi0),
        own_ref[2] + (lo2 + hi0 - hi1),
        own_ref[3] + (hi1 - hi2),
    )


def planes_kernel(*refs):
    phi_ref = refs[3]
    for n in range(3):
        coef_planes(refs[n], phi_ref, refs[4 + 2 * n], refs[5 + 2 * n])


def first_stage(f_ref, lo_ref, hi_ref, phi_ref, sum_ref, cot_ref, c_ref, part_ref, up_ref, dn_ref, scale_ref, pc_ref, co_ref):
    coef_depth(0, f_ref, lo_ref, hi_ref, phi_ref, sum_ref, co_ref, scale_ref, pc_ref)
    c_ref[...] = 0.5 * cot_ref[...]
    apply_depth(c_ref, co_ref, scale_ref, part_ref, up_ref, dn_ref)


def later_stage(halve, *refs):
    earlier, (own_in, lo_ref, hi_ref, co_ref, scale_ref) = refs[:-9], refs[-9:-4]
    c_ref, part_ref, up_ref, dn_ref = refs[-4:]
    for z, back in enumerate(joined(own_in, lo_ref, hi_ref)):
        c = back
        for ref in earlier:
            c = c + ref[z]
        c_ref[z] = 0.5 * c if halve else c
    apply_depth(c_ref, co_ref, scale_ref, part_ref, up_ref, dn_ref)


def window_one(c_ref, co_ref, scale_ref, pc_ref, part_ref, f_ref, lo_ref, hi_ref, phi_ref, sum_ref, own_ref, acc_ref, *coef_refs):
    apply_planes(c_ref, co_ref, scale_ref, pc_ref, part_ref, None, own_ref, acc_ref)
    coef_depth(1, f_ref, lo_ref, hi_ref, phi_ref, sum_ref, *coef_refs[:3])
    coef_planes(phi_ref, phi_ref, *coef_refs[3:], first=0, count=2)


def window_two(c_ref, co_ref, scale_ref, pc_ref, part_ref, acc_in, f_ref, lo_ref, hi_ref, phi_ref, sum_ref, own_ref, acc_ref, *coef_refs):
    apply_planes(c_ref, co_ref, scale_ref, pc_ref, part_ref, acc_in, own_ref, acc_ref)
    coef_depth(2, f_ref, lo_ref, hi_ref, phi_ref, sum_ref, *coef_refs[:3])
    coef_planes(phi_ref, phi_ref, *coef_refs[3:], first=2, count=2)


def window_three(c_ref, co_ref, scale_ref, pc_ref, part_ref, acc_in, lo_ref, hi_ref, phi_ref, sum_low, sum_high, own_ref, acc_ref, *coef_refs):
    apply_planes(c_ref, co_ref, scale_ref, pc_ref, part_ref, acc_in, own_ref, acc_ref)
    coef_depth(3, phi_ref, lo_ref, hi_ref, phi_ref, Halves(sum_low, sum_high, 0), *coef_refs)


def window_four(c_ref, co_low, co_high, scale_ref, pc_ref, part_ref, acc_in, own_ref, acc_ref):
    apply_planes(c_ref, Halves(co_low, co_high, 1), scale_ref, pc_ref, part_ref, acc_in, own_ref, acc_ref)


def finish(first_ref, middle_ref, own_in, lo_ref, hi_ref, acc_in, out_ref):
    for z, back in enumerate(joined(own_in, lo_ref, hi_ref)):
        whole = (acc_in[z] + back) + (first_ref[z] + middle_ref[z])
        for gy in range(whole.shape[0]):
            for gx in range(whole.shape[1]):
                out_ref[gy * whole.shape[1] + gx, z] = whole[gy, gx]


def slab_line(n_gx, n_gy, turns):
    gx, line = 0, []
    for gy in range(n_gy):
        turn = turns[gy % len(turns)]
        line += [(gy, (gx + turn * step) % n_gx) for step in range(n_gx)]
        gx = (gx - turn) % n_gx
    return line


def to_slabs(count, depth, even_at, odd_at, *refs):
    odd_ref, ins, out_ref, scratch = refs[0], refs[1:-2], refs[-2], refs[-1]
    odd = odd_ref[0] == 1
    for n, ref in enumerate(ins):
        block = ref[...].reshape(BX * BY, LANES)
        scratch[...] = block.T
        for j in range(count):
            even_rows = scratch[pl.ds(depth * even_at[j], depth), :]
            odd_rows = scratch[pl.ds(depth * odd_at[j], depth), :]
            out_ref[j, pl.ds(depth * n, depth), :] = jnp.where(odd, odd_rows, even_rows)


def from_slabs(count, depth, even_at, odd_at, odd_ref, in_ref, out_ref, scratch):
    odd = odd_ref[0] == 1
    for at in range(count):
        even_rows, odd_rows = in_ref[even_at.index(at)], in_ref[odd_at.index(at)]
        scratch[pl.ds(depth * at, depth), :] = jnp.where(odd, odd_rows, even_rows)
    out_ref[...] = scratch[...].T.reshape(BX, BY, LANES)


def unpack(n_gy, n_gx, in_ref, f0, f1, f2, f3, f4, up_ref, dn_ref):
    outs = (f0, f1, f2, f3, f4)
    for n, out in enumerate(outs):
        for z in range(4):
            for gy in range(n_gy):
                rows = in_ref[pl.ds(gy * n_gx, n_gx), 4 * n + z, :]
                out[z, gy] = rows
                if n < 4:
                    if z >= 1:
                        up_ref[3 * n + z - 1, gy] = rows
                    if z <= 2:
                        dn_ref[3 * n + z, gy] = rows


def make_shards(sizes, interpret=False):
    n_gx, n_gy, n_gz = sizes["gx"], sizes["gy"], sizes["gz"]
    count = n_gx * n_gy
    depth = LANES // count
    assert depth == 4
    even_line = slab_line(n_gx, n_gy, EVEN_TURNS)
    odd_line = slab_line(n_gx, n_gy, ODD_TURNS)[::-1]
    even_at = [even_line.index((j // n_gx, j % n_gx)) for j in range(count)]
    odd_at = [odd_line.index((j // n_gx, j % n_gx)) for j in range(count)]
    order = []
    for gz in range(n_gz):
        order += [(gx * n_gy + gy) * n_gz + gz for gy, gx in (odd_line if gz % 2 else even_line)]
    total = len(order)
    upward = [(order[i], order[(i + 1) % total]) for i in range(total)]
    downward = [(order[(i + 1) % total], order[i]) for i in range(total)]
    everywhere = ("gx", "gy", "gz")
    vmem = pl.BlockSpec(memory_space=pltpu.VMEM)
    smem = pl.BlockSpec(memory_space=pltpu.SMEM)
    slab = (4, n_gy, n_gx, LANES)
    rim = (3, n_gy, n_gx, LANES)

    def like(*shape):
        return jax.ShapeDtypeStruct(shape, F32)

    def near(*shape):
        return like(*shape) if interpret else pltpu.VMEM(shape, F32)

    def call(kernel, out_shape, *args, first=vmem, scratch=(), name=None, far=False):
        many = isinstance(out_shape, list)
        if not interpret:
            space = pltpu.HBM if far else pltpu.VMEM
            args = [x if x.ndim == 1 else pltpu.with_memory_space_constraint(x, space) for x in args]
        return pl.pallas_call(
            kernel,
            out_shape=out_shape,
            in_specs=[first] + [vmem] * (len(args) - 1),
            out_specs=[vmem] * len(out_shape) if many else vmem,
            scratch_shapes=list(scratch),
            compiler_params=pltpu.CompilerParams(vmem_limit_bytes=8 << 20),
            name=name,
            interpret=interpret,
        )(*args)

    def exchange(up, dn):
        return lax.ppermute(up, everywhere, upward), lax.ppermute(dn, everywhere, downward)

    def shards(phi_start, section_first, section_middle, section_second, cot_final):
        odd = (lax.axis_index("gz") % 2).astype(jnp.int32).reshape(1)
        turn = pltpu.VMEM((LANES, LANES), F32)

        packed = call(
            lambda *refs: to_slabs(count, depth, even_at, odd_at, *refs),
            near(count, 5 * depth, LANES),
            odd, section_second, section_middle, section_first, phi_start, cot_final,
            first=smem, far=True, scratch=[turn], name="to_slabs",
        )
        packed = lax.all_to_all(packed, ("gy", "gx"), 0, 0)
        *fields, rim_up, rim_dn = call(
            lambda *refs: unpack(n_gy, n_gx, *refs),
            [near(*slab)] * 5 + [near(12, *slab[1:])] * 2,
            packed, name="unpack",
        )
        phi, cot = fields[3], fields[4]
        rim_lo, rim_hi = exchange(rim_up, rim_dn)

        coef_flat = [near(2 * PER_AXIS, *slab), near(*slab)]
        coef_half = [near(2 * PER_AXIS, 2, *slab[1:]), near(2, *slab[1:])]
        coef_deep = [near(PER_AXIS, *slab), near(*slab), near(*slab)]
        stage_out = [near(*slab), near(*slab), near(*rim), near(*rim)]
        window_out = [near(*slab), near(*slab)]

        flat0, sum0, flat1, sum1, flat2, sum2 = call(
            planes_kernel, coef_flat * 3, *fields[:3], phi, name="coef_planes"
        )
        c1, part, up, dn, scale0, pc0 = call(
            first_stage, stage_out + [near(*slab), near(*slab)],
            fields[0], rim_lo, rim_hi, phi, sum0, cot,
            scratch=[pltpu.VMEM((PER_AXIS, *slab), F32)], name="stage_one",
        )
        lo, hi = exchange(up, dn)
        own, acc, deep, scale, pc, flat3a, sum3a = call(
            window_one, window_out + coef_deep + coef_half,
            c1, flat0, scale0, pc0, part, fields[1], rim_lo, rim_hi, phi, sum1, name="window_one",
        )
        c2, part, up, dn = call(
            lambda *refs: later_stage(False, *refs), stage_out,
            c1, own, lo, hi, deep, scale, name="stage_two",
        )
        lo, hi = exchange(up, dn)
        own, acc, deep, scale2, pc2, flat3b, sum3b = call(
            window_two, window_out + coef_deep + coef_half,
            c2, flat1, scale, pc, part, acc, fields[2], rim_lo, rim_hi, phi, sum2, name="window_two",
        )
        c3, part, up, dn = call(
            lambda *refs: later_stage(True, *refs), stage_out,
            c1, c2, own, lo, hi, deep, scale2, name="stage_three",
        )
        lo, hi = exchange(up, dn)
        own, acc, deep, scale, pc = call(
            window_three, window_out + coef_deep,
            c3, flat2, scale2, pc2, part, acc, rim_lo, rim_hi, phi, sum3a, sum3b, name="window_three",
        )
        c4, part, up, dn = call(
            lambda *refs: later_stage(False, *refs), stage_out,
            c3, own, lo, hi, deep, scale, name="stage_four",
        )
        lo, hi = exchange(up, dn)
        own, acc = call(
            window_four, window_out, c4, flat3a, flat3b, scale, pc, part, acc, name="window_four",
        )
        slabs = call(finish, near(count, depth, LANES), c4, c3, own, lo, hi, acc, name="finish")
        slabs = lax.all_to_all(slabs, ("gy", "gx"), 0, 0)
        return call(
            lambda *refs: from_slabs(count, depth, even_at, odd_at, *refs),
            like(BX, BY, LANES), odd, slabs, first=smem, scratch=[turn], name="from_slabs",
        )

    return shards


def solution(mesh):
    spec = P("gx", "gy", "gz")
    return jax.shard_map(
        make_shards(dict(mesh.shape)),
        mesh=mesh,
        in_specs=(spec,) * 5,
        out_specs=spec,
        check_vma=False,
    )
```

```python
import jax
import jax.numpy as jnp
from jax import lax
from jax.experimental import pallas as pl
from jax.experimental.pallas import tpu as pltpu
from jax.sharding import PartitionSpec as P

TAU = 0.3
WENO_EPS = 1e-06
SMOOTH_EPS = 0.01
UNROLL_COEF = 2
EVEN_TURNS, ODD_TURNS, FIRST_GX = (-1, 1, -1, 1), (1, 1, -1, -1), 7
UNROLL_DEPTH = 2
LANES = 128
BX, BY = 8, 16
F32 = jnp.float32


def lane_iota(shape):
    return lax.broadcasted_iota(jnp.int32, shape, len(shape) - 1)


def major_roll(v, k):
    n = v.shape[0]
    return jnp.concatenate([v[(g + k) % n][None] for g in range(n)], axis=0)


def shift_x(v, k):
    lane = lane_iota(v.shape)
    rolled = pltpu.roll(v, (-BY * k) % LANES, 2)
    carried = pltpu.roll(rolled, (-1 if k > 0 else 1) % v.shape[1], 1)
    crossing = lane >= LANES - BY * k if k > 0 else lane < -BY * k
    return jnp.where(crossing, carried, rolled)


def shift_y(v, k):
    inner = lane_iota(v.shape) % BY
    rolled = pltpu.roll(v, (-k) % LANES, 2)
    if k > 0:
        carried = major_roll(pltpu.roll(v, (BY - k) % LANES, 2), 1)
        return jnp.where(inner >= BY - k, carried, rolled)
    carried = major_roll(pltpu.roll(v, (-BY - k) % LANES, 2), -1)
    return jnp.where(inner < -k, carried, rolled)


def shifts_x(v, steps):
    lane = lane_iota(v.shape)
    n = v.shape[1]
    rolled = {k: pltpu.roll(v, (-BY * k) % LANES, 2) for k in steps}
    out = {}
    for k, r in rolled.items():
        carried = pltpu.roll(r, (-1 if k > 0 else 1) % n, 1)
        out[k] = jnp.where(lane >= LANES - BY * k if k > 0 else lane < -BY * k, carried, r)
    return out, rolled


def shifts_y(v, steps, rolled):
    inner = lane_iota(v.shape) % BY
    ahead, behind = major_roll(rolled[-1], 1), major_roll(rolled[1], -1)
    out = {}
    for k in steps:
        mixed = jnp.where(inner < k, ahead, v) if k > 0 else jnp.where(inner >= BY + k, behind, v)
        out[k] = pltpu.roll(mixed, (-k) % LANES, 2)
    return out


def gather_x(parts):
    total = parts[0]
    for k, part in parts.items():
        if k:
            total = total + shift_x(part, k)
    return total


def gather_y(parts):
    total = parts[0]
    inner = lane_iota(total.shape) % BY
    ahead = behind = None
    for k, part in parts.items():
        if k == 0:
            continue
        moved = pltpu.roll(part, (-k) % LANES, 2)
        crossing = inner >= BY - k if k > 0 else inner < -k
        total = total + jnp.where(crossing, 0.0, moved)
        over = jnp.where(crossing, moved, 0.0)
        if k > 0:
            ahead = over if ahead is None else ahead + over
        else:
            behind = over if behind is None else behind + over
    if ahead is not None:
        total = total + major_roll(pltpu.roll(ahead, BY, 2), 1)
    if behind is not None:
        total = total + major_roll(pltpu.roll(behind, LANES - BY, 2), -1)
    return total


def weno_center(b, dm, d0, d1, d2):
    e1, e2, e3 = d0 - dm, d1 - d0, d2 - d1
    p1, p2, p3 = 0.5 * e1 + d0, 0.5 * (d0 + d1), 0.5 * e3 - d1
    f1, f2, f3 = (13.0 / 12.0) * e1, (13.0 / 12.0) * e2, (13.0 / 12.0) * e3
    t1 = WENO_EPS + (f1 * e1 + p1 * p1)
    t2 = WENO_EPS + (f2 * e2 + p2 * p2)
    t3 = WENO_EPS + (f3 * e3 + p3 * p3)
    t12 = t1 * t2
    whole = 1.0 / (t12 * t3)
    i3 = whole * t12
    whole3 = whole * t3
    i1, i2 = whole3 * t2, whole3 * t1
    a1, a2, a3 = i1 * i1, i2 * i2, i3 * i3
    m1, m2, m3 = 0.1 * a1, 0.6 * a2, 0.3 * a3
    r1, r3 = 0.1 * a3, 0.3 * a1
    sum_m, sum_p = m1 + m2 + m3, r1 + m2 + r3
    both = 1.0 / (sum_m * sum_p)
    inv_m, inv_p = both * sum_p, both * sum_m
    w1, w2, w3 = m1 * inv_m, m2 * inv_m, m3 * inv_m
    v1, v2, v3 = r1 * inv_p, m2 * inv_p, r3 * inv_p
    y1, y3 = (e1 - e2) * (1.0 / 3.0), (e2 - e3) * (1.0 / 6.0)
    y1h, y3d = 0.5 * y1, 2.0 * y3
    corr_m = w1 * y1 + w3 * y3
    corr_p = v1 * y3d + v3 * y1h
    base = b + e2 * (1.0 / 3.0)
    minus = base + 0.5 * d0 + corr_m
    plus = base - 0.5 * d1 - corr_p
    j1, j2, j3 = -4.0 * i1, -4.0 * i2, -4.0 * i3
    g1, g3 = f1 + 0.5 * p1, f3 + 0.5 * p3
    half_p2 = 0.5 * p2

    def spread(s1, s2, s3, cy1, cy3, own0, own1):
        ce1 = cy1 + s1 * g1
        ce2 = (cy3 - cy1) + ((1.0 / 3.0) + s2 * f2)
        ce3 = s3 * g3 - cy3
        s2p = s2 * half_p2
        cd0 = s1 * p1 + s2p
        cd1 = s2p - s3 * p3
        if own0:
            cd0 = cd0 + 0.5
        if own1:
            cd1 = cd1 - 0.5
        return (-ce1, cd0 + (ce1 - ce2), cd1 + (ce2 - ce3), ce3)

    jac_m = spread(
        j1 * (w1 * (y1 - corr_m)), -j2 * (w2 * corr_m), j3 * (w3 * (y3 - corr_m)),
        w1 * (1.0 / 3.0), w3 * (1.0 / 6.0), True, False,
    )
    jac_p = spread(
        j1 * (v3 * (corr_p - y1h)), j2 * (v2 * corr_p), j3 * (v1 * (corr_p - y3d)),
        v3 * (-1.0 / 6.0), v1 * (-1.0 / 3.0), False, True,
    )
    return minus, plus, jac_m, jac_p


def upwind_term(minus, plus, side):
    u = jnp.maximum(side * minus, 0.0)
    v = jnp.maximum(-side * plus, 0.0)
    uu, vv = u * u, v * v
    gap = uu - vv
    square = gap * gap + SMOOTH_EPS
    root = lax.rsqrt(square)
    slope = gap * root
    term = 0.5 * (uu + vv + square * root)
    return term, 2.0 * ((1.0 + slope) * (u * side)), -2.0 * ((1.0 - slope) * (v * side))


PER_AXIS = 10


def side_of(phi):
    return jnp.where(phi > 0, 1.0, -1.0).astype(F32)


class Halves:
    def __init__(self, low, high, at):
        self.refs, self.at = (low, high), at

    def __getitem__(self, index):
        index = index if isinstance(index, tuple) else (index,)
        half, plane = divmod(index[self.at], 2)
        return self.refs[half][index[: self.at] + (plane,) + index[self.at + 1 :]]


def coef_planes(f_ref, phi_ref, co_ref, sum_ref, first=0, count=4):
    def plane(z, carry):
        f = f_ref[first + z]
        side = side_of(phi_ref[first + z])
        steps = (-3, -2, -1, 1, 2)
        along_x, rolled = shifts_x(f, steps)
        along_y = shifts_y(f, steps, rolled)
        total = None
        for axis, shift, near in ((0, shift_x, along_x), (1, shift_y, along_y)):
            b = [near[-2] - near[-3], near[-1] - near[-2], f - near[-1], near[1] - f, near[2] - near[1]]
            d = [b[i + 1] - b[i] for i in range(4)]
            minus, plus, jac_m, jac_p = weno_center(b[2], *d)
            term, by_minus, by_plus = upwind_term(minus, shift(plus, 1), side)
            for n, part in enumerate((by_minus, by_plus) + jac_m + jac_p):
                co_ref[PER_AXIS * axis + n, z] = part
            total = term if total is None else total + term
        sum_ref[z] = total
        return carry

    lax.fori_loop(0, count, plane, 0, unroll=UNROLL_COEF)


def coef_depth(section, f_ref, lo_ref, hi_ref, phi_ref, sum_ref, co_ref, scale_ref, pc_ref):
    def column(g, carry):
        f = (
            [lo_ref[3 * section + i, g] for i in range(3)]
            + [f_ref[i, g] for i in range(4)]
            + [hi_ref[3 * section + i, g] for i in range(3)]
        )
        b = [None] + [f[i] - f[i - 1] for i in range(1, 10)]
        d = [None, None] + [b[i] - b[i - 1] for i in range(2, 10)]
        centers = [weno_center(b[m + 3], d[m + 2], d[m + 3], d[m + 4], d[m + 5]) for m in range(5)]
        for z in range(4):
            phi = phi_ref[z, g]
            term, by_minus, by_plus = upwind_term(centers[z][0], centers[z + 1][1], side_of(phi))
            root = lax.rsqrt(phi * phi + 1.0)
            square = sum_ref[z, g] + term
            inv = lax.rsqrt(square)
            scale_ref[z, g] = (-0.25 * TAU) * ((phi * root) * inv)
            pc_ref[z, g] = (-TAU) * ((root * root * root) * (square * inv - 1.0))
            parts = (by_minus, by_plus) + centers[z][2] + centers[z + 1][3]
            for n, part in enumerate(parts):
                co_ref[n, z, g] = part
        return carry

    lax.fori_loop(0, 4, column, 0, unroll=UNROLL_COEF)


def apply_depth(c_ref, co_ref, scale_ref, out_ref, up_ref, dn_ref):
    def column(g, carry):
        dbar = [None] * 8
        bbar = [None] * 9

        def add(into, at, value):
            into[at] = value if into[at] is None else into[at] + value

        for z in range(4):
            c = c_ref[z, g] * scale_ref[z, g]
            co = lambda n: co_ref[n, z, g]
            a, p = c * co(0), c * co(1)
            for k in range(4):
                add(dbar, z + k, a * co(2 + k))
                add(dbar, z + k + 1, p * co(6 + k))
            add(bbar, z + 2, a)
            add(bbar, z + 3, p)
        for j in range(8):
            add(bbar, j + 1, dbar[j])
            add(bbar, j, -dbar[j])
        for z in range(4):
            out_ref[z, g] = bbar[z + 2] - bbar[z + 3]
        for k in range(3):
            up_ref[k, g] = bbar[6 + k]
            dn_ref[k, g] = bbar[k]
        return carry

    lax.fori_loop(0, 4, column, 0, unroll=UNROLL_DEPTH)


def apply_planes(c_ref, co_ref, scale_ref, pc_ref, part_ref, acc_ref, out_ref, acc_out_ref):
    for z in range(4):
        whole = c_ref[z]
        c = whole * scale_ref[z]
        total = part_ref[z]
        for axis, shift, gather in ((0, shift_x, gather_x), (1, shift_y, gather_y)):
            co = lambda n: co_ref[PER_AXIS * axis + n, z]
            a = c * co(0)
            g = shift(c * co(1), -1)
            t = [a * co(2 + k) + g * co(6 + k) for k in range(4)]
            b = [-t[0], t[0] - t[1], (a + g) + (t[1] - t[2]), t[2] - t[3], t[3]]
            total = total + gather(
                {0: b[2] - b[3], -1: b[3] - b[4], -2: b[4], 1: b[1] - b[2], 2: b[0] - b[1], 3: t[0]}
            )
        out_ref[z] = total
        local = pc_ref[z] * whole
        acc_out_ref[z] = local if acc_ref is None else acc_ref[z] + local


def joined(own_ref, lo_ref, hi_ref):
    lo0, lo1, lo2 = lo_ref[0], lo_ref[1], lo_ref[2]
    hi0, hi1, hi2 = hi_ref[0], hi_ref[1], hi_ref[2]
    return (
        own_ref[0] + (lo0 - lo1),
        own_ref[1] + (lo1 - lo2 - hi0),
        own_ref[2] + (lo2 + hi0 - hi1),
        own_ref[3] + (hi1 - hi2),
    )


def planes_kernel(*refs):
    phi_ref = refs[3]
    for n in range(3):
        coef_planes(refs[n], phi_ref, refs[4 + 2 * n], refs[5 + 2 * n])


def first_stage(f_ref, lo_ref, hi_ref, phi_ref, sum_ref, cot_ref, c_ref, part_ref, up_ref, dn_ref, scale_ref, pc_ref, co_ref):
    coef_depth(0, f_ref, lo_ref, hi_ref, phi_ref, sum_ref, co_ref, scale_ref, pc_ref)
    c_ref[...] = 0.5 * cot_ref[...]
    apply_depth(c_ref, co_ref, scale_ref, part_ref, up_ref, dn_ref)


def later_stage(halve, *refs):
    earlier, (own_in, lo_ref, hi_ref, co_ref, scale_ref) = refs[:-9], refs[-9:-4]
    c_ref, part_ref, up_ref, dn_ref = refs[-4:]
    for z, back in enumerate(joined(own_in, lo_ref, hi_ref)):
        c = back
        for ref in earlier:
            c = c + ref[z]
        c_ref[z] = 0.5 * c if halve else c
    apply_depth(c_ref, co_ref, scale_ref, part_ref, up_ref, dn_ref)


def window_one(c_ref, co_ref, scale_ref, pc_ref, part_ref, f_ref, lo_ref, hi_ref, phi_ref, sum_ref, own_ref, acc_ref, *coef_refs):
    apply_planes(c_ref, co_ref, scale_ref, pc_ref, part_ref, None, own_ref, acc_ref)
    coef_depth(1, f_ref, lo_ref, hi_ref, phi_ref, sum_ref, *coef_refs[:3])
    coef_planes(phi_ref, phi_ref, *coef_refs[3:], first=0, count=2)


def window_two(c_ref, co_ref, scale_ref, pc_ref, part_ref, acc_in, f_ref, lo_ref, hi_ref, phi_ref, sum_ref, own_ref, acc_ref, *coef_refs):
    apply_planes(c_ref, co_ref, scale_ref, pc_ref, part_ref, acc_in, own_ref, acc_ref)
    coef_depth(2, f_ref, lo_ref, hi_ref, phi_ref, sum_ref, *coef_refs[:3])
    coef_planes(phi_ref, phi_ref, *coef_refs[3:], first=2, count=2)


def window_three(c_ref, co_ref, scale_ref, pc_ref, part_ref, acc_in, lo_ref, hi_ref, phi_ref, sum_low, sum_high, own_ref, acc_ref, *coef_refs):
    apply_planes(c_ref, co_ref, scale_ref, pc_ref, part_ref, acc_in, own_ref, acc_ref)
    coef_depth(3, phi_ref, lo_ref, hi_ref, phi_ref, Halves(sum_low, sum_high, 0), *coef_refs)


def window_four(c_ref, co_low, co_high, scale_ref, pc_ref, part_ref, acc_in, own_ref, acc_ref):
    apply_planes(c_ref, Halves(co_low, co_high, 1), scale_ref, pc_ref, part_ref, acc_in, own_ref, acc_ref)


def finish(first_ref, middle_ref, own_in, lo_ref, hi_ref, acc_in, out_ref):
    for z, back in enumerate(joined(own_in, lo_ref, hi_ref)):
        whole = (acc_in[z] + back) + (first_ref[z] + middle_ref[z])
        for gy in range(whole.shape[0]):
            for gx in range(whole.shape[1]):
                out_ref[gx * whole.shape[0] + gy, z] = whole[gy, gx]


def slab_line(n_gx, n_gy, turns, gx):
    line = []
    for gy in range(n_gy):
        turn = turns[gy % len(turns)]
        line += [(gy, (gx + turn * step) % n_gx) for step in range(n_gx)]
        gx = (gx - turn) % n_gx
    return line


def to_slabs(count, depth, even_at, odd_at, *refs):
    odd_ref, ins, out_ref, scratch = refs[0], refs[1:-2], refs[-2], refs[-1]
    odd = odd_ref[0] == 1
    for n, ref in enumerate(ins):
        block = ref[...].reshape(BX * BY, LANES)
        scratch[...] = block.T
        for j in range(count):
            even_rows = scratch[pl.ds(depth * even_at[j], depth), :]
            odd_rows = scratch[pl.ds(depth * odd_at[j], depth), :]
            out_ref[j, pl.ds(depth * n, depth), :] = jnp.where(odd, odd_rows, even_rows)


def from_slabs(count, depth, even_at, odd_at, odd_ref, in_ref, out_ref, scratch):
    odd = odd_ref[0] == 1
    for at in range(count):
        even_rows, odd_rows = in_ref[even_at.index(at)], in_ref[odd_at.index(at)]
        scratch[pl.ds(depth * at, depth), :] = jnp.where(odd, odd_rows, even_rows)
    out_ref[...] = scratch[...].T.reshape(BX, BY, LANES)


def unpack(n_gy, n_gx, in_ref, f0, f1, f2, f3, f4, up_ref, dn_ref):
    outs = (f0, f1, f2, f3, f4)
    for n, out in enumerate(outs):
        for z in range(4):
            for gy in range(n_gy):
                rows = in_ref[pl.ds(gy, n_gx, stride=n_gy), 4 * n + z, :]
                out[z, gy] = rows
                if n < 4:
                    if z >= 1:
                        up_ref[3 * n + z - 1, gy] = rows
                    if z <= 2:
                        dn_ref[3 * n + z, gy] = rows


def make_shards(sizes, interpret=False):
    n_gx, n_gy, n_gz = sizes["gx"], sizes["gy"], sizes["gz"]
    count = n_gx * n_gy
    depth = LANES // count
    assert depth == 4
    even_line = slab_line(n_gx, n_gy, EVEN_TURNS, FIRST_GX % n_gx)
    odd_line = slab_line(n_gx, n_gy, ODD_TURNS, FIRST_GX % n_gx)[::-1]
    even_at = [even_line.index((j % n_gy, j // n_gy)) for j in range(count)]
    odd_at = [odd_line.index((j % n_gy, j // n_gy)) for j in range(count)]
    order = []
    for gz in range(n_gz):
        order += [(gx * n_gy + gy) * n_gz + gz for gy, gx in (odd_line if gz % 2 else even_line)]
    total = len(order)
    upward = [(order[i], order[(i + 1) % total]) for i in range(total)]
    downward = [(order[(i + 1) % total], order[i]) for i in range(total)]
    everywhere = ("gx", "gy", "gz")
    vmem = pl.BlockSpec(memory_space=pltpu.VMEM)
    smem = pl.BlockSpec(memory_space=pltpu.SMEM)
    slab = (4, n_gy, n_gx, LANES)
    rim = (3, n_gy, n_gx, LANES)

    def like(*shape):
        return jax.ShapeDtypeStruct(shape, F32)

    def near(*shape):
        return like(*shape) if interpret else pltpu.VMEM(shape, F32)

    def call(kernel, out_shape, *args, first=vmem, scratch=(), name=None, far=False):
        many = isinstance(out_shape, list)
        if not interpret:
            space = pltpu.HBM if far else pltpu.VMEM
            args = [x if x.ndim == 1 else pltpu.with_memory_space_constraint(x, space) for x in args]
        return pl.pallas_call(
            kernel,
            out_shape=out_shape,
            in_specs=[first] + [vmem] * (len(args) - 1),
            out_specs=[vmem] * len(out_shape) if many else vmem,
            scratch_shapes=list(scratch),
            compiler_params=pltpu.CompilerParams(vmem_limit_bytes=8 << 20),
            name=name,
            interpret=interpret,
        )(*args)

    def exchange(up, dn):
        return lax.ppermute(up, everywhere, upward), lax.ppermute(dn, everywhere, downward)

    def shards(phi_start, section_first, section_middle, section_second, cot_final):
        odd = (lax.axis_index("gz") % 2).astype(jnp.int32).reshape(1)
        turn = pltpu.VMEM((LANES, LANES), F32)

        packed = call(
            lambda *refs: to_slabs(count, depth, even_at, odd_at, *refs),
            near(count, 5 * depth, LANES),
            odd, section_second, section_middle, section_first, phi_start, cot_final,
            first=smem, far=True, scratch=[turn], name="to_slabs",
        )
        packed = lax.all_to_all(packed, ("gx", "gy"), 0, 0)
        *fields, rim_up, rim_dn = call(
            lambda *refs: unpack(n_gy, n_gx, *refs),
            [near(*slab)] * 5 + [near(12, *slab[1:])] * 2,
            packed, name="unpack",
        )
        phi, cot = fields[3], fields[4]
        rim_lo, rim_hi = exchange(rim_up, rim_dn)

        coef_flat = [near(2 * PER_AXIS, *slab), near(*slab)]
        coef_half = [near(2 * PER_AXIS, 2, *slab[1:]), near(2, *slab[1:])]
        coef_deep = [near(PER_AXIS, *slab), near(*slab), near(*slab)]
        stage_out = [near(*slab), near(*slab), near(*rim), near(*rim)]
        window_out = [near(*slab), near(*slab)]

        flat0, sum0, flat1, sum1, flat2, sum2 = call(
            planes_kernel, coef_flat * 3, *fields[:3], phi, name="coef_planes"
        )
        c1, part, up, dn, scale0, pc0 = call(
            first_stage, stage_out + [near(*slab), near(*slab)],
            fields[0], rim_lo, rim_hi, phi, sum0, cot,
            scratch=[pltpu.VMEM((PER_AXIS, *slab), F32)], name="stage_one",
        )
        lo, hi = exchange(up, dn)
        own, acc, deep, scale, pc, flat3a, sum3a = call(
            window_one, window_out + coef_deep + coef_half,
            c1, flat0, scale0, pc0, part, fields[1], rim_lo, rim_hi, phi, sum1, name="window_one",
        )
        c2, part, up, dn = call(
            lambda *refs: later_stage(False, *refs), stage_out,
            c1, own, lo, hi, deep, scale, name="stage_two",
        )
        lo, hi = exchange(up, dn)
        own, acc, deep, scale2, pc2, flat3b, sum3b = call(
            window_two, window_out + coef_deep + coef_half,
            c2, flat1, scale, pc, part, acc, fields[2], rim_lo, rim_hi, phi, sum2, name="window_two",
        )
        c3, part, up, dn = call(
            lambda *refs: later_stage(True, *refs), stage_out,
            c1, c2, own, lo, hi, deep, scale2, name="stage_three",
        )
        lo, hi = exchange(up, dn)
        own, acc, deep, scale, pc = call(
            window_three, window_out + coef_deep,
            c3, flat2, scale2, pc2, part, acc, rim_lo, rim_hi, phi, sum3a, sum3b, name="window_three",
        )
        c4, part, up, dn = call(
            lambda *refs: later_stage(False, *refs), stage_out,
            c3, own, lo, hi, deep, scale, name="stage_four",
        )
        lo, hi = exchange(up, dn)
        own, acc = call(
            window_four, window_out, c4, flat3a, flat3b, scale, pc, part, acc, name="window_four",
        )
        slabs = call(finish, near(count, depth, LANES), c4, c3, own, lo, hi, acc, name="finish")
        slabs = lax.all_to_all(slabs, ("gx", "gy"), 0, 0)
        return call(
            lambda *refs: from_slabs(count, depth, even_at, odd_at, *refs),
            like(BX, BY, LANES), odd, slabs, first=smem, scratch=[turn], name="from_slabs",
        )

    return shards


def solution(mesh):
    spec = P("gx", "gy", "gz")
    return jax.shard_map(
        make_shards(dict(mesh.shape)),
        mesh=mesh,
        in_specs=(spec,) * 5,
        out_specs=spec,
        check_vma=False,
    )
```

```python
import jax
import jax.numpy as jnp
from jax import lax
from jax.experimental import pallas as pl
from jax.experimental.pallas import tpu as pltpu
from jax.sharding import PartitionSpec as P

TAU = 0.3
WENO_EPS = 1e-06
SMOOTH_EPS = 0.01
UNROLL_COEF = 2
EVEN_TURNS, ODD_TURNS, FIRST_GX = (-1, 1, -1, 1), (1, 1, -1, -1), 7
UNROLL_DEPTH = 2
LANES = 128
BX, BY = 8, 16
F32 = jnp.float32


def lane_iota(shape):
    return lax.broadcasted_iota(jnp.int32, shape, len(shape) - 1)


def major_roll(v, k):
    n = v.shape[0]
    return jnp.concatenate([v[(g + k) % n][None] for g in range(n)], axis=0)


def shift_x(v, k):
    lane = lane_iota(v.shape)
    rolled = pltpu.roll(v, (-BY * k) % LANES, 2)
    carried = pltpu.roll(rolled, (-1 if k > 0 else 1) % v.shape[1], 1)
    crossing = lane >= LANES - BY * k if k > 0 else lane < -BY * k
    return jnp.where(crossing, carried, rolled)


def shift_y(v, k):
    inner = lane_iota(v.shape) % BY
    rolled = pltpu.roll(v, (-k) % LANES, 2)
    if k > 0:
        carried = major_roll(pltpu.roll(v, (BY - k) % LANES, 2), 1)
        return jnp.where(inner >= BY - k, carried, rolled)
    carried = major_roll(pltpu.roll(v, (-BY - k) % LANES, 2), -1)
    return jnp.where(inner < -k, carried, rolled)


def shifts_x(v, steps):
    lane = lane_iota(v.shape)
    n = v.shape[1]
    rolled = {k: pltpu.roll(v, (-BY * k) % LANES, 2) for k in steps}
    out = {}
    for k, r in rolled.items():
        carried = pltpu.roll(r, (-1 if k > 0 else 1) % n, 1)
        out[k] = jnp.where(lane >= LANES - BY * k if k > 0 else lane < -BY * k, carried, r)
    return out, rolled


def shifts_y(v, steps, rolled):
    inner = lane_iota(v.shape) % BY
    ahead, behind = major_roll(rolled[-1], 1), major_roll(rolled[1], -1)
    out = {}
    for k in steps:
        mixed = jnp.where(inner < k, ahead, v) if k > 0 else jnp.where(inner >= BY + k, behind, v)
        out[k] = pltpu.roll(mixed, (-k) % LANES, 2)
    return out


def gather_x(parts):
    total = parts[0]
    for k, part in parts.items():
        if k:
            total = total + shift_x(part, k)
    return total


def gather_y(parts):
    total = parts[0]
    inner = lane_iota(total.shape) % BY
    ahead = behind = None
    for k, part in parts.items():
        if k == 0:
            continue
        moved = pltpu.roll(part, (-k) % LANES, 2)
        crossing = inner >= BY - k if k > 0 else inner < -k
        total = total + jnp.where(crossing, 0.0, moved)
        over = jnp.where(crossing, moved, 0.0)
        if k > 0:
            ahead = over if ahead is None else ahead + over
        else:
            behind = over if behind is None else behind + over
    if ahead is not None:
        total = total + major_roll(pltpu.roll(ahead, BY, 2), 1)
    if behind is not None:
        total = total + major_roll(pltpu.roll(behind, LANES - BY, 2), -1)
    return total


def weno_center(b, dm, d0, d1, d2):
    e1, e2, e3 = d0 - dm, d1 - d0, d2 - d1
    p1, p2, p3 = 0.5 * e1 + d0, 0.5 * (d0 + d1), 0.5 * e3 - d1
    f1, f2, f3 = (13.0 / 12.0) * e1, (13.0 / 12.0) * e2, (13.0 / 12.0) * e3
    t1 = WENO_EPS + (f1 * e1 + p1 * p1)
    t2 = WENO_EPS + (f2 * e2 + p2 * p2)
    t3 = WENO_EPS + (f3 * e3 + p3 * p3)
    t12 = t1 * t2
    whole = 1.0 / (t12 * t3)
    i3 = whole * t12
    whole3 = whole * t3
    i1, i2 = whole3 * t2, whole3 * t1
    a1, a2, a3 = i1 * i1, i2 * i2, i3 * i3
    m1, m2, m3 = 0.1 * a1, 0.6 * a2, 0.3 * a3
    r1, r3 = 0.1 * a3, 0.3 * a1
    sum_m, sum_p = m1 + m2 + m3, r1 + m2 + r3
    both = 1.0 / (sum_m * sum_p)
    inv_m, inv_p = both * sum_p, both * sum_m
    w1, w2, w3 = m1 * inv_m, m2 * inv_m, m3 * inv_m
    v1, v2, v3 = r1 * inv_p, m2 * inv_p, r3 * inv_p
    y1, y3 = (e1 - e2) * (1.0 / 3.0), (e2 - e3) * (1.0 / 6.0)
    y1h, y3d = 0.5 * y1, 2.0 * y3
    corr_m = w1 * y1 + w3 * y3
    corr_p = v1 * y3d + v3 * y1h
    base = b + e2 * (1.0 / 3.0)
    minus = base + 0.5 * d0 + corr_m
    plus = base - 0.5 * d1 - corr_p
    j1, j2, j3 = -4.0 * i1, -4.0 * i2, -4.0 * i3
    g1, g3 = f1 + 0.5 * p1, f3 + 0.5 * p3
    half_p2 = 0.5 * p2

    def spread(s1, s2, s3, cy1, cy3, own0, own1):
        ce1 = cy1 + s1 * g1
        ce2 = (cy3 - cy1) + ((1.0 / 3.0) + s2 * f2)
        ce3 = s3 * g3 - cy3
        s2p = s2 * half_p2
        cd0 = s1 * p1 + s2p
        cd1 = s2p - s3 * p3
        if own0:
            cd0 = cd0 + 0.5
        if own1:
            cd1 = cd1 - 0.5
        return (-ce1, cd0 + (ce1 - ce2), cd1 + (ce2 - ce3), ce3)

    jac_m = spread(
        j1 * (w1 * (y1 - corr_m)), -j2 * (w2 * corr_m), j3 * (w3 * (y3 - corr_m)),
        w1 * (1.0 / 3.0), w3 * (1.0 / 6.0), True, False,
    )
    jac_p = spread(
        j1 * (v3 * (corr_p - y1h)), j2 * (v2 * corr_p), j3 * (v1 * (corr_p - y3d)),
        v3 * (-1.0 / 6.0), v1 * (-1.0 / 3.0), False, True,
    )
    return minus, plus, jac_m, jac_p


def upwind_term(minus, plus, side):
    u = jnp.maximum(side * minus, 0.0)
    v = jnp.maximum(-side * plus, 0.0)
    uu, vv = u * u, v * v
    gap = uu - vv
    square = gap * gap + SMOOTH_EPS
    root = lax.rsqrt(square)
    slope = gap * root
    term = 0.5 * (uu + vv + square * root)
    return term, 2.0 * ((1.0 + slope) * (u * side)), -2.0 * ((1.0 - slope) * (v * side))


PER_AXIS = 10


def side_of(phi):
    return jnp.where(phi > 0, 1.0, -1.0).astype(F32)


class Halves:
    def __init__(self, low, high, at):
        self.refs, self.at = (low, high), at

    def __getitem__(self, index):
        index = index if isinstance(index, tuple) else (index,)
        half, plane = divmod(index[self.at], 2)
        return self.refs[half][index[: self.at] + (plane,) + index[self.at + 1 :]]


def coef_planes(f_ref, phi_ref, co_ref, sum_ref, first=0, count=4):
    def plane(z, carry):
        f = f_ref[first + z]
        side = side_of(phi_ref[first + z])
        steps = (-3, -2, -1, 1, 2)
        along_x, rolled = shifts_x(f, steps)
        along_y = shifts_y(f, steps, rolled)
        total = None
        for axis, shift, near in ((0, shift_x, along_x), (1, shift_y, along_y)):
            b = [near[-2] - near[-3], near[-1] - near[-2], f - near[-1], near[1] - f, near[2] - near[1]]
            d = [b[i + 1] - b[i] for i in range(4)]
            minus, plus, jac_m, jac_p = weno_center(b[2], *d)
            term, by_minus, by_plus = upwind_term(minus, shift(plus, 1), side)
            for n, part in enumerate((by_minus, by_plus) + jac_m + jac_p):
                co_ref[PER_AXIS * axis + n, z] = part
            total = term if total is None else total + term
        sum_ref[z] = total
        return carry

    lax.fori_loop(0, count, plane, 0, unroll=UNROLL_COEF)


def coef_depth(section, f_ref, lo_ref, hi_ref, phi_ref, sum_ref, co_ref, scale_ref, pc_ref, unroll=2):
    def column(g, carry):
        f = (
            [lo_ref[3 * section + i, g] for i in range(3)]
            + [f_ref[i, g] for i in range(4)]
            + [hi_ref[3 * section + i, g] for i in range(3)]
        )
        b = [None] + [f[i] - f[i - 1] for i in range(1, 10)]
        d = [None, None] + [b[i] - b[i - 1] for i in range(2, 10)]
        centers = [weno_center(b[m + 3], d[m + 2], d[m + 3], d[m + 4], d[m + 5]) for m in range(5)]
        for z in range(4):
            phi = phi_ref[z, g]
            term, by_minus, by_plus = upwind_term(centers[z][0], centers[z + 1][1], side_of(phi))
            root = lax.rsqrt(phi * phi + 1.0)
            square = sum_ref[z, g] + term
            inv = lax.rsqrt(square)
            scale_ref[z, g] = (-0.25 * TAU) * ((phi * root) * inv)
            pc_ref[z, g] = (-TAU) * ((root * root * root) * (square * inv - 1.0))
            parts = (by_minus, by_plus) + centers[z][2] + centers[z + 1][3]
            for n, part in enumerate(parts):
                co_ref[n, z, g] = part
        return carry

    lax.fori_loop(0, 4, column, 0, unroll=unroll)


def apply_depth(c_ref, co_ref, scale_ref, out_ref, up_ref, dn_ref):
    def column(g, carry):
        dbar = [None] * 8
        bbar = [None] * 9

        def add(into, at, value):
            into[at] = value if into[at] is None else into[at] + value

        for z in range(4):
            c = c_ref[z, g] * scale_ref[z, g]
            co = lambda n: co_ref[n, z, g]
            a, p = c * co(0), c * co(1)
            for k in range(4):
                add(dbar, z + k, a * co(2 + k))
                add(dbar, z + k + 1, p * co(6 + k))
            add(bbar, z + 2, a)
            add(bbar, z + 3, p)
        for j in range(8):
            add(bbar, j + 1, dbar[j])
            add(bbar, j, -dbar[j])
        for z in range(4):
            out_ref[z, g] = bbar[z + 2] - bbar[z + 3]
        for k in range(3):
            up_ref[k, g] = bbar[6 + k]
            dn_ref[k, g] = bbar[k]
        return carry

    lax.fori_loop(0, 4, column, 0, unroll=UNROLL_DEPTH)


def apply_planes(c_ref, co_ref, scale_ref, pc_ref, part_ref, acc_ref, out_ref, acc_out_ref):
    for z in range(4):
        whole = c_ref[z]
        c = whole * scale_ref[z]
        total = part_ref[z]
        for axis, shift, gather in ((0, shift_x, gather_x), (1, shift_y, gather_y)):
            co = lambda n: co_ref[PER_AXIS * axis + n, z]
            a = c * co(0)
            g = shift(c * co(1), -1)
            t = [a * co(2 + k) + g * co(6 + k) for k in range(4)]
            b = [-t[0], t[0] - t[1], (a + g) + (t[1] - t[2]), t[2] - t[3], t[3]]
            total = total + gather(
                {0: b[2] - b[3], -1: b[3] - b[4], -2: b[4], 1: b[1] - b[2], 2: b[0] - b[1], 3: t[0]}
            )
        out_ref[z] = total
        local = pc_ref[z] * whole
        acc_out_ref[z] = local if acc_ref is None else acc_ref[z] + local


def joined(own_ref, lo_ref, hi_ref):
    lo0, lo1, lo2 = lo_ref[0], lo_ref[1], lo_ref[2]
    hi0, hi1, hi2 = hi_ref[0], hi_ref[1], hi_ref[2]
    return (
        own_ref[0] + (lo0 - lo1),
        own_ref[1] + (lo1 - lo2 - hi0),
        own_ref[2] + (lo2 + hi0 - hi1),
        own_ref[3] + (hi1 - hi2),
    )


def planes_kernel(*refs):
    phi_ref = refs[3]
    for n in range(3):
        coef_planes(refs[n], phi_ref, refs[4 + 2 * n], refs[5 + 2 * n])


def first_stage(f_ref, lo_ref, hi_ref, phi_ref, sum_ref, cot_ref, c_ref, part_ref, up_ref, dn_ref, scale_ref, pc_ref, co_ref):
    coef_depth(0, f_ref, lo_ref, hi_ref, phi_ref, sum_ref, co_ref, scale_ref, pc_ref, unroll=4)
    c_ref[...] = 0.5 * cot_ref[...]
    apply_depth(c_ref, co_ref, scale_ref, part_ref, up_ref, dn_ref)


def later_stage(halve, *refs):
    earlier, (own_in, lo_ref, hi_ref, co_ref, scale_ref) = refs[:-9], refs[-9:-4]
    c_ref, part_ref, up_ref, dn_ref = refs[-4:]
    for z, back in enumerate(joined(own_in, lo_ref, hi_ref)):
        c = back
        for ref in earlier:
            c = c + ref[z]
        c_ref[z] = 0.5 * c if halve else c
    apply_depth(c_ref, co_ref, scale_ref, part_ref, up_ref, dn_ref)


def window_one(c_ref, co_ref, scale_ref, pc_ref, part_ref, f_ref, lo_ref, hi_ref, phi_ref, sum_ref, own_ref, acc_ref, *coef_refs):
    apply_planes(c_ref, co_ref, scale_ref, pc_ref, part_ref, None, own_ref, acc_ref)
    coef_depth(1, f_ref, lo_ref, hi_ref, phi_ref, sum_ref, *coef_refs[:3])
    coef_planes(phi_ref, phi_ref, *coef_refs[3:], first=0, count=2)


def window_two(c_ref, co_ref, scale_ref, pc_ref, part_ref, acc_in, f_ref, lo_ref, hi_ref, phi_ref, sum_ref, own_ref, acc_ref, *coef_refs):
    apply_planes(c_ref, co_ref, scale_ref, pc_ref, part_ref, acc_in, own_ref, acc_ref)
    coef_depth(2, f_ref, lo_ref, hi_ref, phi_ref, sum_ref, *coef_refs[:3])
    coef_planes(phi_ref, phi_ref, *coef_refs[3:], first=2, count=2)


def window_three(c_ref, co_ref, scale_ref, pc_ref, part_ref, acc_in, lo_ref, hi_ref, phi_ref, sum_low, sum_high, own_ref, acc_ref, *coef_refs):
    apply_planes(c_ref, co_ref, scale_ref, pc_ref, part_ref, acc_in, own_ref, acc_ref)
    coef_depth(3, phi_ref, lo_ref, hi_ref, phi_ref, Halves(sum_low, sum_high, 0), *coef_refs)


def window_four(c_ref, co_low, co_high, scale_ref, pc_ref, part_ref, acc_in, own_ref, acc_ref):
    apply_planes(c_ref, Halves(co_low, co_high, 1), scale_ref, pc_ref, part_ref, acc_in, own_ref, acc_ref)


def finish(first_ref, middle_ref, own_in, lo_ref, hi_ref, acc_in, out_ref):
    for z, back in enumerate(joined(own_in, lo_ref, hi_ref)):
        whole = (acc_in[z] + back) + (first_ref[z] + middle_ref[z])
        for gy in range(whole.shape[0]):
            for gx in range(whole.shape[1]):
                out_ref[gx * whole.shape[0] + gy, z] = whole[gy, gx]


def slab_line(n_gx, n_gy, turns, gx):
    line = []
    for gy in range(n_gy):
        turn = turns[gy % len(turns)]
        line += [(gy, (gx + turn * step) % n_gx) for step in range(n_gx)]
        gx = (gx - turn) % n_gx
    return line


def to_slabs(count, depth, even_at, odd_at, *refs):
    odd_ref, ins, out_ref = refs[0], refs[1:-4], refs[-4]
    scratch, bricks, sems = refs[-3:]
    copies = [pltpu.make_async_copy(ref, bricks.at[n], sems.at[n]) for n, ref in enumerate(ins)]
    for copy in copies:
        copy.start()
    odd = odd_ref[0] == 1
    for n, copy in enumerate(copies):
        copy.wait()
        block = bricks[n].reshape(BX * BY, LANES)
        scratch[...] = block.T
        for j in range(count):
            even_rows = scratch[pl.ds(depth * even_at[j], depth), :]
            odd_rows = scratch[pl.ds(depth * odd_at[j], depth), :]
            out_ref[j, pl.ds(depth * n, depth), :] = jnp.where(odd, odd_rows, even_rows)


def from_slabs(count, depth, even_at, odd_at, odd_ref, in_ref, out_ref, scratch):
    odd = odd_ref[0] == 1
    for at in range(count):
        even_rows, odd_rows = in_ref[even_at.index(at)], in_ref[odd_at.index(at)]
        scratch[pl.ds(depth * at, depth), :] = jnp.where(odd, odd_rows, even_rows)
    out_ref[...] = scratch[...].T.reshape(BX, BY, LANES)


def unpack(n_gy, n_gx, in_ref, f0, f1, f2, f3, f4, up_ref, dn_ref):
    outs = (f0, f1, f2, f3, f4)
    for n, out in enumerate(outs):
        for z in range(4):
            for gy in range(n_gy):
                rows = in_ref[pl.ds(gy, n_gx, stride=n_gy), 4 * n + z, :]
                out[z, gy] = rows
                if n < 4:
                    if z >= 1:
                        up_ref[3 * n + z - 1, gy] = rows
                    if z <= 2:
                        dn_ref[3 * n + z, gy] = rows


def make_shards(sizes, interpret=False):
    n_gx, n_gy, n_gz = sizes["gx"], sizes["gy"], sizes["gz"]
    count = n_gx * n_gy
    depth = LANES // count
    assert depth == 4
    even_line = slab_line(n_gx, n_gy, EVEN_TURNS, FIRST_GX % n_gx)
    odd_line = slab_line(n_gx, n_gy, ODD_TURNS, FIRST_GX % n_gx)[::-1]
    even_at = [even_line.index((j % n_gy, j // n_gy)) for j in range(count)]
    odd_at = [odd_line.index((j % n_gy, j // n_gy)) for j in range(count)]
    order = []
    for gz in range(n_gz):
        order += [(gx * n_gy + gy) * n_gz + gz for gy, gx in (odd_line if gz % 2 else even_line)]
    total = len(order)
    upward = [(order[i], order[(i + 1) % total]) for i in range(total)]
    downward = [(order[(i + 1) % total], order[i]) for i in range(total)]
    everywhere = ("gx", "gy", "gz")
    vmem = pl.BlockSpec(memory_space=pltpu.VMEM)
    smem = pl.BlockSpec(memory_space=pltpu.SMEM)
    slab = (4, n_gy, n_gx, LANES)
    rim = (3, n_gy, n_gx, LANES)

    def like(*shape):
        return jax.ShapeDtypeStruct(shape, F32)

    def near(*shape):
        return like(*shape) if interpret else pltpu.VMEM(shape, F32)

    def call(kernel, out_shape, *args, first=vmem, scratch=(), name=None, far=False):
        many = isinstance(out_shape, list)
        if not interpret:
            space = pltpu.HBM if far else pltpu.VMEM
            args = [x if x.ndim == 1 else pltpu.with_memory_space_constraint(x, space) for x in args]
        return pl.pallas_call(
            kernel,
            out_shape=out_shape,
            in_specs=[first] + [pl.BlockSpec(memory_space=pltpu.HBM) if far else vmem] * (len(args) - 1),
            out_specs=[vmem] * len(out_shape) if many else vmem,
            scratch_shapes=list(scratch),
            compiler_params=pltpu.CompilerParams(vmem_limit_bytes=8 << 20),
            name=name,
            interpret=interpret,
        )(*args)

    def exchange(up, dn):
        return lax.ppermute(up, everywhere, upward), lax.ppermute(dn, everywhere, downward)

    def shards(phi_start, section_first, section_middle, section_second, cot_final):
        odd = (lax.axis_index("gz") % 2).astype(jnp.int32).reshape(1)
        turn = pltpu.VMEM((LANES, LANES), F32)

        packed = call(
            lambda *refs: to_slabs(count, depth, even_at, odd_at, *refs),
            near(count, 5 * depth, LANES),
            odd, section_second, section_middle, section_first, phi_start, cot_final,
            first=smem, far=True, name="to_slabs",
            scratch=[turn, pltpu.VMEM((5, BX, BY, LANES), F32), pltpu.SemaphoreType.DMA((5,))],
        )
        packed = lax.all_to_all(packed, ("gx", "gy"), 0, 0)
        *fields, rim_up, rim_dn = call(
            lambda *refs: unpack(n_gy, n_gx, *refs),
            [near(*slab)] * 5 + [near(12, *slab[1:])] * 2,
            packed, name="unpack",
        )
        phi, cot = fields[3], fields[4]
        rim_lo, rim_hi = exchange(rim_up, rim_dn)

        coef_flat = [near(2 * PER_AXIS, *slab), near(*slab)]
        coef_half = [near(2 * PER_AXIS, 2, *slab[1:]), near(2, *slab[1:])]
        coef_deep = [near(PER_AXIS, *slab), near(*slab), near(*slab)]
        stage_out = [near(*slab), near(*slab), near(*rim), near(*rim)]
        window_out = [near(*slab), near(*slab)]

        flat0, sum0, flat1, sum1, flat2, sum2 = call(
            planes_kernel, coef_flat * 3, *fields[:3], phi, name="coef_planes"
        )
        c1, part, up, dn, scale0, pc0 = call(
            first_stage, stage_out + [near(*slab), near(*slab)],
            fields[0], rim_lo, rim_hi, phi, sum0, cot,
            scratch=[pltpu.VMEM((PER_AXIS, *slab), F32)], name="stage_one",
        )
        lo, hi = exchange(up, dn)
        own, acc, deep, scale, pc, flat3a, sum3a = call(
            window_one, window_out + coef_deep + coef_half,
            c1, flat0, scale0, pc0, part, fields[1], rim_lo, rim_hi, phi, sum1, name="window_one",
        )
        c2, part, up, dn = call(
            lambda *refs: later_stage(False, *refs), stage_out,
            c1, own, lo, hi, deep, scale, name="stage_two",
        )
        lo, hi = exchange(up, dn)
        own, acc, deep, scale2, pc2, flat3b, sum3b = call(
            window_two, window_out + coef_deep + coef_half,
            c2, flat1, scale, pc, part, acc, fields[2], rim_lo, rim_hi, phi, sum2, name="window_two",
        )
        c3, part, up, dn = call(
            lambda *refs: later_stage(True, *refs), stage_out,
            c1, c2, own, lo, hi, deep, scale2, name="stage_three",
        )
        lo, hi = exchange(up, dn)
        own, acc, deep, scale, pc = call(
            window_three, window_out + coef_deep,
            c3, flat2, scale2, pc2, part, acc, rim_lo, rim_hi, phi, sum3a, sum3b, name="window_three",
        )
        c4, part, up, dn = call(
            lambda *refs: later_stage(False, *refs), stage_out,
            c3, own, lo, hi, deep, scale, name="stage_four",
        )
        lo, hi = exchange(up, dn)
        own, acc = call(
            window_four, window_out, c4, flat3a, flat3b, scale, pc, part, acc, name="window_four",
        )
        slabs = call(finish, near(count, depth, LANES), c4, c3, own, lo, hi, acc, name="finish")
        slabs = lax.all_to_all(slabs, ("gx", "gy"), 0, 0)
        return call(
            lambda *refs: from_slabs(count, depth, even_at, odd_at, *refs),
            like(BX, BY, LANES), odd, slabs, first=smem, scratch=[turn], name="from_slabs",
        )

    return shards


def solution(mesh):
    spec = P("gx", "gy", "gz")
    return jax.shard_map(
        make_shards(dict(mesh.shape)),
        mesh=mesh,
        in_specs=(spec,) * 5,
        out_specs=spec,
        check_vma=False,
    )
```

```python
import jax
import jax.numpy as jnp
from jax import lax
from jax.experimental import pallas as pl
from jax.experimental.pallas import tpu as pltpu
from jax.sharding import PartitionSpec as P

TAU = 0.3
WENO_EPS = 1e-06
SMOOTH_EPS = 0.01
UNROLL_COEF = 2
EVEN_TURNS, ODD_TURNS, FIRST_GX = (-1, 1, -1, 1), (1, 1, -1, -1), 7
UNROLL_DEPTH = 2
LANES = 128
BX, BY = 8, 16
F32 = jnp.float32


def lane_iota(shape):
    return lax.broadcasted_iota(jnp.int32, shape, len(shape) - 1)


def major_roll(v, k):
    n = v.shape[0]
    return jnp.concatenate([v[(g + k) % n][None] for g in range(n)], axis=0)


def shift_x(v, k):
    lane = lane_iota(v.shape)
    rolled = pltpu.roll(v, (-BY * k) % LANES, 2)
    carried = pltpu.roll(rolled, (-1 if k > 0 else 1) % v.shape[1], 1)
    crossing = lane >= LANES - BY * k if k > 0 else lane < -BY * k
    return jnp.where(crossing, carried, rolled)


def shift_y(v, k):
    inner = lane_iota(v.shape) % BY
    rolled = pltpu.roll(v, (-k) % LANES, 2)
    if k > 0:
        carried = major_roll(pltpu.roll(v, (BY - k) % LANES, 2), 1)
        return jnp.where(inner >= BY - k, carried, rolled)
    carried = major_roll(pltpu.roll(v, (-BY - k) % LANES, 2), -1)
    return jnp.where(inner < -k, carried, rolled)


def shifts_x(v, steps):
    lane = lane_iota(v.shape)
    n = v.shape[1]
    rolled = {k: pltpu.roll(v, (-BY * k) % LANES, 2) for k in steps}
    out = {}
    for k, r in rolled.items():
        carried = pltpu.roll(r, (-1 if k > 0 else 1) % n, 1)
        out[k] = jnp.where(lane >= LANES - BY * k if k > 0 else lane < -BY * k, carried, r)
    return out, rolled


def shifts_y(v, steps, rolled):
    inner = lane_iota(v.shape) % BY
    ahead, behind = major_roll(rolled[-1], 1), major_roll(rolled[1], -1)
    out = {}
    for k in steps:
        mixed = jnp.where(inner < k, ahead, v) if k > 0 else jnp.where(inner >= BY + k, behind, v)
        out[k] = pltpu.roll(mixed, (-k) % LANES, 2)
    return out


def gather_x(parts):
    total = parts[0]
    for k, part in parts.items():
        if k:
            total = total + shift_x(part, k)
    return total


def gather_y(parts):
    total = parts[0]
    inner = lane_iota(total.shape) % BY
    ahead = behind = None
    for k, part in parts.items():
        if k == 0:
            continue
        moved = pltpu.roll(part, (-k) % LANES, 2)
        crossing = inner >= BY - k if k > 0 else inner < -k
        total = total + jnp.where(crossing, 0.0, moved)
        over = jnp.where(crossing, moved, 0.0)
        if k > 0:
            ahead = over if ahead is None else ahead + over
        else:
            behind = over if behind is None else behind + over
    if ahead is not None:
        total = total + major_roll(pltpu.roll(ahead, BY, 2), 1)
    if behind is not None:
        total = total + major_roll(pltpu.roll(behind, LANES - BY, 2), -1)
    return total


def weno_center(b, dm, d0, d1, d2):
    e1, e2, e3 = d0 - dm, d1 - d0, d2 - d1
    p1, p2, p3 = 0.5 * e1 + d0, 0.5 * (d0 + d1), 0.5 * e3 - d1
    f1, f2, f3 = (13.0 / 12.0) * e1, (13.0 / 12.0) * e2, (13.0 / 12.0) * e3
    t1 = WENO_EPS + (f1 * e1 + p1 * p1)
    t2 = WENO_EPS + (f2 * e2 + p2 * p2)
    t3 = WENO_EPS + (f3 * e3 + p3 * p3)
    t12 = t1 * t2
    whole = 1.0 / (t12 * t3)
    i3 = whole * t12
    whole3 = whole * t3
    i1, i2 = whole3 * t2, whole3 * t1
    a1, a2, a3 = i1 * i1, i2 * i2, i3 * i3
    m1, m2, m3 = 0.1 * a1, 0.6 * a2, 0.3 * a3
    r1, r3 = 0.1 * a3, 0.3 * a1
    sum_m, sum_p = m1 + m2 + m3, r1 + m2 + r3
    both = 1.0 / (sum_m * sum_p)
    inv_m, inv_p = both * sum_p, both * sum_m
    w1, w2, w3 = m1 * inv_m, m2 * inv_m, m3 * inv_m
    v1, v2, v3 = r1 * inv_p, m2 * inv_p, r3 * inv_p
    y1, y3 = (e1 - e2) * (1.0 / 3.0), (e2 - e3) * (1.0 / 6.0)
    y1h, y3d = 0.5 * y1, 2.0 * y3
    corr_m = w1 * y1 + w3 * y3
    corr_p = v1 * y3d + v3 * y1h
    base = b + e2 * (1.0 / 3.0)
    minus = base + 0.5 * d0 + corr_m
    plus = base - 0.5 * d1 - corr_p
    j1, j2, j3 = -4.0 * i1, -4.0 * i2, -4.0 * i3
    g1, g3 = f1 + 0.5 * p1, f3 + 0.5 * p3
    half_p2 = 0.5 * p2

    def spread(s1, s2, s3, cy1, cy3, own0, own1):
        ce1 = cy1 + s1 * g1
        ce2 = (cy3 - cy1) + ((1.0 / 3.0) + s2 * f2)
        ce3 = s3 * g3 - cy3
        s2p = s2 * half_p2
        cd0 = s1 * p1 + s2p
        cd1 = s2p - s3 * p3
        if own0:
            cd0 = cd0 + 0.5
        if own1:
            cd1 = cd1 - 0.5
        return (-ce1, cd0 + (ce1 - ce2), cd1 + (ce2 - ce3), ce3)

    jac_m = spread(
        j1 * (w1 * (y1 - corr_m)), -j2 * (w2 * corr_m), j3 * (w3 * (y3 - corr_m)),
        w1 * (1.0 / 3.0), w3 * (1.0 / 6.0), True, False,
    )
    jac_p = spread(
        j1 * (v3 * (corr_p - y1h)), j2 * (v2 * corr_p), j3 * (v1 * (corr_p - y3d)),
        v3 * (-1.0 / 6.0), v1 * (-1.0 / 3.0), False, True,
    )
    return minus, plus, jac_m, jac_p


def upwind_term(minus, plus, side):
    u = jnp.maximum(side * minus, 0.0)
    v = jnp.maximum(-side * plus, 0.0)
    uu, vv = u * u, v * v
    gap = uu - vv
    square = gap * gap + SMOOTH_EPS
    root = lax.rsqrt(square)
    slope = gap * root
    term = 0.5 * (uu + vv + square * root)
    return term, 2.0 * ((1.0 + slope) * (u * side)), -2.0 * ((1.0 - slope) * (v * side))


PER_AXIS = 10


def side_of(phi):
    return jnp.where(phi > 0, 1.0, -1.0).astype(F32)


class Halves:
    def __init__(self, low, high, at):
        self.refs, self.at = (low, high), at

    def __getitem__(self, index):
        index = index if isinstance(index, tuple) else (index,)
        half, plane = divmod(index[self.at], 2)
        return self.refs[half][index[: self.at] + (plane,) + index[self.at + 1 :]]


def coef_planes(f_ref, phi_ref, co_ref, sum_ref, first=0, count=4):
    def plane(z, carry):
        f = f_ref[first + z]
        side = side_of(phi_ref[first + z])
        steps = (-3, -2, -1, 1, 2)
        along_x, rolled = shifts_x(f, steps)
        along_y = shifts_y(f, steps, rolled)
        total = None
        for axis, shift, near in ((0, shift_x, along_x), (1, shift_y, along_y)):
            b = [near[-2] - near[-3], near[-1] - near[-2], f - near[-1], near[1] - f, near[2] - near[1]]
            d = [b[i + 1] - b[i] for i in range(4)]
            minus, plus, jac_m, jac_p = weno_center(b[2], *d)
            term, by_minus, by_plus = upwind_term(minus, shift(plus, 1), side)
            for n, part in enumerate((by_minus, by_plus) + jac_m + jac_p):
                co_ref[PER_AXIS * axis + n, z] = part
            total = term if total is None else total + term
        sum_ref[z] = total
        return carry

    lax.fori_loop(0, count, plane, 0, unroll=UNROLL_COEF)


def coef_depth(section, f_ref, lo_ref, hi_ref, phi_ref, sum_ref, co_ref, scale_ref, pc_ref, unroll=2):
    def column(g, carry):
        f = (
            [lo_ref[3 * section + i, g] for i in range(3)]
            + [f_ref[i, g] for i in range(4)]
            + [hi_ref[3 * section + i, g] for i in range(3)]
        )
        b = [None] + [f[i] - f[i - 1] for i in range(1, 10)]
        d = [None, None] + [b[i] - b[i - 1] for i in range(2, 10)]
        centers = [weno_center(b[m + 3], d[m + 2], d[m + 3], d[m + 4], d[m + 5]) for m in range(5)]
        for z in range(4):
            phi = phi_ref[z, g]
            term, by_minus, by_plus = upwind_term(centers[z][0], centers[z + 1][1], side_of(phi))
            root = lax.rsqrt(phi * phi + 1.0)
            square = sum_ref[z, g] + term
            inv = lax.rsqrt(square)
            scale_ref[z, g] = (-0.25 * TAU) * ((phi * root) * inv)
            pc_ref[z, g] = (-TAU) * ((root * root * root) * (square * inv - 1.0))
            parts = (by_minus, by_plus) + centers[z][2] + centers[z + 1][3]
            for n, part in enumerate(parts):
                co_ref[n, z, g] = part
        return carry

    lax.fori_loop(0, 4, column, 0, unroll=unroll)


def apply_depth(c_ref, co_ref, scale_ref, out_ref, up_ref, dn_ref):
    def column(g, carry):
        dbar = [None] * 8
        bbar = [None] * 9

        def add(into, at, value):
            into[at] = value if into[at] is None else into[at] + value

        for z in range(4):
            c = c_ref[z, g] * scale_ref[z, g]
            co = lambda n: co_ref[n, z, g]
            a, p = c * co(0), c * co(1)
            for k in range(4):
                add(dbar, z + k, a * co(2 + k))
                add(dbar, z + k + 1, p * co(6 + k))
            add(bbar, z + 2, a)
            add(bbar, z + 3, p)
        for j in range(8):
            add(bbar, j + 1, dbar[j])
            add(bbar, j, -dbar[j])
        for z in range(4):
            out_ref[z, g] = bbar[z + 2] - bbar[z + 3]
        for k in range(3):
            up_ref[k, g] = bbar[6 + k]
            dn_ref[k, g] = bbar[k]
        return carry

    lax.fori_loop(0, 4, column, 0, unroll=UNROLL_DEPTH)


def apply_planes(c_ref, co_ref, scale_ref, pc_ref, part_ref, acc_ref, out_ref, acc_out_ref):
    for z in range(4):
        whole = c_ref[z]
        c = whole * scale_ref[z]
        total = part_ref[z]
        for axis, shift, gather in ((0, shift_x, gather_x), (1, shift_y, gather_y)):
            co = lambda n: co_ref[PER_AXIS * axis + n, z]
            a = c * co(0)
            g = shift(c * co(1), -1)
            t = [a * co(2 + k) + g * co(6 + k) for k in range(4)]
            b = [-t[0], t[0] - t[1], (a + g) + (t[1] - t[2]), t[2] - t[3], t[3]]
            total = total + gather(
                {0: b[2] - b[3], -1: b[3] - b[4], -2: b[4], 1: b[1] - b[2], 2: b[0] - b[1], 3: t[0]}
            )
        out_ref[z] = total
        local = pc_ref[z] * whole
        acc_out_ref[z] = local if acc_ref is None else acc_ref[z] + local


def joined(own_ref, lo_ref, hi_ref):
    lo0, lo1, lo2 = lo_ref[0], lo_ref[1], lo_ref[2]
    hi0, hi1, hi2 = hi_ref[0], hi_ref[1], hi_ref[2]
    return (
        own_ref[0] + (lo0 - lo1),
        own_ref[1] + (lo1 - lo2 - hi0),
        own_ref[2] + (lo2 + hi0 - hi1),
        own_ref[3] + (hi1 - hi2),
    )


def planes_kernel(*refs):
    phi_ref = refs[3]
    for n in range(3):
        coef_planes(refs[n], phi_ref, refs[4 + 2 * n], refs[5 + 2 * n])


def first_stage(f_ref, lo_ref, hi_ref, phi_ref, sum_ref, cot_ref, c_ref, part_ref, up_ref, dn_ref, scale_ref, pc_ref, co_ref):
    coef_depth(0, f_ref, lo_ref, hi_ref, phi_ref, sum_ref, co_ref, scale_ref, pc_ref, unroll=4)
    c_ref[...] = 0.5 * cot_ref[...]
    apply_depth(c_ref, co_ref, scale_ref, part_ref, up_ref, dn_ref)


def later_stage(halve, *refs):
    earlier, (own_in, lo_ref, hi_ref, co_ref, scale_ref) = refs[:-9], refs[-9:-4]
    c_ref, part_ref, up_ref, dn_ref = refs[-4:]
    for z, back in enumerate(joined(own_in, lo_ref, hi_ref)):
        c = back
        for ref in earlier:
            c = c + ref[z]
        c_ref[z] = 0.5 * c if halve else c
    apply_depth(c_ref, co_ref, scale_ref, part_ref, up_ref, dn_ref)


def window_one(c_ref, co_ref, scale_ref, pc_ref, part_ref, f_ref, lo_ref, hi_ref, phi_ref, sum_ref, own_ref, acc_ref, *coef_refs):
    apply_planes(c_ref, co_ref, scale_ref, pc_ref, part_ref, None, own_ref, acc_ref)
    coef_depth(1, f_ref, lo_ref, hi_ref, phi_ref, sum_ref, *coef_refs[:3])
    coef_planes(phi_ref, phi_ref, *coef_refs[3:], first=0, count=2)


def window_two(c_ref, co_ref, scale_ref, pc_ref, part_ref, acc_in, f_ref, lo_ref, hi_ref, phi_ref, sum_ref, own_ref, acc_ref, *coef_refs):
    apply_planes(c_ref, co_ref, scale_ref, pc_ref, part_ref, acc_in, own_ref, acc_ref)
    coef_depth(2, f_ref, lo_ref, hi_ref, phi_ref, sum_ref, *coef_refs[:3])
    coef_planes(phi_ref, phi_ref, *coef_refs[3:], first=2, count=2)


def window_three(c_ref, co_ref, scale_ref, pc_ref, part_ref, acc_in, lo_ref, hi_ref, phi_ref, sum_low, sum_high, own_ref, acc_ref, *coef_refs):
    apply_planes(c_ref, co_ref, scale_ref, pc_ref, part_ref, acc_in, own_ref, acc_ref)
    coef_depth(3, phi_ref, lo_ref, hi_ref, phi_ref, Halves(sum_low, sum_high, 0), *coef_refs)


def window_four(middle_ref, c_ref, co_low, co_high, scale_ref, pc_ref, part_ref, acc_in, own_ref, acc_ref):
    apply_planes(c_ref, Halves(co_low, co_high, 1), scale_ref, pc_ref, part_ref, acc_in, own_ref, acc_ref)
    for z in range(4):
        own_ref[z] = own_ref[z] + (acc_ref[z] + (c_ref[z] + middle_ref[z]))


def finish(own_in, lo_ref, hi_ref, out_ref):
    for z, whole in enumerate(joined(own_in, lo_ref, hi_ref)):
        for gy in range(whole.shape[0]):
            for gx in range(whole.shape[1]):
                out_ref[gx * whole.shape[0] + gy, z] = whole[gy, gx]


def slab_line(n_gx, n_gy, turns, gx):
    line = []
    for gy in range(n_gy):
        turn = turns[gy % len(turns)]
        line += [(gy, (gx + turn * step) % n_gx) for step in range(n_gx)]
        gx = (gx - turn) % n_gx
    return line


def to_slabs(count, depth, even_at, odd_at, *refs):
    odd_ref, ins, out_ref, scratch = refs[0], refs[1:-2], refs[-2], refs[-1]
    odd = odd_ref[0] == 1
    for n, ref in enumerate(ins):
        block = ref[...].reshape(BX * BY, LANES)
        scratch[...] = block.T
        for j in range(count):
            even_rows = scratch[pl.ds(depth * even_at[j], depth), :]
            odd_rows = scratch[pl.ds(depth * odd_at[j], depth), :]
            out_ref[j, pl.ds(depth * n, depth), :] = jnp.where(odd, odd_rows, even_rows)


def from_slabs(count, depth, even_at, odd_at, odd_ref, in_ref, out_ref, scratch):
    odd = odd_ref[0] == 1
    for at in range(count):
        even_rows, odd_rows = in_ref[even_at.index(at)], in_ref[odd_at.index(at)]
        scratch[pl.ds(depth * at, depth), :] = jnp.where(odd, odd_rows, even_rows)
    out_ref[...] = scratch[...].T.reshape(BX, BY, LANES)


def unpack(n_gy, n_gx, in_ref, f0, f1, f2, f3, f4, up_ref, dn_ref):
    outs = (f0, f1, f2, f3, f4)
    for n, out in enumerate(outs):
        for z in range(4):
            for gy in range(n_gy):
                rows = in_ref[pl.ds(gy, n_gx, stride=n_gy), 4 * n + z, :]
                out[z, gy] = rows
                if n < 4:
                    if z >= 1:
                        up_ref[3 * n + z - 1, gy] = rows
                    if z <= 2:
                        dn_ref[3 * n + z, gy] = rows


def make_shards(sizes, interpret=False):
    n_gx, n_gy, n_gz = sizes["gx"], sizes["gy"], sizes["gz"]
    count = n_gx * n_gy
    depth = LANES // count
    assert depth == 4
    even_line = slab_line(n_gx, n_gy, EVEN_TURNS, FIRST_GX % n_gx)
    odd_line = slab_line(n_gx, n_gy, ODD_TURNS, FIRST_GX % n_gx)[::-1]
    even_at = [even_line.index((j % n_gy, j // n_gy)) for j in range(count)]
    odd_at = [odd_line.index((j % n_gy, j // n_gy)) for j in range(count)]
    order = []
    for gz in range(n_gz):
        order += [(gx * n_gy + gy) * n_gz + gz for gy, gx in (odd_line if gz % 2 else even_line)]
    total = len(order)
    upward = [(order[i], order[(i + 1) % total]) for i in range(total)]
    downward = [(order[(i + 1) % total], order[i]) for i in range(total)]
    everywhere = ("gx", "gy", "gz")
    vmem = pl.BlockSpec(memory_space=pltpu.VMEM)
    smem = pl.BlockSpec(memory_space=pltpu.SMEM)
    slab = (4, n_gy, n_gx, LANES)
    rim = (3, n_gy, n_gx, LANES)

    def like(*shape):
        return jax.ShapeDtypeStruct(shape, F32)

    def near(*shape):
        return like(*shape) if interpret else pltpu.VMEM(shape, F32)

    def call(kernel, out_shape, *args, first=vmem, scratch=(), name=None, far=False):
        many = isinstance(out_shape, list)
        if not interpret:
            space = pltpu.HBM if far else pltpu.VMEM
            args = [x if x.ndim == 1 else pltpu.with_memory_space_constraint(x, space) for x in args]
        return pl.pallas_call(
            kernel,
            out_shape=out_shape,
            in_specs=[first] + [vmem] * (len(args) - 1),
            out_specs=[vmem] * len(out_shape) if many else vmem,
            scratch_shapes=list(scratch),
            compiler_params=pltpu.CompilerParams(vmem_limit_bytes=8 << 20),
            name=name,
            interpret=interpret,
        )(*args)

    def exchange(up, dn):
        return lax.ppermute(up, everywhere, upward), lax.ppermute(dn, everywhere, downward)

    def shards(phi_start, section_first, section_middle, section_second, cot_final):
        odd = (lax.axis_index("gz") % 2).astype(jnp.int32).reshape(1)
        turn = pltpu.VMEM((LANES, LANES), F32)

        packed = call(
            lambda *refs: to_slabs(count, depth, even_at, odd_at, *refs),
            near(count, 5 * depth, LANES),
            odd, section_second, section_middle, section_first, phi_start, cot_final,
            first=smem, far=True, scratch=[turn], name="to_slabs",
        )
        packed = lax.all_to_all(packed, ("gx", "gy"), 0, 0)
        *fields, rim_up, rim_dn = call(
            lambda *refs: unpack(n_gy, n_gx, *refs),
            [near(*slab)] * 5 + [near(12, *slab[1:])] * 2,
            packed, name="unpack",
        )
        phi, cot = fields[3], fields[4]
        rim_lo, rim_hi = exchange(rim_up, rim_dn)

        coef_flat = [near(2 * PER_AXIS, *slab), near(*slab)]
        coef_half = [near(2 * PER_AXIS, 2, *slab[1:]), near(2, *slab[1:])]
        coef_deep = [near(PER_AXIS, *slab), near(*slab), near(*slab)]
        stage_out = [near(*slab), near(*slab), near(*rim), near(*rim)]
        window_out = [near(*slab), near(*slab)]

        flat0, sum0, flat1, sum1, flat2, sum2 = call(
            planes_kernel, coef_flat * 3, *fields[:3], phi, name="coef_planes"
        )
        c1, part, up, dn, scale0, pc0 = call(
            first_stage, stage_out + [near(*slab), near(*slab)],
            fields[0], rim_lo, rim_hi, phi, sum0, cot,
            scratch=[pltpu.VMEM((PER_AXIS, *slab), F32)], name="stage_one",
        )
        lo, hi = exchange(up, dn)
        own, acc, deep, scale, pc, flat3a, sum3a = call(
            window_one, window_out + coef_deep + coef_half,
            c1, flat0, scale0, pc0, part, fields[1], rim_lo, rim_hi, phi, sum1, name="window_one",
        )
        c2, part, up, dn = call(
            lambda *refs: later_stage(False, *refs), stage_out,
            c1, own, lo, hi, deep, scale, name="stage_two",
        )
        lo, hi = exchange(up, dn)
        own, acc, deep, scale2, pc2, flat3b, sum3b = call(
            window_two, window_out + coef_deep + coef_half,
            c2, flat1, scale, pc, part, acc, fields[2], rim_lo, rim_hi, phi, sum2, name="window_two",
        )
        c3, part, up, dn = call(
            lambda *refs: later_stage(True, *refs), stage_out,
            c1, c2, own, lo, hi, deep, scale2, name="stage_three",
        )
        lo, hi = exchange(up, dn)
        own, acc, deep, scale, pc = call(
            window_three, window_out + coef_deep,
            c3, flat2, scale2, pc2, part, acc, rim_lo, rim_hi, phi, sum3a, sum3b, name="window_three",
        )
        c4, part, up, dn = call(
            lambda *refs: later_stage(False, *refs), stage_out,
            c3, own, lo, hi, deep, scale, name="stage_four",
        )
        lo, hi = exchange(up, dn)
        own = call(
            window_four, near(*slab), c3, c4, flat3a, flat3b, scale, pc, part, acc,
            scratch=[pltpu.VMEM(slab, F32)], name="window_four",
        )
        slabs = call(finish, near(count, depth, LANES), own, lo, hi, name="finish")
        slabs = lax.all_to_all(slabs, ("gx", "gy"), 0, 0)
        return call(
            lambda *refs: from_slabs(count, depth, even_at, odd_at, *refs),
            like(BX, BY, LANES), odd, slabs, first=smem, scratch=[turn], name="from_slabs",
        )

    return shards


def solution(mesh):
    spec = P("gx", "gy", "gz")
    return jax.shard_map(
        make_shards(dict(mesh.shape)),
        mesh=mesh,
        in_specs=(spec,) * 5,
        out_specs=spec,
        check_vma=False,
    )
```

```python
import jax
import jax.numpy as jnp
from jax import lax
from jax.experimental import pallas as pl
from jax.experimental.pallas import tpu as pltpu
from jax.sharding import PartitionSpec as P

TAU = 0.3
WENO_EPS = 1e-06
SMOOTH_EPS = 0.01
UNROLL_COEF = 2
EVEN_TURNS, ODD_TURNS, FIRST_GX = (-1, 1, -1, 1), (1, 1, -1, -1), 7
UNROLL_DEPTH = 4
LANES = 128
BX, BY = 8, 16
F32 = jnp.float32


def lane_iota(shape):
    return lax.broadcasted_iota(jnp.int32, shape, len(shape) - 1)


def major_roll(v, k):
    n = v.shape[0]
    return jnp.concatenate([v[(g + k) % n][None] for g in range(n)], axis=0)


def shift_x(v, k):
    lane = lane_iota(v.shape)
    rolled = pltpu.roll(v, (-BY * k) % LANES, 2)
    carried = pltpu.roll(rolled, (-1 if k > 0 else 1) % v.shape[1], 1)
    crossing = lane >= LANES - BY * k if k > 0 else lane < -BY * k
    return jnp.where(crossing, carried, rolled)


def shift_y(v, k):
    inner = lane_iota(v.shape) % BY
    rolled = pltpu.roll(v, (-k) % LANES, 2)
    if k > 0:
        carried = major_roll(pltpu.roll(v, (BY - k) % LANES, 2), 1)
        return jnp.where(inner >= BY - k, carried, rolled)
    carried = major_roll(pltpu.roll(v, (-BY - k) % LANES, 2), -1)
    return jnp.where(inner < -k, carried, rolled)


def shifts_x(v, steps):
    lane = lane_iota(v.shape)
    n = v.shape[1]
    rolled = {k: pltpu.roll(v, (-BY * k) % LANES, 2) for k in steps}
    out = {}
    for k, r in rolled.items():
        carried = pltpu.roll(r, (-1 if k > 0 else 1) % n, 1)
        out[k] = jnp.where(lane >= LANES - BY * k if k > 0 else lane < -BY * k, carried, r)
    return out, rolled


def shifts_y(v, steps, rolled):
    inner = lane_iota(v.shape) % BY
    ahead, behind = major_roll(rolled[-1], 1), major_roll(rolled[1], -1)
    out = {}
    for k in steps:
        mixed = jnp.where(inner < k, ahead, v) if k > 0 else jnp.where(inner >= BY + k, behind, v)
        out[k] = pltpu.roll(mixed, (-k) % LANES, 2)
    return out


def gather_x(parts):
    total = parts[0]
    for k, part in parts.items():
        if k:
            total = total + shift_x(part, k)
    return total


def gather_y(parts):
    total = parts[0]
    inner = lane_iota(total.shape) % BY
    ahead = behind = None
    for k, part in parts.items():
        if k == 0:
            continue
        moved = pltpu.roll(part, (-k) % LANES, 2)
        crossing = inner >= BY - k if k > 0 else inner < -k
        total = total + jnp.where(crossing, 0.0, moved)
        over = jnp.where(crossing, moved, 0.0)
        if k > 0:
            ahead = over if ahead is None else ahead + over
        else:
            behind = over if behind is None else behind + over
    if ahead is not None:
        total = total + major_roll(pltpu.roll(ahead, BY, 2), 1)
    if behind is not None:
        total = total + major_roll(pltpu.roll(behind, LANES - BY, 2), -1)
    return total


def weno_center(b, dm, d0, d1, d2):
    e1, e2, e3 = d0 - dm, d1 - d0, d2 - d1
    p1, p2, p3 = 0.5 * e1 + d0, 0.5 * (d0 + d1), 0.5 * e3 - d1
    f1, f2, f3 = (13.0 / 12.0) * e1, (13.0 / 12.0) * e2, (13.0 / 12.0) * e3
    t1 = WENO_EPS + (f1 * e1 + p1 * p1)
    t2 = WENO_EPS + (f2 * e2 + p2 * p2)
    t3 = WENO_EPS + (f3 * e3 + p3 * p3)
    t12 = t1 * t2
    whole = 1.0 / (t12 * t3)
    i3 = whole * t12
    whole3 = whole * t3
    i1, i2 = whole3 * t2, whole3 * t1
    a1, a2, a3 = i1 * i1, i2 * i2, i3 * i3
    m1, m2, m3 = 0.1 * a1, 0.6 * a2, 0.3 * a3
    r1, r3 = 0.1 * a3, 0.3 * a1
    sum_m, sum_p = m1 + m2 + m3, r1 + m2 + r3
    both = 1.0 / (sum_m * sum_p)
    inv_m, inv_p = both * sum_p, both * sum_m
    w1, w2, w3 = m1 * inv_m, m2 * inv_m, m3 * inv_m
    v1, v2, v3 = r1 * inv_p, m2 * inv_p, r3 * inv_p
    y1, y3 = (e1 - e2) * (1.0 / 3.0), (e2 - e3) * (1.0 / 6.0)
    y1h, y3d = 0.5 * y1, 2.0 * y3
    corr_m = w1 * y1 + w3 * y3
    corr_p = v1 * y3d + v3 * y1h
    base = b + e2 * (1.0 / 3.0)
    minus = base + 0.5 * d0 + corr_m
    plus = base - 0.5 * d1 - corr_p
    j1, j2, j3 = -4.0 * i1, -4.0 * i2, -4.0 * i3
    g1, g3 = f1 + 0.5 * p1, f3 + 0.5 * p3
    half_p2 = 0.5 * p2

    def spread(s1, s2, s3, cy1, cy3, own0, own1):
        ce1 = cy1 + s1 * g1
        ce2 = (cy3 - cy1) + ((1.0 / 3.0) + s2 * f2)
        ce3 = s3 * g3 - cy3
        s2p = s2 * half_p2
        cd0 = s1 * p1 + s2p
        cd1 = s2p - s3 * p3
        if own0:
            cd0 = cd0 + 0.5
        if own1:
            cd1 = cd1 - 0.5
        return (-ce1, cd0 + (ce1 - ce2), cd1 + (ce2 - ce3), ce3)

    jac_m = spread(
        j1 * (w1 * (y1 - corr_m)), -j2 * (w2 * corr_m), j3 * (w3 * (y3 - corr_m)),
        w1 * (1.0 / 3.0), w3 * (1.0 / 6.0), True, False,
    )
    jac_p = spread(
        j1 * (v3 * (corr_p - y1h)), j2 * (v2 * corr_p), j3 * (v1 * (corr_p - y3d)),
        v3 * (-1.0 / 6.0), v1 * (-1.0 / 3.0), False, True,
    )
    return minus, plus, jac_m, jac_p


def upwind_term(minus, plus, side):
    u = jnp.maximum(side * minus, 0.0)
    v = jnp.maximum(-side * plus, 0.0)
    uu, vv = u * u, v * v
    gap = uu - vv
    square = gap * gap + SMOOTH_EPS
    root = lax.rsqrt(square)
    slope = gap * root
    term = 0.5 * (uu + vv + square * root)
    return term, 2.0 * ((1.0 + slope) * (u * side)), -2.0 * ((1.0 - slope) * (v * side))


PER_AXIS = 10


def side_of(phi):
    return jnp.where(phi > 0, 1.0, -1.0).astype(F32)


class Halves:
    def __init__(self, low, high, at):
        self.refs, self.at = (low, high), at

    def __getitem__(self, index):
        index = index if isinstance(index, tuple) else (index,)
        half, plane = divmod(index[self.at], 2)
        return self.refs[half][index[: self.at] + (plane,) + index[self.at + 1 :]]


def coef_planes(f_ref, phi_ref, co_ref, sum_ref, first=0, count=4):
    def plane(z, carry):
        f = f_ref[first + z]
        side = side_of(phi_ref[first + z])
        steps = (-3, -2, -1, 1, 2)
        along_x, rolled = shifts_x(f, steps)
        along_y = shifts_y(f, steps, rolled)
        total = None
        for axis, shift, near in ((0, shift_x, along_x), (1, shift_y, along_y)):
            b = [near[-2] - near[-3], near[-1] - near[-2], f - near[-1], near[1] - f, near[2] - near[1]]
            d = [b[i + 1] - b[i] for i in range(4)]
            minus, plus, jac_m, jac_p = weno_center(b[2], *d)
            term, by_minus, by_plus = upwind_term(minus, shift(plus, 1), side)
            for n, part in enumerate((by_minus, by_plus) + jac_m + jac_p):
                co_ref[PER_AXIS * axis + n, z] = part
            total = term if total is None else total + term
        sum_ref[z] = total
        return carry

    lax.fori_loop(0, count, plane, 0, unroll=UNROLL_COEF)


def coef_depth(section, f_ref, lo_ref, hi_ref, phi_ref, sum_ref, co_ref, scale_ref, pc_ref, unroll=2):
    def column(g, carry):
        f = (
            [lo_ref[3 * section + i, g] for i in range(3)]
            + [f_ref[i, g] for i in range(4)]
            + [hi_ref[3 * section + i, g] for i in range(3)]
        )
        b = [None] + [f[i] - f[i - 1] for i in range(1, 10)]
        d = [None, None] + [b[i] - b[i - 1] for i in range(2, 10)]
        centers = [weno_center(b[m + 3], d[m + 2], d[m + 3], d[m + 4], d[m + 5]) for m in range(5)]
        for z in range(4):
            phi = phi_ref[z, g]
            term, by_minus, by_plus = upwind_term(centers[z][0], centers[z + 1][1], side_of(phi))
            root = lax.rsqrt(phi * phi + 1.0)
            square = sum_ref[z, g] + term
            inv = lax.rsqrt(square)
            scale_ref[z, g] = (-0.25 * TAU) * ((phi * root) * inv)
            pc_ref[z, g] = (-TAU) * ((root * root * root) * (square * inv - 1.0))
            parts = (by_minus, by_plus) + centers[z][2] + centers[z + 1][3]
            for n, part in enumerate(parts):
                co_ref[n, z, g] = part
        return carry

    lax.fori_loop(0, 4, column, 0, unroll=unroll)


def apply_depth(c_ref, co_ref, scale_ref, out_ref, up_ref, dn_ref):
    def column(g, carry):
        dbar = [None] * 8
        bbar = [None] * 9

        def add(into, at, value):
            into[at] = value if into[at] is None else into[at] + value

        for z in range(4):
            c = c_ref[z, g] * scale_ref[z, g]
            co = lambda n: co_ref[n, z, g]
            a, p = c * co(0), c * co(1)
            for k in range(4):
                add(dbar, z + k, a * co(2 + k))
                add(dbar, z + k + 1, p * co(6 + k))
            add(bbar, z + 2, a)
            add(bbar, z + 3, p)
        for j in range(8):
            add(bbar, j + 1, dbar[j])
            add(bbar, j, -dbar[j])
        for z in range(4):
            out_ref[z, g] = bbar[z + 2] - bbar[z + 3]
        for k in range(3):
            up_ref[k, g] = bbar[6 + k]
            dn_ref[k, g] = bbar[k]
        return carry

    lax.fori_loop(0, 4, column, 0, unroll=UNROLL_DEPTH)


def apply_planes(c_ref, co_ref, scale_ref, pc_ref, part_ref, acc_ref, out_ref, acc_out_ref):
    for z in range(4):
        whole = c_ref[z]
        c = whole * scale_ref[z]
        total = part_ref[z]
        for axis, shift, gather in ((0, shift_x, gather_x), (1, shift_y, gather_y)):
            co = lambda n: co_ref[PER_AXIS * axis + n, z]
            a = c * co(0)
            g = shift(c * co(1), -1)
            t = [a * co(2 + k) + g * co(6 + k) for k in range(4)]
            b = [-t[0], t[0] - t[1], (a + g) + (t[1] - t[2]), t[2] - t[3], t[3]]
            total = total + gather(
                {0: b[2] - b[3], -1: b[3] - b[4], -2: b[4], 1: b[1] - b[2], 2: b[0] - b[1], 3: t[0]}
            )
        out_ref[z] = total
        local = pc_ref[z] * whole
        acc_out_ref[z] = local if acc_ref is None else acc_ref[z] + local


def joined(own_ref, lo_ref, hi_ref):
    lo0, lo1, lo2 = lo_ref[0], lo_ref[1], lo_ref[2]
    hi0, hi1, hi2 = hi_ref[0], hi_ref[1], hi_ref[2]
    return (
        own_ref[0] + (lo0 - lo1),
        own_ref[1] + (lo1 - lo2 - hi0),
        own_ref[2] + (lo2 + hi0 - hi1),
        own_ref[3] + (hi1 - hi2),
    )


def planes_kernel(*refs):
    phi_ref = refs[3]
    for n in range(3):
        coef_planes(refs[n], phi_ref, refs[4 + 2 * n], refs[5 + 2 * n])


def first_stage(f_ref, lo_ref, hi_ref, phi_ref, sum_ref, cot_ref, c_ref, part_ref, up_ref, dn_ref, scale_ref, pc_ref, co_ref):
    coef_depth(0, f_ref, lo_ref, hi_ref, phi_ref, sum_ref, co_ref, scale_ref, pc_ref, unroll=4)
    c_ref[...] = 0.5 * cot_ref[...]
    apply_depth(c_ref, co_ref, scale_ref, part_ref, up_ref, dn_ref)


def later_stage(halve, *refs):
    earlier, (own_in, lo_ref, hi_ref, co_ref, scale_ref) = refs[:-9], refs[-9:-4]
    c_ref, part_ref, up_ref, dn_ref = refs[-4:]
    for z, back in enumerate(joined(own_in, lo_ref, hi_ref)):
        c = back
        for ref in earlier:
            c = c + ref[z]
        c_ref[z] = 0.5 * c if halve else c
    apply_depth(c_ref, co_ref, scale_ref, part_ref, up_ref, dn_ref)


def window_one(c_ref, co_ref, scale_ref, pc_ref, part_ref, f_ref, lo_ref, hi_ref, phi_ref, sum_ref, own_ref, acc_ref, *coef_refs):
    apply_planes(c_ref, co_ref, scale_ref, pc_ref, part_ref, None, own_ref, acc_ref)
    coef_depth(1, f_ref, lo_ref, hi_ref, phi_ref, sum_ref, *coef_refs[:3])
    coef_planes(phi_ref, phi_ref, *coef_refs[3:], first=0, count=2)


def window_two(c_ref, co_ref, scale_ref, pc_ref, part_ref, acc_in, f_ref, lo_ref, hi_ref, phi_ref, sum_ref, own_ref, acc_ref, *coef_refs):
    apply_planes(c_ref, co_ref, scale_ref, pc_ref, part_ref, acc_in, own_ref, acc_ref)
    coef_depth(2, f_ref, lo_ref, hi_ref, phi_ref, sum_ref, *coef_refs[:3])
    coef_planes(phi_ref, phi_ref, *coef_refs[3:], first=2, count=2)


def window_three(c_ref, co_ref, scale_ref, pc_ref, part_ref, acc_in, lo_ref, hi_ref, phi_ref, sum_low, sum_high, own_ref, acc_ref, *coef_refs):
    apply_planes(c_ref, co_ref, scale_ref, pc_ref, part_ref, acc_in, own_ref, acc_ref)
    coef_depth(3, phi_ref, lo_ref, hi_ref, phi_ref, Halves(sum_low, sum_high, 0), *coef_refs)


def window_four(middle_ref, c_ref, co_low, co_high, scale_ref, pc_ref, part_ref, acc_in, own_ref, acc_ref):
    apply_planes(c_ref, Halves(co_low, co_high, 1), scale_ref, pc_ref, part_ref, acc_in, own_ref, acc_ref)
    for z in range(4):
        own_ref[z] = own_ref[z] + (acc_ref[z] + (c_ref[z] + middle_ref[z]))


def finish(own_in, lo_ref, hi_ref, out_ref):
    for z, whole in enumerate(joined(own_in, lo_ref, hi_ref)):
        for gy in range(whole.shape[0]):
            for gx in range(whole.shape[1]):
                out_ref[gx * whole.shape[0] + gy, z] = whole[gy, gx]


def slab_line(n_gx, n_gy, turns, gx):
    line = []
    for gy in range(n_gy):
        turn = turns[gy % len(turns)]
        line += [(gy, (gx + turn * step) % n_gx) for step in range(n_gx)]
        gx = (gx - turn) % n_gx
    return line


def to_slabs(count, depth, even_at, odd_at, *refs):
    odd_ref, ins, out_ref, scratch = refs[0], refs[1:-2], refs[-2], refs[-1]
    odd = odd_ref[0] == 1
    for n, ref in enumerate(ins):
        block = ref[...].reshape(BX * BY, LANES)
        scratch[...] = block.T
        for j in range(count):
            even_rows = scratch[pl.ds(depth * even_at[j], depth), :]
            odd_rows = scratch[pl.ds(depth * odd_at[j], depth), :]
            out_ref[j, pl.ds(depth * n, depth), :] = jnp.where(odd, odd_rows, even_rows)


def from_slabs(count, depth, even_at, odd_at, odd_ref, in_ref, out_ref, scratch):
    odd = odd_ref[0] == 1
    for at in range(count):
        even_rows, odd_rows = in_ref[even_at.index(at)], in_ref[odd_at.index(at)]
        scratch[pl.ds(depth * at, depth), :] = jnp.where(odd, odd_rows, even_rows)
    out_ref[...] = scratch[...].T.reshape(BX, BY, LANES)


def unpack(n_gy, n_gx, in_ref, f0, f1, f2, f3, f4, up_ref, dn_ref):
    outs = (f0, f1, f2, f3, f4)
    for n, out in enumerate(outs):
        for z in range(4):
            for gy in range(n_gy):
                rows = in_ref[pl.ds(gy, n_gx, stride=n_gy), 4 * n + z, :]
                out[z, gy] = rows
                if n < 4:
                    if z >= 1:
                        up_ref[3 * n + z - 1, gy] = rows
                    if z <= 2:
                        dn_ref[3 * n + z, gy] = rows


def make_shards(sizes, interpret=False):
    n_gx, n_gy, n_gz = sizes["gx"], sizes["gy"], sizes["gz"]
    count = n_gx * n_gy
    depth = LANES // count
    assert depth == 4
    even_line = slab_line(n_gx, n_gy, EVEN_TURNS, FIRST_GX % n_gx)
    odd_line = slab_line(n_gx, n_gy, ODD_TURNS, FIRST_GX % n_gx)[::-1]
    even_at = [even_line.index((j % n_gy, j // n_gy)) for j in range(count)]
    odd_at = [odd_line.index((j % n_gy, j // n_gy)) for j in range(count)]
    order = []
    for gz in range(n_gz):
        order += [(gx * n_gy + gy) * n_gz + gz for gy, gx in (odd_line if gz % 2 else even_line)]
    total = len(order)
    upward = [(order[i], order[(i + 1) % total]) for i in range(total)]
    downward = [(order[(i + 1) % total], order[i]) for i in range(total)]
    everywhere = ("gx", "gy", "gz")
    vmem = pl.BlockSpec(memory_space=pltpu.VMEM)
    smem = pl.BlockSpec(memory_space=pltpu.SMEM)
    slab = (4, n_gy, n_gx, LANES)
    rim = (3, n_gy, n_gx, LANES)

    def like(*shape):
        return jax.ShapeDtypeStruct(shape, F32)

    def near(*shape):
        return like(*shape) if interpret else pltpu.VMEM(shape, F32)

    def call(kernel, out_shape, *args, first=vmem, scratch=(), name=None, far=False):
        many = isinstance(out_shape, list)
        if not interpret:
            space = pltpu.HBM if far else pltpu.VMEM
            args = [x if x.ndim == 1 else pltpu.with_memory_space_constraint(x, space) for x in args]
        return pl.pallas_call(
            kernel,
            out_shape=out_shape,
            in_specs=[first] + [vmem] * (len(args) - 1),
            out_specs=[vmem] * len(out_shape) if many else vmem,
            scratch_shapes=list(scratch),
            compiler_params=pltpu.CompilerParams(vmem_limit_bytes=8 << 20),
            name=name,
            interpret=interpret,
        )(*args)

    def exchange(up, dn):
        return lax.ppermute(up, everywhere, upward), lax.ppermute(dn, everywhere, downward)

    def shards(phi_start, section_first, section_middle, section_second, cot_final):
        odd = (lax.axis_index("gz") % 2).astype(jnp.int32).reshape(1)
        turn = pltpu.VMEM((LANES, LANES), F32)

        packed = call(
            lambda *refs: to_slabs(count, depth, even_at, odd_at, *refs),
            near(count, 5 * depth, LANES),
            odd, section_second, section_middle, section_first, phi_start, cot_final,
            first=smem, far=True, scratch=[turn], name="to_slabs",
        )
        packed = lax.all_to_all(packed, ("gx", "gy"), 0, 0)
        *fields, rim_up, rim_dn = call(
            lambda *refs: unpack(n_gy, n_gx, *refs),
            [near(*slab)] * 5 + [near(12, *slab[1:])] * 2,
            packed, name="unpack",
        )
        phi, cot = fields[3], fields[4]
        rim_lo, rim_hi = exchange(rim_up, rim_dn)

        coef_flat = [near(2 * PER_AXIS, *slab), near(*slab)]
        coef_half = [near(2 * PER_AXIS, 2, *slab[1:]), near(2, *slab[1:])]
        coef_deep = [near(PER_AXIS, *slab), near(*slab), near(*slab)]
        stage_out = [near(*slab), near(*slab), near(*rim), near(*rim)]
        window_out = [near(*slab), near(*slab)]

        flat0, sum0, flat1, sum1, flat2, sum2 = call(
            planes_kernel, coef_flat * 3, *fields[:3], phi, name="coef_planes"
        )
        c1, part, up, dn, scale0, pc0 = call(
            first_stage, stage_out + [near(*slab), near(*slab)],
            fields[0], rim_lo, rim_hi, phi, sum0, cot,
            scratch=[pltpu.VMEM((PER_AXIS, *slab), F32)], name="stage_one",
        )
        lo, hi = exchange(up, dn)
        own, acc, deep, scale, pc, flat3a, sum3a = call(
            window_one, window_out + coef_deep + coef_half,
            c1, flat0, scale0, pc0, part, fields[1], rim_lo, rim_hi, phi, sum1, name="window_one",
        )
        c2, part, up, dn = call(
            lambda *refs: later_stage(False, *refs), stage_out,
            c1, own, lo, hi, deep, scale, name="stage_two",
        )
        lo, hi = exchange(up, dn)
        own, acc, deep, scale2, pc2, flat3b, sum3b = call(
            window_two, window_out + coef_deep + coef_half,
            c2, flat1, scale, pc, part, acc, fields[2], rim_lo, rim_hi, phi, sum2, name="window_two",
        )
        c3, part, up, dn = call(
            lambda *refs: later_stage(True, *refs), stage_out,
            c1, c2, own, lo, hi, deep, scale2, name="stage_three",
        )
        lo, hi = exchange(up, dn)
        own, acc, deep, scale, pc = call(
            window_three, window_out + coef_deep,
            c3, flat2, scale2, pc2, part, acc, rim_lo, rim_hi, phi, sum3a, sum3b, name="window_three",
        )
        c4, part, up, dn = call(
            lambda *refs: later_stage(False, *refs), stage_out,
            c3, own, lo, hi, deep, scale, name="stage_four",
        )
        lo, hi = exchange(up, dn)
        own = call(
            window_four, near(*slab), c3, c4, flat3a, flat3b, scale, pc, part, acc,
            scratch=[pltpu.VMEM(slab, F32)], name="window_four",
        )
        slabs = call(finish, near(count, depth, LANES), own, lo, hi, name="finish")
        slabs = lax.all_to_all(slabs, ("gx", "gy"), 0, 0)
        return call(
            lambda *refs: from_slabs(count, depth, even_at, odd_at, *refs),
            like(BX, BY, LANES), odd, slabs, first=smem, scratch=[turn], name="from_slabs",
        )

    return shards


def solution(mesh):
    spec = P("gx", "gy", "gz")
    return jax.shard_map(
        make_shards(dict(mesh.shape)),
        mesh=mesh,
        in_specs=(spec,) * 5,
        out_specs=spec,
        check_vma=False,
    )
```
